256 devices in a mesh: shot: 32 (over z_hi, y, x), space: 8 (over z_lo, core).
Axes of the slice: x: 4, y: 4, z: 8 (z_hi: 2, z_lo: 4; z = z_hi * 4 + z_lo), core: 2. Of those that a mesh axis runs over, the one named last changes fastest.
Arguments:
- velocity: float32 [1024, 2048], P('space'), may hold values from 1.5 to 4.5
- encoder_weight: float32 [4, 4, 64], replicated, may hold values from -1.5 to 1.5
- encoder_bias: float32 [64], replicated, may hold values from -3 to 3
- source_amplitude: float32 [64], replicated, may hold values from -12 to 12
- source_row: int32 [128], P('shot'), may hold values from 0 to 255
- source_column: int32 [128], P('shot'), may hold values from 0 to 511
- receiver_rows: int32 [128, 16], P('shot'), may hold values from 0 to 255
- point_weight: bfloat16 [64, 64], replicated, may hold values from -0.75 to 0.75
- spectral_weight: bfloat16 [48, 24, 64, 128], P(None, 'space'), may hold values from -1.5 to 1.5
- layer_bias: float32 [64], replicated, may hold values from -3 to 3
- out_weight: float32 [64], replicated, may hold values from -0.75 to 0.75
- observed: float32 [128, 16, 512], P('shot'), may hold values from -6 to 6
Outputs:
- misfit: float32 [128], P('shot')
- velocity_gradient: float32 [1024, 2048], P('space', 'shot')
The draws below stay inside these ranges and needn't reach their ends.
Inputs may be any that keep to these rules, and one draw needn't show every extreme that they name: `receiver_rows`: receivers of one shot may share a row.
All inputs are finite; a program needn't handle non-finite values.
Results may differ from the reference program's by a relative error of at most 0.0065.
Values may be sent and summed in bfloat16 or wider, within the bound.
No kernel may reach another device: no remote copies, remote signals or barrier semaphores. Data moves between devices by JAX's collectives and lax.ppermute only.
A program may use at most 128 MiB of HBM per device.

```python
import math
import jax
import jax.numpy as jnp
from jax import lax

C = 64
KX = 48
KY = 24
GH = 256
GW = 512
REC = 16
SHOTS = 128
VH = 1024
VW = 2048


def plant(drawn, stream_key, least, top_value):
    spot = [jax.random.randint(jax.random.fold_in(stream_key, axis), (), 0, length) for axis, length in enumerate(drawn.shape)]
    widest = drawn.shape.index(max(drawn.shape))
    neighbour = spot[:widest] + [(spot[widest] + 1) % drawn.shape[widest]] + spot[widest + 1:]
    return drawn.at[tuple(spot)].set(least).at[tuple(neighbour)].set(top_value)


def shard_levels(rng, shape, pieces, least, top_value):
    def one(position, shards_of):
        heights = jax.random.uniform(jax.random.fold_in(jax.random.fold_in(rng, 6), position), (shards_of,), jnp.float32, least / len(pieces), top_value / len(pieces))
        return jnp.repeat(jnp.exp(heights), shape[position] // shards_of).reshape((-1,) + (1,) * (len(shape) - position - 1))

    loudness = one(*pieces[0])
    for cut in pieces[1:]:
        loudness = loudness * one(*cut)
    return loudness


def noise(key, extent, width, reach, cuts=(), held_as=jnp.bfloat16):
    array = jax.random.normal(key, extent, jnp.float32) * width
    if len(cuts) > 0:
        array = shard_levels(key, extent, cuts, -0.22, 0.18) * array
    return jnp.clip(array, min=-reach, max=reach).astype(held_as)


def setup_inputs(seed: int = 0) -> dict:
    arg_keys = jax.random.split(jax.random.key(seed), 13)
    velocity = jnp.clip(1.5 + 3.0 * jax.random.uniform(arg_keys[0], (VH, VW), jnp.float32) ** shard_levels(arg_keys[0], (VH, VW), ((0, 8),), -0.2, 0.2), 1.5, 4.5)
    encoder_weight = noise(arg_keys[1], (4, 4, C), 16 ** -0.5, 1.5, (), jnp.float32)
    encoder_bias = noise(arg_keys[2], (C,), 0.5, 3.0, (), jnp.float32)
    source_amplitude = noise(arg_keys[3], (C,), 2.0, 12.0, (), jnp.float32)
    source_row = plant(jax.random.randint(arg_keys[4], (SHOTS,), 0, GH), jax.random.fold_in(arg_keys[4], 1), 0, GH - 1).astype(jnp.int32)
    source_column = plant(jax.random.randint(arg_keys[5], (SHOTS,), 0, GW), jax.random.fold_in(arg_keys[5], 1), 0, GW - 1).astype(jnp.int32)
    receiver_rows = plant(jax.random.randint(arg_keys[6], (SHOTS, REC), 0, GH), jax.random.fold_in(arg_keys[6], 1), 0, GH - 1).astype(jnp.int32)
    point_weight = noise(arg_keys[7], (C, C), C ** -0.5, 0.75)
    spectral_weight = noise(arg_keys[8], (KX, KY, C, 2 * C), 0.25, 1.5, ((1, 8),))
    layer_bias = noise(arg_keys[9], (C,), 0.5, 3.0, (), jnp.float32)
    out_weight = noise(arg_keys[10], (C,), C ** -0.5, 0.75, (), jnp.float32)
    observed = noise(arg_keys[11], (SHOTS, REC, GW), 1.0, 6.0, ((0, 32),), jnp.float32)
    return {"velocity": velocity, "encoder_weight": encoder_weight, "encoder_bias": encoder_bias, "source_amplitude": source_amplitude, "source_row": source_row, "source_column": source_column, "receiver_rows": receiver_rows, "point_weight": point_weight, "spectral_weight": spectral_weight, "layer_bias": layer_bias, "out_weight": out_weight, "observed": observed}


VELOCITY_MEAN = 3.0
VELOCITY_SCALE = 1.5
BUMP_SPREAD = 32.0
EPSILON = 1e-06
HIGHEST = lax.Precision.HIGHEST

def build_tables(grid_rows, grid_columns, row_modes, column_modes):
    column_index = jnp.arange(grid_columns, dtype=jnp.int32)
    mode_index = jnp.arange(column_modes, dtype=jnp.int32)
    column_phase = (column_index[:, None] * mode_index[None, :] % grid_columns).astype(jnp.float32) * (2.0 * math.pi / grid_columns)
    mode_weight = jnp.where(mode_index == 0, 1.0, 2.0).astype(jnp.float32)
    root_columns = 1.0 / math.sqrt(grid_columns)
    forward_plain = jnp.stack([jnp.cos(column_phase), -jnp.sin(column_phase)], axis=1) * root_columns
    backward_plain = jnp.stack([jnp.cos(column_phase).T, -jnp.sin(column_phase).T], axis=0) * root_columns
    forward_weighted = forward_plain * mode_weight[None, None, :]
    backward_weighted = backward_plain * mode_weight[None, :, None]
    row_index = jnp.arange(grid_rows, dtype=jnp.int32)
    row_mode_index = jnp.arange(row_modes, dtype=jnp.int32)
    frequency = jnp.where(row_mode_index < row_modes // 2, row_mode_index, row_mode_index - row_modes)
    row_phase = (frequency[:, None] * row_index[None, :] % grid_rows).astype(jnp.float32) * (2.0 * math.pi / grid_rows)
    root_rows = 1.0 / math.sqrt(grid_rows)
    cosine_rows = jnp.cos(row_phase) * root_rows
    sine_rows = jnp.sin(row_phase) * root_rows
    return tuple((element.astype(jnp.bfloat16) for element in (forward_plain, backward_plain, forward_weighted, backward_weighted, cosine_rows, sine_rows)))

def rounded(values):
    return lax.optimization_barrier(values.astype(jnp.bfloat16)).astype(jnp.float32)

def unchanged(values):
    return values

def mix_modes(spectrum, weights, adjoint):
    channels = weights.shape[2]
    real_part = spectrum[..., :channels]
    imaginary_part = spectrum[..., channels:]
    if adjoint:
        result_real = jnp.einsum('...kyq,kycq->...kyc', spectrum, weights, precision=HIGHEST, preferred_element_type=jnp.float32)
        rotated = jnp.concatenate([imaginary_part, -real_part], axis=-1)
        result_imaginary = jnp.einsum('...kyq,kycq->...kyc', rotated, weights, precision=HIGHEST, preferred_element_type=jnp.float32)
    else:
        leading = jnp.einsum('...kyc,kycq->...kyq', real_part, weights, precision=HIGHEST, preferred_element_type=jnp.float32)
        trailing = jnp.einsum('...kyc,kycq->...kyq', imaginary_part, weights, precision=HIGHEST, preferred_element_type=jnp.float32)
        result_real = leading[..., :channels] - trailing[..., channels:]
        result_imaginary = leading[..., channels:] + trailing[..., :channels]
    return jnp.concatenate([result_real, result_imaginary], axis=-1)

def spectral(values, weights, table_in, table_out, cosine_rows, sine_rows, adjoint):
    keep = unchanged if adjoint else rounded
    channels = values.shape[0]
    along_columns = jnp.einsum('chw,wpk->hkpc', values.astype(jnp.float32), table_in.astype(jnp.float32), precision=HIGHEST)
    along_columns = keep(along_columns.reshape(along_columns.shape[0], along_columns.shape[1], 2 * channels))
    cosine_wide = cosine_rows.astype(jnp.float32)
    sine_wide = sine_rows.astype(jnp.float32)
    leading = jnp.einsum('kh,hyx->kyx', cosine_wide, along_columns, precision=HIGHEST)
    trailing = jnp.einsum('kh,hyx->kyx', sine_wide, along_columns, precision=HIGHEST)
    spectrum = keep(jnp.concatenate([leading[..., :channels] + trailing[..., channels:], leading[..., channels:] - trailing[..., :channels]], axis=-1))
    mixture = keep(mix_modes(spectrum, weights.astype(jnp.float32), adjoint))
    leading = jnp.einsum('kh,kyx->hyx', cosine_wide, mixture, precision=HIGHEST)
    trailing = jnp.einsum('kh,kyx->hyx', sine_wide, mixture, precision=HIGHEST)
    rows_back = keep(jnp.concatenate([leading[..., :channels] - trailing[..., channels:], trailing[..., :channels] + leading[..., channels:]], axis=-1))
    rows_back = rows_back.reshape(rows_back.shape[0], rows_back.shape[1], 2, channels)
    return jnp.einsum('hkpo,pkw->ohw', rows_back, table_out.astype(jnp.float32), precision=HIGHEST)

def misfit_of(predicted, recorded, taper_gain):
    weighted = predicted * taper_gain
    target = recorded * taper_gain
    predicted_scale = jnp.sqrt(jnp.mean(weighted * weighted) + EPSILON)
    target_scale = jnp.sqrt(jnp.mean(target * target) + EPSILON)
    differ = weighted / predicted_scale - target / target_scale
    return 0.5 * jnp.mean(differ * differ)

def reference(velocity, encoder_weight, encoder_bias, source_amplitude, source_row, source_column, receiver_rows, point_weight, spectral_weight, layer_bias, out_weight, observed):
    column_in, column_out, weighted_in, weighted_out, cosine_rows, sine_rows = build_tables(GH, GW, KX, KY)
    normalized = (velocity - VELOCITY_MEAN) / VELOCITY_SCALE
    patches = normalized.reshape(GH, 4, GW, 4)
    encoded = jnp.einsum('hawb,abc->chw', patches, encoder_weight, precision=HIGHEST) + encoder_bias[:, None, None]
    row_place = jnp.arange(GH, dtype=jnp.int32).astype(jnp.float32)
    column_place = jnp.arange(GW, dtype=jnp.int32).astype(jnp.float32)
    taper_gain = 0.5 + column_place / GW
    point_wide = point_weight.astype(jnp.float32)

    def one_shot(running, inputs):
        row_source, column_source, receivers, recorded = inputs
        row_gap = row_place - row_source.astype(jnp.float32)
        column_gap = column_place - column_source.astype(jnp.float32)
        source_bump = jnp.exp(-(row_gap[:, None] * row_gap[:, None] + column_gap[None, :] * column_gap[None, :]) / BUMP_SPREAD)
        lifted = rounded(encoded + source_amplitude[:, None, None] * source_bump[None])
        pointwise = jnp.einsum('co,chw->ohw', point_wide, lifted, precision=HIGHEST)
        spectral_out = spectral(lifted, spectral_weight, column_in, weighted_out, cosine_rows, sine_rows, False)
        preactivation = pointwise + spectral_out + layer_bias[:, None, None]
        activation, activation_back = jax.vjp(jax.nn.gelu, preactivation)
        output_field = jnp.einsum('c,chw->hw', out_weight, activation, precision=HIGHEST)
        receiver_mask = (receivers[:, None] == jnp.arange(GH, dtype=jnp.int32)[None, :]).astype(jnp.float32)
        predicted = jnp.dot(receiver_mask, output_field, precision=HIGHEST)
        misfit, misfit_back = jax.vjp(lambda values: misfit_of(values, recorded, taper_gain), predicted)
        data_gradient = misfit_back(jnp.asarray(GH * GW, jnp.float32))[0]
        field_gradient = jnp.dot(receiver_mask.T, data_gradient, precision=HIGHEST)
        inner_gradient = rounded(activation_back(out_weight[:, None, None] * field_gradient[None])[0])
        lifted_gradient = jnp.einsum('co,ohw->chw', point_wide, inner_gradient, precision=HIGHEST)
        lifted_gradient = lifted_gradient + spectral(inner_gradient, spectral_weight, weighted_in, column_out, cosine_rows, sine_rows, True)
        return (running + lifted_gradient, misfit)
    starting = jnp.zeros((C, GH, GW), jnp.float32)
    summed, misfits = lax.scan(one_shot, starting, (source_row, source_column, receiver_rows, observed))
    patch_gradient = jnp.einsum('abc,chw->hawb', encoder_weight, summed, precision=HIGHEST) / VELOCITY_SCALE
    cell_gradient = patch_gradient.reshape(VH, VW)
    velocity_gradient = cell_gradient / jnp.sqrt(jnp.mean(cell_gradient * cell_gradient) + EPSILON)
    return (misfits, velocity_gradient)
```

```python
import math

import jax
import jax.numpy as jnp
import ml_dtypes
import numpy as np
from jax import lax
from jax.experimental import pallas as pl
from jax.experimental.pallas import tpu as pltpu
from jax.sharding import PartitionSpec as P

C = 64
KX = 48
KY = 24
GH = 256
GW = 512
REC = 16
SPACE = 8
SHOT = 32
ROWS = GH // SPACE
KOWN = KY // SPACE
PAIRS = 64
EPSILON = 1e-06
VELOCITY_MEAN = 3.0
VELOCITY_SCALE = 1.5
HIGHEST = lax.Precision.HIGHEST
F32 = jnp.float32
BF16 = jnp.bfloat16
VMEM_LIMIT = 56 << 20


def bf(values):
    return np.asarray(values, np.float32).astype(ml_dtypes.bfloat16)


def as64(values):
    return values.astype(np.float64)


def make_tables():
    k = np.arange(KY)
    w = np.arange(GW)
    phase = (k[:, None] * w[None, :] % GW) * (2.0 * math.pi / GW)
    plain = bf(np.stack([np.cos(phase), -np.sin(phase)], 1) / math.sqrt(GW))
    f = np.where(np.arange(KX) < KX // 2, np.arange(KX), np.arange(KX) - KX)
    phase = (f[:, None] * np.arange(GH)[None, :] % GH) * (2.0 * math.pi / GH)
    cos_rows = bf(np.cos(phase) / math.sqrt(GH))
    sin_rows = bf(np.sin(phase) / math.sqrt(GH))
    return plain, cos_rows, sin_rows


PLAIN, COS_ROWS, SIN_ROWS = make_tables()
MODE_WEIGHT = np.where(np.arange(KY) == 0, 1.0, 2.0)


def columns_table():
    table = np.zeros((GW, 4, SPACE, 32), np.float32)
    plain = PLAIN.astype(np.float32).reshape(SPACE, 6, GW)
    for b in range(4):
        table[:, b, :, 6 * b : 6 * b + 6] = plain.transpose(2, 0, 1)
    return bf(table.reshape(4 * GW, 256))


def rows_table():
    table = np.zeros((SPACE, 4, KX, 2, ROWS, 4), np.float32)
    for p in range(SPACE):
        for a in range(4):
            table[p, a, :, 0, :, a] = COS_ROWS[:, ROWS * p : ROWS * p + ROWS]
            table[p, a, :, 1, :, a] = SIN_ROWS[:, ROWS * p : ROWS * p + ROWS]
    return bf(table.reshape(SPACE, 4 * KX, 256))


def ones_table():
    wsum = as64(PLAIN).sum(-1)
    c, s = as64(COS_ROWS).sum(-1), as64(SIN_ROWS).sum(-1)
    table = np.zeros((SPACE, KX, 128), np.float32)
    for q in range(SPACE):
        for k in range(KOWN):
            re, im = wsum[3 * q + k]
            table[q, :, 24 + 2 * k] = c * re + s * im
            table[q, :, 25 + 2 * k] = c * im - s * re
    return table


def select_table():
    table = np.zeros((128, 4, 4, 128), np.float32)
    for b in range(4):
        table[np.arange(128), b, b, np.arange(128)] = 1.0
    return bf(table.reshape(512, 512))


def weighted_table():
    plain = PLAIN.astype(np.float32) * MODE_WEIGHT[:, None, None]
    return bf(plain.reshape(SPACE, KOWN, 2, GW).transpose(1, 2, 0, 3).reshape(48, GW))


def gram_tables():
    full = np.concatenate([as64(COS_ROWS), as64(SIN_ROWS)], 0)
    gram_rows = full @ full.T
    e = as64(PLAIN).reshape(48, GW)
    gram = e @ e.T
    wide = np.zeros((SPACE, 4, 32, SPACE, 4, 32))
    gram = gram.reshape(SPACE, 6, SPACE, 6)
    for a in range(4):
        for b in range(4):
            wide[:, a, b * 6 : b * 6 + 6, :, a, b * 6 : b * 6 + 6] = gram
    wide = wide.reshape(1024, 1024)
    diag_rows = np.broadcast_to(np.diag(gram_rows)[:, None], (96, 128))
    off_rows = bf(gram_rows - np.diag(np.diag(gram_rows)))
    diag_wide = np.diag(wide)[None, :]
    off_wide = bf(wide - np.diag(np.diag(wide)))
    return (
        np.asarray(diag_rows, np.float32),
        off_rows,
        np.asarray(diag_wide, np.float32),
        off_wide,
    )


COLUMNS = columns_table()
ROW_SUMS = rows_table()
ONES = ones_table()
SELECT = select_table()
WEIGHTED = weighted_table()
DIAG_ROWS, OFF_ROWS, DIAG_WIDE, OFF_WIDE = gram_tables()
PAIRED_ROWS = np.zeros((2, 64, GH), np.float32)
PAIRED_ROWS[0, :KX], PAIRED_ROWS[1, :KX] = COS_ROWS, SIN_ROWS
PAIRED_ROWS = bf(PAIRED_ROWS.reshape(128, GH))
OWN_COLUMNS = np.zeros((SPACE, 8, GW), np.float32)
OWN_COLUMNS[:, :6] = PLAIN.reshape(SPACE, 6, GW)
OWN_COLUMNS = bf(OWN_COLUMNS)


def lanes_table():
    table = np.zeros((KOWN, 2, 128, 128), np.float32)
    for k in range(KOWN):
        for part in range(2):
            for ab in range(16):
                table[k, part, ab, 32 * (ab // 4) + 6 * (ab % 4) + 2 * k + part] = 1.0
    return bf(table.reshape(KOWN * 2, 128, 128))


def block_table():
    table = np.zeros((SHOT, SPACE, 4, 32, 16, 4), np.float32)
    plain = PLAIN.astype(np.float32).reshape(SPACE, 6, SHOT, 16)
    for b in range(4):
        table[:, :, :, 6 * b : 6 * b + 6, :, b] = plain.transpose(2, 0, 1, 3)[:, :, None]
    return bf(table.reshape(SHOT, 1024, 64))


LANES = lanes_table()
BLOCKS = block_table()
BOTH_ROWS = bf(np.concatenate([COS_ROWS.astype(np.float32), SIN_ROWS.astype(np.float32)], 0))
ROWS_BACK = bf(
    BOTH_ROWS.astype(np.float32).T.reshape(SPACE, ROWS, 96)
)


def split(values):
    high = values.astype(BF16)
    return high, (values - high.astype(F32)).astype(BF16)


def dot(a, b, dims=((1,), (0,))):
    return lax.dot_general(a, b, (dims, ((), ())), preferred_element_type=F32)


def dot_split(a, b):
    high, low = split(b)
    return dot(a, high) + dot(a, low)


def minus_i(x):
    lane = lax.broadcasted_iota(jnp.int32, x.shape, 1)
    swapped = pltpu.roll(x, 64, 1)
    return jnp.where(lane < 64, swapped, -swapped)


def times_i(x):
    lane = lax.broadcasted_iota(jnp.int32, x.shape, 1)
    swapped = pltpu.roll(x, 64, 1)
    return jnp.where(lane < 64, -swapped, swapped)


def full_spec(shape):
    return pl.BlockSpec(shape, lambda *_: (0,) * len(shape))


def own_spec(shape, place=0):
    return pl.BlockSpec((1,) + shape, lambda i, *own: (own[place][0],) + (0,) * len(shape))


def call(body, prefetch, out_shape, in_specs, out_specs, scratch=(), name=None):
    return pl.pallas_call(
        body,
        out_shape=out_shape,
        grid_spec=pltpu.PrefetchScalarGridSpec(
            num_scalar_prefetch=prefetch,
            grid=(1,),
            in_specs=in_specs,
            out_specs=out_specs,
            scratch_shapes=list(scratch),
        ),
        compiler_params=pltpu.CompilerParams(vmem_limit_bytes=VMEM_LIMIT),
        name=name,
    )


def shaped(shape, dtype=F32):
    return jax.ShapeDtypeStruct(shape, dtype)


def velocity_body(own, v_ref, cols_ref, rows_ref, out_ref):
    vn = (v_ref[...] - VELOCITY_MEAN) / VELOCITY_SCALE
    high, low = split(vn)
    xx = dot(high, cols_ref[...]) + dot(low, cols_ref[...])
    even = lax.broadcasted_iota(jnp.int32, xx.shape, 1) % 2 == 0
    turned = jnp.where(even, pltpu.roll(xx, 255, 1), -pltpu.roll(xx, 1, 1))
    stacked = jnp.concatenate([xx, turned], axis=0)
    yy = dot_split(rows_ref[0], stacked)
    group = lax.broadcasted_iota(jnp.int32, (KX, 128), 1) // 32
    for q in range(SPACE):
        total = jnp.zeros((KX, 128), F32)
        for a in range(4):
            piece = yy[KX * a : KX * a + KX, 128 * (q // 4) : 128 * (q // 4) + 128]
            shift = (32 * a - 32 * (q % 4)) % 128
            if shift:
                piece = pltpu.roll(piece, shift, 1)
            total = jnp.where(group == a, piece, total)
        out_ref[q] = total


def column_of(row):
    return jnp.broadcast_to(row, (128, C)).T


def planes_body(
    own, v_ref, sel_ref, enc_ref, bias_ref, amp_ref, point_ref, layer_ref, weight_ref, lanes_ref,
    out_ref, wk_ref, vec_ref, place_ref, high_ref, low_ref, tmp,
):
    for m in range(4):
        vn = (v_ref[:, 512 * m : 512 * m + 512] - VELOCITY_MEAN) / VELOCITY_SCALE
        high, low = split(vn)
        tmp[...] = dot(high, sel_ref[...]) + dot(low, sel_ref[...])
        for h in range(ROWS):
            for b in range(4):
                out_ref[h, 4 * b : 4 * b + 4, 128 * m : 128 * m + 128] = tmp[
                    4 * h : 4 * h + 4, 128 * b : 128 * b + 128
                ]
    stack = jnp.concatenate(
        [enc_ref[...], bias_ref[...], amp_ref[...], jnp.zeros((6, C), F32)], axis=0
    )
    high, low = split(stack)
    pointed = dot(high, point_ref[...]) + dot(low, point_ref[...])
    swapped = jnp.concatenate(
        [pointed[4 * a + b : 4 * a + b + 1] for b in range(4) for a in range(4)], axis=0
    )
    high, low = split(swapped)
    wk_ref[0:16] = high
    wk_ref[16:32] = high
    wk_ref[32:48] = low
    vec_ref[0] = column_of(pointed[17:18])
    vec_ref[1] = column_of(pointed[16:17] + layer_ref[...])
    vec_ref[2] = column_of(weight_ref[...])
    turned = jnp.concatenate([pointed[:16], jnp.zeros((112, C), F32)], axis=0).T
    scaled = turned * (1.0 / VELOCITY_SCALE)
    for e in range(8):
        high, low = split(pltpu.roll(scaled, 16 * e, 1) if e else scaled)
        place_ref[e, 0:C] = high
        place_ref[e, C : 2 * C] = low
    th, tl = split(scaled)
    for k in range(KOWN):
        reach = jnp.where((own[0] == 0) & (k == 0), 1.0, 0.5)
        for part in range(2):
            wide = (dot(th, lanes_ref[2 * k + part]) + dot(tl, lanes_ref[2 * k + part])) * reach
            high, low = split(wide)
            high_ref[k, C * part : C * part + C] = high
            low_ref[k, C * part : C * part + C] = low


def operator_body(
    own, enc_ref, bias_ref, amp_ref, w_ref, index_ref, rows_ref, cols_ref, out_ref, side_ref, bump_ref
):
    stack = jnp.concatenate(
        [enc_ref[...], bias_ref[...], amp_ref[...], jnp.zeros((6, C), F32)], axis=0
    )
    high, low = split(stack)
    lhs = jnp.concatenate([high.astype(F32), low.astype(F32)], axis=0).astype(BF16)

    def step(j, carry):
        for k in range(KOWN):
            both = dot(lhs, w_ref[j, k])
            out_ref[pl.ds(k * KX * 24 + j, 24, stride=KX), :] = both[:24] + both[24:]
        return carry

    lax.fori_loop(0, KX, step, 0, unroll=8)
    receiver, row, column = index_ref[:, 0:1], index_ref[:, 1:2], index_ref[:, 2:3]
    line = lax.broadcasted_iota(jnp.int32, (PAIRS, GH), 1).astype(F32)
    chosen = jnp.where(line == receiver, 1.0, 0.0).astype(BF16)
    at_rows = dot(chosen, rows_ref[...], ((1,), (1,)))
    gap = line - row
    high, low = split(jnp.exp(gap * gap * (-1.0 / 32.0)))
    row_side = dot(high, rows_ref[...], ((1,), (1,))) + dot(low, rows_ref[...], ((1,), (1,)))
    gap = lax.broadcasted_iota(jnp.int32, (PAIRS, GW), 1).astype(F32) - column
    bump = jnp.exp(gap * gap * (-1.0 / 32.0))
    high, low = split(bump)
    column_side = dot(high, cols_ref[0], ((1,), (1,))) + dot(low, cols_ref[0], ((1,), (1,)))
    gap = receiver - row
    bump_ref[...] = bump * jnp.exp(gap * gap * (-1.0 / 32.0))
    lane = lax.broadcasted_iota(jnp.int32, (PAIRS, 128), 1)
    first = at_rows * row_side
    second = at_rows * pltpu.roll(row_side, 64, 1)
    both = jnp.where(
        lane < 64, first + pltpu.roll(first, 64, 1), second - pltpu.roll(second, 64, 1)
    )
    turned = times_i(both)
    for k in range(KOWN):
        side_ref[k, :, 0:128] = at_rows.astype(BF16)
        side_ref[k, :, 128:256] = (
            both * column_side[:, 2 * k : 2 * k + 1] + turned * column_side[:, 2 * k + 1 : 2 * k + 2]
        ).astype(BF16)


def mix_body(own, v_ref, ones_ref, t_ref, l_ref, out_ref):
    spectrum = ones_ref[0]
    for q in range(SPACE):
        spectrum = spectrum + v_ref[q]
    for k in range(KOWN):
        first = jnp.zeros((KX, 128), F32)
        second = jnp.zeros((KX, 128), F32)
        for ab in range(17):
            lane = (ab // 4) * 32 + (ab % 4) * 6 + 2 * k if ab < 16 else 24 + 2 * k
            plane = t_ref[pl.ds((k * 24 + ab) * KX, KX), :]
            first = first + spectrum[:, lane : lane + 1] * plane
            second = second + spectrum[:, lane + 1 : lane + 2] * plane
        modes = first + times_i(second)
        source = t_ref[pl.ds((k * 24 + 17) * KX, KX), :]
        none = jnp.zeros((16, 128), F32)
        rhs = jnp.concatenate(
            [modes, none, times_i(modes), none, source, none, times_i(source), none], axis=0
        )
        values = dot(l_ref[k], rhs.astype(BF16)).astype(BF16)
        for z in range(SPACE // 2):
            out_ref[z, :, 128 * k : 128 * k + 128] = values


def gain_row():
    return 0.5 + lax.broadcasted_iota(jnp.int32, (1, GW), 1).astype(F32) * (1.0 / GW)


def forward_body(
    own, rows_ref, d_ref, other_ref, planes_ref, table_ref, wk_ref, col_ref, vec_ref, obs_ref,
    pred_ref, slope_ref, stats_ref, dd, acc,
):
    p = own[0]
    gain = gain_row()
    for m in range(3):
        for z in range(SPACE // 2):
            for source, core in ((d_ref, p % 2), (other_ref, 1 - p % 2)):
                start = pl.multiple_of(PAIRS * (SPACE * m + 2 * z + core), PAIRS)
                dd[pl.ds(start, PAIRS), :] = source[z, :, 128 * m : 128 * m + 128].astype(F32)
    acc[...] = jnp.zeros_like(acc)
    root = math.sqrt(2.0 / math.pi)

    def step(r, carry):
        row = rows_ref[r] - p * ROWS

        @pl.when((row >= 0) & (row < ROWS))
        def _():
            s = r // REC
            pieces = []
            for m in range(3):
                block = dd[pl.ds(SPACE * PAIRS * m + r, SPACE, stride=PAIRS), :]
                pieces.append(block[:, :64])
                pieces.append(pltpu.roll(block, 64, 1)[:, :64])
            lhs = jnp.concatenate(pieces, axis=0).astype(BF16)
            lhs = jnp.concatenate([lhs, wk_ref[...]], axis=0)
            high, low = split(planes_ref[row])
            rhs = jnp.concatenate([table_ref[...], high, low, high], axis=0)
            x = dot(lhs, rhs, ((0,), (0,)))
            amp, const, weight = vec_ref[0], vec_ref[1], vec_ref[2]
            col = col_ref[pl.ds(r, 1), :]
            total = []
            for m in range(4):
                lanes = slice(128 * m, 128 * m + 128)
                xm = x[:, lanes] + const + amp * col[:, lanes]
                square = xm * xm
                t = jnp.tanh(root * (xm + 0.044715 * (square * xm)))
                cdf = 0.5 * (1.0 + t)
                slope = cdf + xm * (
                    (0.5 * root) * (1.0 - t * t) * (1.0 + 3.0 * 0.044715 * square)
                )
                slope_ref[pl.ds(pl.multiple_of(r * C, C), C), lanes] = (slope * weight).astype(BF16)
                total.append(jnp.sum(weight * (xm * cdf), axis=0, keepdims=True))
            predicted = jnp.concatenate(total, axis=1)
            pred_ref[pl.ds(r, 1), :] = predicted
            weighted = predicted * gain
            target = obs_ref[pl.ds(r, 1), :] * gain
            acc[pl.ds(s, 1), :] += weighted * weighted
            acc[pl.ds(s + 4, 1), :] += weighted * target

        return carry

    lax.fori_loop(0, PAIRS, step, 0)
    stats = acc[:, :128] + acc[:, 128:256] + acc[:, 256:384] + acc[:, 384:]
    for q in range(SPACE):
        stats_ref[q] = stats


def backward_body(
    own, rows_ref, shot, stats_ref, obs_ref, pred_ref, slope_ref, table_ref, place_ref,
    cols_ref, near_ref, next_ref, far_ref, last_ref, misfit_ref, coef, acc, planes,
):
    p = own[0]
    count = float(REC * GW)
    stats = stats_ref[0]
    for q in range(1, SPACE):
        stats = stats + stats_ref[q]
    stats = jnp.sum(stats, axis=1, keepdims=True)
    gain = gain_row()
    for s in range(4):
        target = obs_ref[REC * s : REC * s + REC, :] * gain
        tt = jnp.sum(jnp.sum(target * target, axis=0, keepdims=True), axis=1, keepdims=True) / count
        ww = stats[s : s + 1] / count
        wt = stats[s + 4 : s + 5] / count
        sp2 = ww + EPSILON
        isp = 1.0 / jnp.sqrt(sp2)
        isq = 1.0 / jnp.sqrt(tt + EPSILON)
        kappa = ww / sp2 - wt * isp * isq
        coef[s : s + 1, :] = jnp.broadcast_to(isp, (1, GW))
        coef[s + 4 : s + 5, :] = jnp.broadcast_to(isq, (1, GW))
        coef[s + 8 : s + 9, :] = jnp.broadcast_to(kappa, (1, GW))
        coef[s + 12 : s + 13, :] = jnp.zeros((1, GW), F32)
    acc[...] = jnp.zeros_like(acc)
    planes[...] = jnp.zeros_like(planes)

    def step(r, carry):
        row = rows_ref[r] - p * ROWS

        @pl.when((row >= 0) & (row < ROWS))
        def _():
            s = r // REC
            isp = coef[pl.ds(s, 1), :]
            isq = coef[pl.ds(s + 4, 1), :]
            kappa = coef[pl.ds(s + 8, 1), :]
            weighted = pred_ref[pl.ds(r, 1), :] * gain * isp
            target = obs_ref[pl.ds(r, 1), :] * gain * isq
            differ = weighted - target
            coef[pl.ds(s + 12, 1), :] += differ * differ
            data = (GH * GW / count) * gain * isp * (differ - kappa * weighted)
            slope = slope_ref[pl.ds(pl.multiple_of(r * C, C), C), :].astype(F32)
            inner = (slope * data).astype(BF16)
            spectra = dot(table_ref[...], inner, ((1,), (1,)))
            acc[pl.ds(pl.multiple_of(row * 48, 8), 48), 0:64] += spectra
            eighth = row % 8
            two = jnp.concatenate([inner, inner], axis=0)
            planes[row // 8] += dot(two, place_ref[eighth], ((0,), (0,)))

        return carry

    lax.fori_loop(0, PAIRS, step, 0)
    lane = lax.broadcasted_iota(jnp.int32, (ROWS, 128), 1)
    for q in range(SPACE):
        for m in range(3):
            even = acc[pl.ds(16 * m + q, ROWS, stride=48), :]
            odd = acc[pl.ds(16 * m + 8 + q, ROWS, stride=48), :]
            joined = jnp.where(lane < 64, even, pltpu.roll(odd, 64, 1))
            cols_ref[q, :, 128 * m : 128 * m + 128] = joined.astype(BF16)
    x = shot[0] % 4
    for by, grad_ref in enumerate((near_ref, next_ref, far_ref, last_ref)):
        column = (x + by) % 4
        for zy in range(8):
            for g in range(4):
                start = pl.multiple_of(64 * zy + 16 * column, 16)
                grad_ref[64 * zy + 16 * g : 64 * zy + 16 * g + 16, :] = planes[
                    g, pl.ds(start, 16), :
                ].astype(BF16)
    for s in range(4):
        row = coef[s + 12 : s + 13, :]
        misfit_ref[s : s + 1, :] = (
            row[:, :128] + row[:, 128:256] + row[:, 256:384] + row[:, 384:]
        )
    misfit_ref[4:8, :] = jnp.zeros((4, 128), F32)


def adjoint_body(a_ref, rows_ref, out_ref):
    values = jnp.concatenate([a_ref[q] for q in range(SPACE)], axis=0)
    y = dot(rows_ref[...], values)
    for k in range(KOWN):
        lanes = slice(128 * k, 128 * k + 128)
        out_ref[KX * k : KX * k + KX, :] = y[:KX, lanes] + minus_i(y[KX:, lanes])


MODES = KOWN * KX


def along_x_body(shot, a_ref, b_ref, c_ref, d_ref, near_ref, next_ref, far_ref, last_ref, tmp):
    tmp[...] = (a_ref[...].astype(F32) + b_ref[...].astype(F32)) + (
        c_ref[...].astype(F32) + d_ref[...].astype(F32)
    )
    y = shot[0] // 4 % 4
    for by, out_ref in enumerate((near_ref, next_ref, far_ref, last_ref)):
        for z in range(2):
            start = pl.multiple_of(64 * (4 * z + (y + by) % 4), 64)
            out_ref[64 * z : 64 * z + 64, :] = tmp[pl.ds(start, 64), :]


def along_y_body(a_ref, b_ref, c_ref, d_ref, modes_ref, out_ref):
    out_ref[0:MODES, :] = modes_ref[...]
    out_ref[MODES:, :] = (a_ref[...] + b_ref[...]) + (c_ref[...] + d_ref[...])


def along_z_body(shot, a_ref, b_ref, local_ref, out_ref, tmp):
    out_ref[0:MODES, :] = a_ref[0:MODES, :] + b_ref[0:MODES, :]
    total = a_ref[MODES:, :] + b_ref[MODES:, :]
    tmp[...] = total
    local_ref[...] = tmp[pl.ds(pl.multiple_of(64 * (shot[0] // 16), 64), 64), :]
    out_ref[MODES : MODES + 8, :] = jnp.broadcast_to(
        jnp.sum(total * total, axis=0, keepdims=True), (8, 128)
    )


def adjoint_mix_body(
    near_ref, next_ref, far_ref, last_ref, t_ref, high_ref, low_ref, extra_ref, out_ref
):
    lane = lax.broadcasted_iota(jnp.int32, (KX, 128), 1)
    total = jnp.zeros((KX, 128), F32)
    cross = jnp.zeros((KX, 128), F32)
    for k in range(KOWN):
        own = slice(KX * k, KX * k + KX)
        spectrum = (near_ref[own, :] + next_ref[own, :]) + (far_ref[own, :] + last_ref[own, :])
        turned = minus_i(spectrum)
        for ab in range(16):
            base = (ab // 4) * 32 + (ab % 4) * 6 + 2 * k
            plane = t_ref[pl.ds((k * 24 + ab) * KX, KX), :]
            re = jnp.sum(spectrum * plane, axis=1, keepdims=True)
            im = jnp.sum(turned * plane, axis=1, keepdims=True)
            total = jnp.where(lane == base, re, total)
            total = jnp.where(lane == base + 1, im, total)
        sh, sl = split(spectrum)
        cross = cross + dot(sh, high_ref[k]) + dot(sl, high_ref[k]) + dot(sh, low_ref[k])
    total = total * (1.0 / VELOCITY_SCALE)
    product = jnp.sum(total * cross, axis=0, keepdims=True)
    own = slice(MODES, MODES + 1)
    squares = (near_ref[own, :] + next_ref[own, :]) + (far_ref[own, :] + last_ref[own, :])
    for z in range(SPACE // 2):
        out_ref[z, :KX, :] = total
        out_ref[z, KX : KX + 1, :] = product
        out_ref[z, KX + 1 : KX + 5, :] = extra_ref[0:4, :]
        out_ref[z, KX + 5 : KX + 6, :] = squares
        out_ref[z, KX + 6 : KX + 8, :] = jnp.zeros((2, 128), F32)


def output_body(
    own, shot, m_ref, other_ref, back_ref, block_ref, local_ref, diag_rows_ref, off_rows_ref, diag_ref, off_ref,
    out_ref, misfit_ref, tmp,
):
    lane = lax.broadcasted_iota(jnp.int32, (KX, 128), 1)
    upper, lower = [], []
    tail = jnp.zeros((8, 128), F32)
    even = own[0] % 2 == 0
    for q in range(SPACE):
        mine, theirs = m_ref[q // 2], other_ref[q // 2]
        whole = jnp.where(even, mine, theirs) if q % 2 == 0 else jnp.where(even, theirs, mine)
        x = whole[:KX]
        tail = tail + whole[KX:]
        turned = jnp.where(lane % 2 == 0, -pltpu.roll(x, 127, 1), pltpu.roll(x, 1, 1))
        upper.append(x)
        lower.append(turned)
    n = jnp.concatenate(
        [jnp.concatenate(upper, axis=1), jnp.concatenate(lower, axis=1)], axis=0
    )
    high, low = split(n)
    nearly = dot(off_rows_ref[...], high)
    diag = jnp.concatenate([diag_rows_ref[...]] * 8, axis=1)
    left = n * diag + nearly
    right = n * diag_ref[...] + dot(high, off_ref[...])
    square = jnp.sum(jnp.sum(left * right, axis=0, keepdims=True), axis=1, keepdims=True)
    sums = jnp.sum(tail, axis=1, keepdims=True)
    total = square + 2.0 * sums[0:1] + sums[5:6]
    scale = 1.0 / jnp.sqrt(total / float(16 * GH * GW) + EPSILON)
    rows = dot(back_ref[0], high) + dot(back_ref[0], low)
    group = lax.broadcasted_iota(jnp.int32, (ROWS, 1024), 1) % 128 // 32
    rows = jnp.concatenate([jnp.where(group == a, rows, 0.0) for a in range(4)], axis=0)
    rh, rl = split(rows)
    block = dot(rh, block_ref[0]) + dot(rl, block_ref[0])
    for a in range(4):
        tmp[pl.ds(a, ROWS, stride=4), 0:64] = block[ROWS * a : ROWS * a + ROWS]
    out_ref[...] = (tmp[...].T[0:64] + local_ref[...]) * scale
    place = lax.broadcasted_iota(jnp.int32, (1, 4), 1)
    misfit = jnp.zeros((1, 4), F32)
    for s in range(4):
        misfit = jnp.where(place == s, sums[s + 1 : s + 2] * (0.5 / float(REC * GW)), misfit)
    misfit_ref[...] = misfit


def turn(size, stride, count, by):
    pairs = []
    for i in range(count):
        digit = (i // stride) % size
        pairs.append((i, i + ((digit + by) % size - digit) * stride))
    return pairs


def from_x(*parts):
    return [
        lax.ppermute(part, "shot", turn(4, 1, SHOT, by + 1)) for by, part in enumerate(parts)
    ]


def from_y(*parts):
    return [
        lax.ppermute(part, "shot", turn(4, 4, SHOT, by + 1)) for by, part in enumerate(parts)
    ]


def gather_space(copies):
    mine = lax.all_to_all(
        copies, "space", 0, 0, axis_index_groups=[[0, 2, 4, 6], [1, 3, 5, 7]], tiled=True
    )
    return mine, lax.ppermute(mine, "space", [(n, n ^ 1) for n in range(SPACE)])


def shards(
    velocity,
    encoder_weight,
    encoder_bias,
    source_amplitude,
    source_row,
    source_column,
    receiver_rows,
    point_weight,
    spectral_weight,
    layer_bias,
    out_weight,
    observed,
):
    p = lax.axis_index("space").astype(jnp.int32)
    i = lax.axis_index("shot").astype(jnp.int32)
    own, shot = p[None], i[None]
    fine = (128, 4 * GW)
    operator_rows = KOWN * KX * 24
    encoder = encoder_weight.reshape(16, C)
    bias, amplitude = encoder_bias[None], source_amplitude[None]
    rows = receiver_rows.reshape(PAIRS)
    index = jnp.stack(
        [rows, jnp.repeat(source_row, REC), jnp.repeat(source_column, REC)], axis=1
    ).astype(F32)
    both_rows = jnp.asarray(BOTH_ROWS)
    table = jnp.asarray(WEIGHTED)
    record = observed.reshape(PAIRS, GW)
    row_spec = full_spec((1, C))

    partial = call(
        velocity_body, 1, shaped((SPACE, KX, 128)),
        [full_spec(fine), full_spec((4 * GW, 256)), own_spec((192, 256))],
        full_spec((SPACE, KX, 128)), name="velocity_spectrum",
    )(own, velocity, jnp.asarray(COLUMNS), jnp.asarray(ROW_SUMS))
    spectra = lax.all_to_all(partial, "space", 0, 0, tiled=True)

    index, _ = lax.optimization_barrier((index, partial))
    operator, sides, bumps = call(
        operator_body, 1,
        (shaped((operator_rows, 128)), shaped((KOWN, PAIRS, 256), BF16), shaped((PAIRS, GW))),
        [
            full_spec((16, C)), row_spec, row_spec, full_spec((KX, KOWN, C, 128)),
            full_spec((PAIRS, 3)), full_spec((128, GH)), own_spec((8, GW)),
        ],
        (full_spec((operator_rows, 128)), full_spec((KOWN, PAIRS, 256)), full_spec((PAIRS, GW))),
        name="operator",
    )(
        own, encoder, bias, amplitude, spectral_weight, index, jnp.asarray(PAIRED_ROWS),
        jnp.asarray(OWN_COLUMNS),
    )

    sent = call(
        mix_body, 1, shaped((SPACE // 2, PAIRS, 384), BF16),
        [
            full_spec((SPACE, KX, 128)), own_spec((KX, 128)),
            full_spec((operator_rows, 128)), full_spec((KOWN, PAIRS, 256)),
        ],
        full_spec((SPACE // 2, PAIRS, 384)), name="mix_modes",
    )(own, spectra, jnp.asarray(ONES), operator, sides)
    gathered, others = gather_space(sent)

    late_bias, _ = lax.optimization_barrier((layer_bias[None], sent))
    planes, wk, vectors, placed, spread_high, spread_low = call(
        planes_body, 1,
        (
            shaped((ROWS, 16, GW)), shaped((48, C), BF16), shaped((3, C, 128)),
            shaped((8, 128, 128), BF16), shaped((KOWN, 128, 128), BF16),
            shaped((KOWN, 128, 128), BF16),
        ),
        [
            full_spec(fine), full_spec((512, 512)), full_spec((16, C)), row_spec, row_spec,
            full_spec((C, C)), row_spec, row_spec, full_spec((KOWN * 2, 128, 128)),
        ],
        (
            full_spec((ROWS, 16, GW)), full_spec((48, C)), full_spec((3, C, 128)),
            full_spec((8, 128, 128)), full_spec((KOWN, 128, 128)), full_spec((KOWN, 128, 128)),
        ),
        [pltpu.VMEM((128, 512), F32)], name="velocity_planes",
    )(
        own, velocity, jnp.asarray(SELECT), encoder, bias, amplitude, point_weight, late_bias,
        out_weight[None], jnp.asarray(LANES),
    )

    predicted, slopes, stats = call(
        forward_body, 2,
        (shaped((PAIRS, GW)), shaped((PAIRS * C, GW), BF16), shaped((SPACE, 8, 128))),
        [
            full_spec((SPACE // 2, PAIRS, 384)), full_spec((SPACE // 2, PAIRS, 384)),
            full_spec((ROWS, 16, GW)), full_spec((48, GW)),
            full_spec((48, C)), full_spec((PAIRS, GW)), full_spec((3, C, 128)),
            full_spec((PAIRS, GW)),
        ],
        (full_spec((PAIRS, GW)), full_spec((PAIRS * C, GW)), full_spec((SPACE, 8, 128))),
        [pltpu.VMEM((3 * SPACE * PAIRS, 128), F32), pltpu.VMEM((8, GW), F32)], name="forward_rows",
    )(own, rows, gathered, others, planes, table, wk, bumps, vectors, record)
    stats = lax.all_to_all(stats, "space", 0, 0, tiled=True)

    columns, near, after, far, last, misfits = call(
        backward_body, 3,
        (shaped((SPACE, ROWS, 384), BF16),) + (shaped((GW, 128), BF16),) * 4 + (shaped((8, 128)),),
        [
            full_spec((SPACE, 8, 128)), full_spec((PAIRS, GW)),
            full_spec((PAIRS, GW)), full_spec((PAIRS * C, GW)), full_spec((48, GW)),
            full_spec((8, 128, 128)),
        ],
        (full_spec((SPACE, ROWS, 384)),) + (full_spec((GW, 128)),) * 4 + (full_spec((8, 128)),),
        [
            pltpu.VMEM((16, GW), F32), pltpu.VMEM((ROWS * 48, 128), F32),
            pltpu.VMEM((4, GW, 128), F32),
        ],
        name="backward_rows",
    )(own, rows, shot, stats, record, predicted, slopes, table, placed)

    columns = lax.all_to_all(columns, "space", 0, 0, tiled=True)
    adjoint = call(
        adjoint_body, 0, shaped((KOWN * KX, 128)),
        [full_spec((SPACE, ROWS, 384)), full_spec((96, GH))],
        full_spec((KOWN * KX, 128)), name="adjoint_rows",
    )(columns, both_rows)
    arrived = from_x(after, far, last)
    blocks = call(
        along_x_body, 1, (shaped((128, 128)),) * 4, [full_spec((GW, 128))] * 4,
        (full_spec((128, 128)),) * 4, [pltpu.VMEM((GW, 128), F32)], name="along_x",
    )(shot, near, *arrived)
    sums = call(
        along_y_body, 0, shaped((MODES + 128, 128)),
        [full_spec((128, 128))] * 4 + [full_spec((MODES, 128))],
        full_spec((MODES + 128, 128)), name="along_y",
    )(blocks[0], *from_y(*blocks[1:]), adjoint)
    local, sums = call(
        along_z_body, 1, (shaped((64, 128)), shaped((MODES + 8, 128))),
        [full_spec((MODES + 128, 128))] * 2,
        (full_spec((64, 128)), full_spec((MODES + 8, 128))), [pltpu.VMEM((128, 128), F32)],
        name="along_z",
    )(shot, sums, lax.ppermute(sums, "shot", turn(2, 16, SHOT, 1)))
    parts = from_x(sums, sums, sums)
    sums = (sums + parts[0]) + (parts[1] + parts[2])

    modes = call(
        adjoint_mix_body, 0, shaped((SPACE // 2, KX + 8, 128)),
        [full_spec((MODES + 8, 128))] * 4
        + [
            full_spec((operator_rows, 128)), full_spec((KOWN, 128, 128)),
            full_spec((KOWN, 128, 128)), full_spec((8, 128)),
        ],
        full_spec((SPACE // 2, KX + 8, 128)), name="adjoint_mix",
    )(sums, *from_y(sums, sums, sums), operator, spread_high, spread_low, misfits)
    modes, other_modes = gather_space(modes)
    local = local.reshape(4, 16, 8, 4, 4).transpose(1, 4, 0, 2, 3).reshape(64, 128)

    block, misfit = call(
        output_body, 2, (shaped((64, 128)), shaped((1, 4))),
        [
            full_spec((SPACE // 2, KX + 8, 128)), full_spec((SPACE // 2, KX + 8, 128)),
            own_spec((ROWS, 96)), own_spec((1024, 64), 1),
            full_spec((64, 128)), full_spec((96, 128)), full_spec((96, 96)),
            full_spec((1, 1024)), full_spec((1024, 1024)),
        ],
        (full_spec((64, 128)), full_spec((1, 4))), [pltpu.VMEM((128, 128), F32)],
        name="output_block",
    )(
        own, shot, modes, other_modes, jnp.asarray(ROWS_BACK), jnp.asarray(BLOCKS), local, jnp.asarray(DIAG_ROWS),
        jnp.asarray(OFF_ROWS), jnp.asarray(DIAG_WIDE), jnp.asarray(OFF_WIDE),
    )
    return (misfit.reshape(4), block.T)


def solution(mesh):
    in_specs = (
        P("space", None),
        P(),
        P(),
        P(),
        P("shot"),
        P("shot"),
        P("shot", None),
        P(),
        P(None, "space", None, None),
        P(),
        P(),
        P("shot", None, None),
    )
    out_specs = (P("shot"), P("space", "shot"))
    return jax.shard_map(shards, mesh=mesh, in_specs=in_specs, out_specs=out_specs, check_vma=False)
```

```python
import math

import jax
import jax.numpy as jnp
import ml_dtypes
import numpy as np
from jax import lax
from jax.experimental import pallas as pl
from jax.experimental.pallas import tpu as pltpu
from jax.sharding import PartitionSpec as P

C = 64
KX = 48
KY = 24
GH = 256
GW = 512
REC = 16
SPACE = 8
SHOT = 32
ROWS = GH // SPACE
KOWN = KY // SPACE
COUNT = 64
FIRST = 72
PAIRS = 64
EPSILON = 1e-06
VELOCITY_MEAN = 3.0
VELOCITY_SCALE = 1.5
HIGHEST = lax.Precision.HIGHEST
F32 = jnp.float32
BF16 = jnp.bfloat16
SMALL = 28 << 20
LARGE = 56 << 20


def bf(values):
    return np.asarray(values, np.float32).astype(ml_dtypes.bfloat16)


def as64(values):
    return values.astype(np.float64)


def make_tables():
    k = np.arange(KY)
    w = np.arange(GW)
    phase = (k[:, None] * w[None, :] % GW) * (2.0 * math.pi / GW)
    plain = bf(np.stack([np.cos(phase), -np.sin(phase)], 1) / math.sqrt(GW))
    f = np.where(np.arange(KX) < KX // 2, np.arange(KX), np.arange(KX) - KX)
    phase = (f[:, None] * np.arange(GH)[None, :] % GH) * (2.0 * math.pi / GH)
    cos_rows = bf(np.cos(phase) / math.sqrt(GH))
    sin_rows = bf(np.sin(phase) / math.sqrt(GH))
    return plain, cos_rows, sin_rows


PLAIN, COS_ROWS, SIN_ROWS = make_tables()
MODE_WEIGHT = np.where(np.arange(KY) == 0, 1.0, 2.0)


def columns_table():
    table = np.zeros((GW, 4, SPACE, 32), np.float32)
    plain = PLAIN.astype(np.float32).reshape(SPACE, 6, GW)
    for b in range(4):
        table[:, b, :, 6 * b : 6 * b + 6] = plain.transpose(2, 0, 1)
    return bf(table.reshape(4 * GW, 256))


def rows_table():
    table = np.zeros((SPACE, 4, KX, 2, ROWS, 4), np.float32)
    for p in range(SPACE):
        for a in range(4):
            table[p, a, :, 0, :, a] = COS_ROWS[:, ROWS * p : ROWS * p + ROWS]
            table[p, a, :, 1, :, a] = SIN_ROWS[:, ROWS * p : ROWS * p + ROWS]
    return bf(table.reshape(SPACE, 4 * KX, 256))


def ones_table():
    wsum = as64(PLAIN).sum(-1)
    c, s = as64(COS_ROWS).sum(-1), as64(SIN_ROWS).sum(-1)
    table = np.zeros((SPACE, KX, 128), np.float32)
    for q in range(SPACE):
        for k in range(KOWN):
            re, im = wsum[3 * q + k]
            table[q, :, 24 + 2 * k] = c * re + s * im
            table[q, :, 25 + 2 * k] = c * im - s * re
    return table


def select_table():
    table = np.zeros((128, 4, 4, 128), np.float32)
    for b in range(4):
        table[np.arange(128), b, b, np.arange(128)] = 1.0
    return bf(table.reshape(512, 512))


def weighted_table():
    plain = PLAIN.astype(np.float32) * MODE_WEIGHT[:, None, None]
    return bf(plain.reshape(SPACE, KOWN, 2, GW).transpose(1, 2, 0, 3).reshape(48, GW))


def gram_tables():
    full = np.concatenate([as64(COS_ROWS), as64(SIN_ROWS)], 0)
    gram_rows = full @ full.T
    e = as64(PLAIN).reshape(48, GW)
    gram = e @ e.T
    wide = np.zeros((SPACE, 4, 32, SPACE, 4, 32))
    gram = gram.reshape(SPACE, 6, SPACE, 6)
    for a in range(4):
        for b in range(4):
            wide[:, a, b * 6 : b * 6 + 6, :, a, b * 6 : b * 6 + 6] = gram
    wide = wide.reshape(1024, 1024)
    diag_rows = np.broadcast_to(np.diag(gram_rows)[:, None], (96, 128))
    off_rows = bf(gram_rows - np.diag(np.diag(gram_rows)))
    diag_wide = np.diag(wide)[None, :]
    off_wide = bf(wide - np.diag(np.diag(wide)))
    return (
        np.asarray(diag_rows, np.float32),
        off_rows,
        np.asarray(diag_wide, np.float32),
        off_wide,
    )


COLUMNS = columns_table()
ROW_SUMS = rows_table()
ONES = ones_table()
SELECT = select_table()
WEIGHTED = weighted_table()
DIAG_ROWS, OFF_ROWS, DIAG_WIDE, OFF_WIDE = gram_tables()
PAIRED_ROWS = np.zeros((2, 64, GH), np.float32)
PAIRED_ROWS[0, :KX], PAIRED_ROWS[1, :KX] = COS_ROWS, SIN_ROWS
PAIRED_ROWS = bf(PAIRED_ROWS.reshape(128, GH))
OWN_COLUMNS = np.zeros((SPACE, 8, GW), np.float32)
OWN_COLUMNS[:, :6] = PLAIN.reshape(SPACE, 6, GW)
OWN_COLUMNS = bf(OWN_COLUMNS)


def lanes_table():
    table = np.zeros((KOWN, 2, 128, 128), np.float32)
    for k in range(KOWN):
        for part in range(2):
            for ab in range(16):
                table[k, part, ab, 32 * (ab // 4) + 6 * (ab % 4) + 2 * k + part] = 1.0
    return bf(table.reshape(KOWN * 2, 128, 128))


def block_table():
    table = np.zeros((SHOT, SPACE, 4, 32, 16, 4), np.float32)
    plain = PLAIN.astype(np.float32).reshape(SPACE, 6, SHOT, 16)
    for b in range(4):
        table[:, :, :, 6 * b : 6 * b + 6, :, b] = plain.transpose(2, 0, 1, 3)[:, :, None]
    return bf(table.reshape(SHOT, 1024, 64))


LANES = lanes_table()
BLOCKS = block_table()
BOTH_ROWS = bf(np.concatenate([COS_ROWS.astype(np.float32), SIN_ROWS.astype(np.float32)], 0))
ROWS_BACK = bf(
    BOTH_ROWS.astype(np.float32).T.reshape(SPACE, ROWS, 96)
)


def split(values):
    high = values.astype(BF16)
    return high, (values - high.astype(F32)).astype(BF16)


def dot(a, b, dims=((1,), (0,))):
    return lax.dot_general(a, b, (dims, ((), ())), preferred_element_type=F32)


def dot_split(a, b):
    high, low = split(b)
    return dot(a, high) + dot(a, low)


def minus_i(x):
    lane = lax.broadcasted_iota(jnp.int32, x.shape, 1)
    swapped = pltpu.roll(x, 64, 1)
    return jnp.where(lane < 64, swapped, -swapped)


def times_i(x):
    lane = lax.broadcasted_iota(jnp.int32, x.shape, 1)
    swapped = pltpu.roll(x, 64, 1)
    return jnp.where(lane < 64, -swapped, swapped)


def full_spec(shape):
    return pl.BlockSpec(shape, lambda *_: (0,) * len(shape))


def own_spec(shape, place=0):
    return pl.BlockSpec((1,) + shape, lambda i, *own: (own[place][0],) + (0,) * len(shape))


def kept_spec(shape):
    return pl.BlockSpec(memory_space=pltpu.VMEM)


def call(body, prefetch, out_shape, in_specs, out_specs, scratch=(), name=None, limit=LARGE):
    return pl.pallas_call(
        body,
        out_shape=out_shape,
        grid_spec=pltpu.PrefetchScalarGridSpec(
            num_scalar_prefetch=prefetch,
            grid=(1,),
            in_specs=in_specs,
            out_specs=out_specs,
            scratch_shapes=list(scratch),
        ),
        compiler_params=pltpu.CompilerParams(vmem_limit_bytes=limit),
        name=name,
    )


def shaped(shape, dtype=F32):
    return jax.ShapeDtypeStruct(shape, dtype)


def velocity_body(own, v_ref, cols_ref, rows_ref, out_ref):
    vn = (v_ref[...] - VELOCITY_MEAN) / VELOCITY_SCALE
    high, low = split(vn)
    xx = dot(high, cols_ref[...]) + dot(low, cols_ref[...])
    even = lax.broadcasted_iota(jnp.int32, xx.shape, 1) % 2 == 0
    turned = jnp.where(even, pltpu.roll(xx, 255, 1), -pltpu.roll(xx, 1, 1))
    stacked = jnp.concatenate([xx, turned], axis=0)
    yy = dot_split(rows_ref[0], stacked)
    group = lax.broadcasted_iota(jnp.int32, (KX, 128), 1) // 32
    for q in range(SPACE):
        total = jnp.zeros((KX, 128), F32)
        for a in range(4):
            piece = yy[KX * a : KX * a + KX, 128 * (q // 4) : 128 * (q // 4) + 128]
            shift = (32 * a - 32 * (q % 4)) % 128
            if shift:
                piece = pltpu.roll(piece, shift, 1)
            total = jnp.where(group == a, piece, total)
        out_ref[q] = total


def column_of(row):
    return jnp.broadcast_to(row, (128, C)).T


def planes_body(
    own, rows_ref, v_ref, sel_ref, enc_ref, bias_ref, amp_ref, point_ref, layer_ref, weight_ref, lanes_ref,
    out_ref, wk_ref, vec_ref, place_ref, high_ref, low_ref, list_ref, tmp,
):
    def find(r, count):
        row = rows_ref[r >> 4, r & 15] - own[0] * ROWS
        list_ref[count] = r
        list_ref[FIRST + count] = row
        return count + jnp.where((row >= 0) & (row < ROWS), 1, 0)

    list_ref[COUNT] = lax.fori_loop(0, PAIRS, find, 0)
    for m in range(4):
        vn = (v_ref[:, 512 * m : 512 * m + 512] - VELOCITY_MEAN) / VELOCITY_SCALE
        high, low = split(vn)
        tmp[...] = dot(high, sel_ref[...]) + dot(low, sel_ref[...])
        for h in range(ROWS):
            for b in range(4):
                out_ref[h, 4 * b : 4 * b + 4, 128 * m : 128 * m + 128] = tmp[
                    4 * h : 4 * h + 4, 128 * b : 128 * b + 128
                ]
    stack = jnp.concatenate(
        [enc_ref[...], bias_ref[...], amp_ref[...], jnp.zeros((6, C), F32)], axis=0
    )
    high, low = split(stack)
    pointed = dot(high, point_ref[...]) + dot(low, point_ref[...])
    swapped = jnp.concatenate(
        [pointed[4 * a + b : 4 * a + b + 1] for b in range(4) for a in range(4)], axis=0
    )
    high, low = split(swapped)
    wk_ref[0:16] = high
    wk_ref[16:32] = high
    wk_ref[32:48] = low
    vec_ref[0] = column_of(pointed[17:18])
    vec_ref[1] = column_of(pointed[16:17] + layer_ref[...])
    vec_ref[2] = column_of(weight_ref[...])
    turned = jnp.concatenate([pointed[:16], jnp.zeros((112, C), F32)], axis=0).T
    scaled = turned * (1.0 / VELOCITY_SCALE)
    for e in range(8):
        high, low = split(pltpu.roll(scaled, 16 * e, 1) if e else scaled)
        place_ref[e, 0:C] = high
        place_ref[e, C : 2 * C] = low
    th, tl = split(scaled)
    for k in range(KOWN):
        reach = jnp.where((own[0] == 0) & (k == 0), 1.0, 0.5)
        for part in range(2):
            wide = (dot(th, lanes_ref[2 * k + part]) + dot(tl, lanes_ref[2 * k + part])) * reach
            high, low = split(wide)
            high_ref[k, C * part : C * part + C] = high
            low_ref[k, C * part : C * part + C] = low


def operator_body(
    own, source_row, source_column, enc_ref, bias_ref, amp_ref, w_ref, index_ref, rows_ref,
    cols_ref, out_ref, side_ref, bump_ref,
):
    stack = jnp.concatenate(
        [enc_ref[...], bias_ref[...], amp_ref[...], jnp.zeros((6, C), F32)], axis=0
    )
    high, low = split(stack)
    lhs = jnp.concatenate([high.astype(F32), low.astype(F32)], axis=0).astype(BF16)

    def step(j, carry):
        for k in range(KOWN):
            both = dot(lhs, w_ref[j, k])
            out_ref[pl.ds(k * KX * 24 + j, 24, stride=KX), :] = both[:24] + both[24:]
        return carry

    lax.fori_loop(0, KX, step, 0, unroll=8)
    square = (REC, REC)
    same = lax.broadcasted_iota(jnp.int32, square, 0) == lax.broadcasted_iota(jnp.int32, square, 1)
    receivers, row, column = [], [], []
    for s in range(4):
        wide = jnp.broadcast_to(index_ref[s : s + 1, :].astype(F32), square)
        receivers.append(jnp.sum(jnp.where(same, wide, 0.0), axis=1, keepdims=True))
        row.append(jnp.full((REC, 1), source_row[s], jnp.int32).astype(F32))
        column.append(jnp.full((REC, 1), source_column[s], jnp.int32).astype(F32))
    receiver = jnp.concatenate(receivers, axis=0)
    row = jnp.concatenate(row, axis=0)
    column = jnp.concatenate(column, axis=0)
    line = lax.broadcasted_iota(jnp.int32, (PAIRS, GH), 1).astype(F32)
    chosen = jnp.where(line == receiver, 1.0, 0.0).astype(BF16)
    at_rows = dot(chosen, rows_ref[...], ((1,), (1,)))
    gap = line - row
    high, low = split(jnp.exp(gap * gap * (-1.0 / 32.0)))
    row_side = dot(high, rows_ref[...], ((1,), (1,))) + dot(low, rows_ref[...], ((1,), (1,)))
    gap = lax.broadcasted_iota(jnp.int32, (PAIRS, GW), 1).astype(F32) - column
    bump = jnp.exp(gap * gap * (-1.0 / 32.0))
    high, low = split(bump)
    column_side = dot(high, cols_ref[0], ((1,), (1,))) + dot(low, cols_ref[0], ((1,), (1,)))
    gap = receiver - row
    bump_ref[...] = bump * jnp.exp(gap * gap * (-1.0 / 32.0))
    lane = lax.broadcasted_iota(jnp.int32, (PAIRS, 128), 1)
    first = at_rows * row_side
    second = at_rows * pltpu.roll(row_side, 64, 1)
    both = jnp.where(
        lane < 64, first + pltpu.roll(first, 64, 1), second - pltpu.roll(second, 64, 1)
    )
    turned = times_i(both)
    for k in range(KOWN):
        side_ref[k, :, 0:128] = at_rows.astype(BF16)
        side_ref[k, :, 128:256] = (
            both * column_side[:, 2 * k : 2 * k + 1] + turned * column_side[:, 2 * k + 1 : 2 * k + 2]
        ).astype(BF16)


def mix_body(own, v_ref, ones_ref, t_ref, l_ref, out_ref):
    spectrum = ones_ref[0]
    for q in range(SPACE):
        spectrum = spectrum + v_ref[q]
    for k in range(KOWN):
        first = jnp.zeros((KX, 128), F32)
        second = jnp.zeros((KX, 128), F32)
        for ab in range(17):
            lane = (ab // 4) * 32 + (ab % 4) * 6 + 2 * k if ab < 16 else 24 + 2 * k
            plane = t_ref[pl.ds((k * 24 + ab) * KX, KX), :]
            first = first + spectrum[:, lane : lane + 1] * plane
            second = second + spectrum[:, lane + 1 : lane + 2] * plane
        modes = first + times_i(second)
        source = t_ref[pl.ds((k * 24 + 17) * KX, KX), :]
        none = jnp.zeros((16, 128), F32)
        rhs = jnp.concatenate(
            [modes, none, times_i(modes), none, source, none, times_i(source), none], axis=0
        )
        values = dot(l_ref[k], rhs.astype(BF16)).astype(BF16)
        for z in range(SPACE // 2):
            out_ref[z, :, 128 * k : 128 * k + 128] = values


def gain_row():
    return 0.5 + lax.broadcasted_iota(jnp.int32, (1, GW), 1).astype(F32) * (1.0 / GW)


def forward_body(
    own, list_ref, d_ref, other_ref, planes_ref, table_ref, wk_ref, col_ref, vec_ref, obs_ref,
    pred_ref, slope_ref, stats_ref, dd, acc, slopes, sems,
):
    p = own[0]
    count = list_ref[COUNT]
    gain = gain_row()
    for m in range(3):
        for z in range(SPACE // 2):
            for source, core in ((d_ref, p % 2), (other_ref, 1 - p % 2)):
                start = pl.multiple_of(PAIRS * (SPACE * m + 2 * z + core), PAIRS)
                dd[pl.ds(start, PAIRS), :] = source[z, :, 128 * m : 128 * m + 128].astype(F32)
    acc[...] = jnp.zeros_like(acc)
    root = math.sqrt(2.0 / math.pi)

    def preactivation(n):
        r = list_ref[n]
        pieces = []
        for m in range(3):
            block = dd[pl.ds(SPACE * PAIRS * m + r, SPACE, stride=PAIRS), :]
            pieces.append(block[:, :64])
            pieces.append(pltpu.roll(block, 64, 1)[:, :64])
        lhs = jnp.concatenate(pieces, axis=0).astype(BF16)
        lhs = jnp.concatenate([lhs, wk_ref[...]], axis=0)
        high, low = split(planes_ref[list_ref[FIRST + n]])
        rhs = jnp.concatenate([table_ref[...], high, low, high], axis=0)
        return r, dot(lhs, rhs, ((0,), (0,)))

    def outgoing(t):
        rows = pl.ds(pl.multiple_of(2 * C * t, 2 * C), 2 * C)
        return pltpu.make_async_copy(slopes.at[rows], slope_ref.at[rows], sems.at[t])

    def step(t, carry):
        second = jnp.minimum(2 * t + 1, count - 1)
        both = [preactivation(2 * t), preactivation(second)]
        weights = [1.0, jnp.where(2 * t + 1 < count, 1.0, 0.0)]
        for e, (r, x) in enumerate(both):
            amp, const, weight = vec_ref[0], vec_ref[1], vec_ref[2]
            col = col_ref[pl.ds(r, 1), :]
            total = []
            for m in range(4):
                lanes = slice(128 * m, 128 * m + 128)
                xm = x[:, lanes] + const + amp * col[:, lanes]
                square = xm * xm
                u = jnp.tanh(root * (xm + 0.044715 * (square * xm)))
                cdf = 0.5 * (1.0 + u)
                slope = cdf + xm * (
                    (0.5 * root) * (1.0 - u * u) * (1.0 + 3.0 * 0.044715 * square)
                )
                slopes[pl.ds(pl.multiple_of(C * (2 * t + e), C), C), lanes] = (
                    slope * weight
                ).astype(BF16)
                total.append(jnp.sum(weight * (xm * cdf), axis=0, keepdims=True))
            predicted = jnp.concatenate(total, axis=1)
            pred_ref[pl.ds(r, 1), :] = predicted
            weighted = predicted * gain * weights[e]
            target = obs_ref[pl.ds(r, 1), :] * gain
            s = r >> 4
            acc[pl.ds(s, 1), :] += weighted * weighted
            acc[pl.ds(s + 4, 1), :] += weighted * target
        outgoing(t).start()
        return carry

    def finish(t, carry):
        outgoing(t).wait()
        return carry

    lax.fori_loop(0, (count + 1) >> 1, step, 0)
    stats = acc[:, :128] + acc[:, 128:256] + acc[:, 256:384] + acc[:, 384:]
    for q in range(SPACE):
        stats_ref[q] = stats
    lax.fori_loop(0, (count + 1) >> 1, finish, 0)


def backward_body(
    own, list_ref, shot, stats_ref, obs_ref, pred_ref, slope_ref, table_ref, place_ref,
    cols_ref, near_ref, next_ref, far_ref, last_ref, misfit_ref, coef, acc, planes, slopes, sems,
):
    pairs = list_ref[COUNT]

    def incoming(t):
        rows = pl.ds(pl.multiple_of(2 * C * t, 2 * C), 2 * C)
        return pltpu.make_async_copy(slope_ref.at[rows], slopes.at[rows], sems.at[t])

    def begin(t, carry):
        incoming(t).start()
        return carry

    lax.fori_loop(0, (pairs + 1) >> 1, begin, 0)
    count = float(REC * GW)
    stats = stats_ref[0]
    for q in range(1, SPACE):
        stats = stats + stats_ref[q]
    stats = jnp.sum(stats, axis=1, keepdims=True)
    gain = gain_row()
    for s in range(4):
        target = obs_ref[REC * s : REC * s + REC, :] * gain
        tt = jnp.sum(jnp.sum(target * target, axis=0, keepdims=True), axis=1, keepdims=True) / count
        ww = stats[s : s + 1] / count
        wt = stats[s + 4 : s + 5] / count
        sp2 = ww + EPSILON
        isp = 1.0 / jnp.sqrt(sp2)
        isq = 1.0 / jnp.sqrt(tt + EPSILON)
        kappa = ww / sp2 - wt * isp * isq
        coef[s : s + 1, :] = jnp.broadcast_to(isp, (1, GW))
        coef[s + 4 : s + 5, :] = jnp.broadcast_to(isq, (1, GW))
        coef[s + 8 : s + 9, :] = jnp.broadcast_to(kappa, (1, GW))
        coef[s + 12 : s + 13, :] = jnp.zeros((1, GW), F32)
    acc[...] = jnp.zeros_like(acc)
    planes[...] = jnp.zeros_like(planes)

    def inner_gradient(t, e, r, valid):
        s = r >> 4
        isp = coef[pl.ds(s, 1), :]
        isq = coef[pl.ds(s + 4, 1), :]
        kappa = coef[pl.ds(s + 8, 1), :]
        weighted = pred_ref[pl.ds(r, 1), :] * gain * isp
        target = obs_ref[pl.ds(r, 1), :] * gain * isq
        differ = (weighted - target) * valid
        coef[pl.ds(s + 12, 1), :] += differ * differ
        data = (GH * GW / count) * gain * isp * (differ - kappa * weighted * valid)
        slope = slopes[pl.ds(pl.multiple_of(C * (2 * t + e), C), C), :].astype(F32)
        return (slope * data).astype(BF16)

    def step(t, carry):
        second = jnp.minimum(2 * t + 1, pairs - 1)
        valid = jnp.where(2 * t + 1 < pairs, 1.0, 0.0)
        incoming(t).wait()
        one = inner_gradient(t, 0, list_ref[2 * t], 1.0)
        two = inner_gradient(t, 1, list_ref[second], valid)
        spectra = dot(table_ref[...], jnp.concatenate([one, two], axis=0), ((1,), (1,)))
        for e, (n, inner) in enumerate(((2 * t, one), (second, two))):
            row = list_ref[FIRST + n]
            half = slice(64 * e, 64 * e + 64)
            acc[pl.ds(pl.multiple_of(row * 48, 8), 48), half] += spectra[:, half]
            twice = jnp.concatenate([inner, inner], axis=0)
            planes[row >> 3] += dot(twice, place_ref[row & 7], ((0,), (0,)))
        return carry

    lax.fori_loop(0, (pairs + 1) >> 1, step, 0)
    lane = lax.broadcasted_iota(jnp.int32, (ROWS, 128), 1)
    for q in range(SPACE):
        for m in range(3):
            even = acc[pl.ds(16 * m + q, ROWS, stride=48), :]
            odd = acc[pl.ds(16 * m + 8 + q, ROWS, stride=48), :]
            joined = jnp.where(lane < 64, even + pltpu.roll(even, 64, 1), odd + pltpu.roll(odd, 64, 1))
            cols_ref[q, :, 128 * m : 128 * m + 128] = joined.astype(BF16)
    x = shot[0] % 4
    for by, grad_ref in enumerate((near_ref, next_ref, far_ref, last_ref)):
        column = (x + by) % 4
        for zy in range(8):
            for g in range(4):
                start = pl.multiple_of(64 * zy + 16 * column, 16)
                grad_ref[64 * zy + 16 * g : 64 * zy + 16 * g + 16, :] = planes[
                    g, pl.ds(start, 16), :
                ].astype(BF16)
    for s in range(4):
        row = coef[s + 12 : s + 13, :]
        misfit_ref[s : s + 1, :] = (
            row[:, :128] + row[:, 128:256] + row[:, 256:384] + row[:, 384:]
        )
    misfit_ref[4:8, :] = jnp.zeros((4, 128), F32)


def adjoint_body(a_ref, rows_ref, out_ref):
    values = jnp.concatenate([a_ref[q] for q in range(SPACE)], axis=0)
    y = dot(rows_ref[...], values)
    for k in range(KOWN):
        lanes = slice(128 * k, 128 * k + 128)
        out_ref[KX * k : KX * k + KX, :] = y[:KX, lanes] + minus_i(y[KX:, lanes])


MODES = KOWN * KX


def along_x_body(shot, a_ref, b_ref, c_ref, d_ref, near_ref, next_ref, far_ref, last_ref, tmp):
    tmp[...] = (a_ref[...].astype(F32) + b_ref[...].astype(F32)) + (
        c_ref[...].astype(F32) + d_ref[...].astype(F32)
    )
    y = shot[0] // 4 % 4
    for by, out_ref in enumerate((near_ref, next_ref, far_ref, last_ref)):
        for z in range(2):
            start = pl.multiple_of(64 * (4 * z + (y + by) % 4), 64)
            out_ref[64 * z : 64 * z + 64, :] = tmp[pl.ds(start, 64), :]


def along_y_body(a_ref, b_ref, c_ref, d_ref, modes_ref, out_ref):
    out_ref[0:MODES, :] = modes_ref[...]
    out_ref[MODES:, :] = (a_ref[...] + b_ref[...]) + (c_ref[...] + d_ref[...])


def along_z_body(shot, a_ref, b_ref, local_ref, out_ref, tmp):
    out_ref[0:MODES, :] = a_ref[0:MODES, :] + b_ref[0:MODES, :]
    total = a_ref[MODES:, :] + b_ref[MODES:, :]
    tmp[...] = total
    local_ref[...] = tmp[pl.ds(pl.multiple_of(64 * (shot[0] // 16), 64), 64), :]
    out_ref[MODES : MODES + 8, :] = jnp.broadcast_to(
        jnp.sum(total * total, axis=0, keepdims=True), (8, 128)
    )


def adjoint_mix_body(
    near_ref, next_ref, far_ref, last_ref, t_ref, high_ref, low_ref, extra_ref, out_ref
):
    lane = lax.broadcasted_iota(jnp.int32, (KX, 128), 1)
    total = jnp.zeros((KX, 128), F32)
    cross = jnp.zeros((KX, 128), F32)
    for k in range(KOWN):
        own = slice(KX * k, KX * k + KX)
        spectrum = (near_ref[own, :] + next_ref[own, :]) + (far_ref[own, :] + last_ref[own, :])
        turned = minus_i(spectrum)
        for ab in range(16):
            base = (ab // 4) * 32 + (ab % 4) * 6 + 2 * k
            plane = t_ref[pl.ds((k * 24 + ab) * KX, KX), :]
            re = jnp.sum(spectrum * plane, axis=1, keepdims=True)
            im = jnp.sum(turned * plane, axis=1, keepdims=True)
            total = jnp.where(lane == base, re, total)
            total = jnp.where(lane == base + 1, im, total)
        sh, sl = split(spectrum)
        cross = cross + dot(sh, high_ref[k]) + dot(sl, high_ref[k]) + dot(sh, low_ref[k])
    total = total * (1.0 / VELOCITY_SCALE)
    product = jnp.sum(total * cross, axis=0, keepdims=True)
    own = slice(MODES, MODES + 1)
    squares = (near_ref[own, :] + next_ref[own, :]) + (far_ref[own, :] + last_ref[own, :])
    for z in range(SPACE // 2):
        out_ref[z, :KX, :] = total
        out_ref[z, KX : KX + 1, :] = product
        out_ref[z, KX + 1 : KX + 5, :] = extra_ref[0:4, :]
        out_ref[z, KX + 5 : KX + 6, :] = squares
        out_ref[z, KX + 6 : KX + 8, :] = jnp.zeros((2, 128), F32)


def output_body(
    own, m_ref, other_ref, back_ref, block_ref, local_ref, diag_rows_ref, off_rows_ref, diag_ref, off_ref,
    out_ref, misfit_ref, tmp,
):
    lane = lax.broadcasted_iota(jnp.int32, (KX, 128), 1)
    upper, lower = [], []
    tail = jnp.zeros((8, 128), F32)
    even = own[0] % 2 == 0
    for q in range(SPACE):
        mine, theirs = m_ref[q // 2], other_ref[q // 2]
        whole = jnp.where(even, mine, theirs) if q % 2 == 0 else jnp.where(even, theirs, mine)
        x = whole[:KX]
        tail = tail + whole[KX:]
        turned = jnp.where(lane % 2 == 0, -pltpu.roll(x, 127, 1), pltpu.roll(x, 1, 1))
        upper.append(x)
        lower.append(turned)
    n = jnp.concatenate(
        [jnp.concatenate(upper, axis=1), jnp.concatenate(lower, axis=1)], axis=0
    )
    high, low = split(n)
    nearly = dot(off_rows_ref[...], high)
    diag = jnp.concatenate([diag_rows_ref[...]] * 8, axis=1)
    left = n * diag + nearly
    right = n * diag_ref[...] + dot(high, off_ref[...])
    square = jnp.sum(jnp.sum(left * right, axis=0, keepdims=True), axis=1, keepdims=True)
    sums = jnp.sum(tail, axis=1, keepdims=True)
    total = square + 2.0 * sums[0:1] + sums[5:6]
    scale = 1.0 / jnp.sqrt(total / float(16 * GH * GW) + EPSILON)
    rows = dot(back_ref[0], high) + dot(back_ref[0], low)
    group = lax.broadcasted_iota(jnp.int32, (ROWS, 1024), 1) % 128 // 32
    rows = jnp.concatenate([jnp.where(group == a, rows, 0.0) for a in range(4)], axis=0)
    rh, rl = split(rows)
    block = dot(rh, block_ref[...]) + dot(rl, block_ref[...])
    for a in range(4):
        tmp[pl.ds(a, ROWS, stride=4), 0:64] = block[ROWS * a : ROWS * a + ROWS]
    out_ref[...] = (tmp[...].T[0:64] + local_ref[...]) * scale
    place = lax.broadcasted_iota(jnp.int32, (1, 4), 1)
    misfit = jnp.zeros((1, 4), F32)
    for s in range(4):
        misfit = jnp.where(place == s, sums[s + 1 : s + 2] * (0.5 / float(REC * GW)), misfit)
    misfit_ref[...] = misfit


def turn(size, stride, count, by):
    pairs = []
    for i in range(count):
        digit = (i // stride) % size
        pairs.append((i, i + ((digit + by) % size - digit) * stride))
    return pairs


def from_x(*parts):
    return [
        lax.ppermute(part, "shot", turn(4, 1, SHOT, by + 1)) for by, part in enumerate(parts)
    ]


def from_y(*parts):
    return [
        lax.ppermute(part, "shot", turn(4, 4, SHOT, by + 1)) for by, part in enumerate(parts)
    ]


def gather_z(copies):
    return lax.all_to_all(
        copies, "space", 0, 0, axis_index_groups=[[0, 2, 4, 6], [1, 3, 5, 7]], tiled=True
    )


def from_core(values):
    return lax.ppermute(values, "space", [(n, n ^ 1) for n in range(SPACE)])


def shards(
    velocity,
    encoder_weight,
    encoder_bias,
    source_amplitude,
    source_row,
    source_column,
    receiver_rows,
    point_weight,
    spectral_weight,
    layer_bias,
    out_weight,
    observed,
):
    p = lax.axis_index("space").astype(jnp.int32)
    i = lax.axis_index("shot").astype(jnp.int32)
    own, shot = p[None], i[None]
    fine = (128, 4 * GW)
    operator_rows = KOWN * KX * 24
    encoder = encoder_weight.reshape(16, C)
    bias, amplitude = encoder_bias[None], source_amplitude[None]
    both_rows = jnp.asarray(BOTH_ROWS)
    table = jnp.asarray(WEIGHTED)
    record = observed.reshape(PAIRS, GW)
    row_spec = full_spec((1, C))

    partial = call(
        velocity_body, 1, shaped((SPACE, KX, 128)),
        [full_spec(fine), full_spec((4 * GW, 256)), own_spec((192, 256))],
        kept_spec((SPACE, KX, 128)), name="velocity_spectrum",
    )(own, velocity, jnp.asarray(COLUMNS), jnp.asarray(ROW_SUMS))
    spectra = lax.all_to_all(partial, "space", 0, 0, tiled=True)

    bias, _ = lax.optimization_barrier((bias, partial))
    operator, sides, bumps = call(
        operator_body, 3,
        (shaped((operator_rows, 128)), shaped((KOWN, PAIRS, 256), BF16), shaped((PAIRS, GW))),
        [
            full_spec((16, C)), row_spec, row_spec, full_spec((KX, KOWN, C, 128)),
            full_spec((4, REC)), full_spec((128, GH)), own_spec((8, GW)),
        ],
        (full_spec((operator_rows, 128)), full_spec((KOWN, PAIRS, 256)), full_spec((PAIRS, GW))),
        name="operator",
    )(
        own, source_row, source_column, encoder, bias, amplitude, spectral_weight, receiver_rows,
        jnp.asarray(PAIRED_ROWS),
        jnp.asarray(OWN_COLUMNS),
    )

    sent = call(
        mix_body, 1, shaped((SPACE // 2, PAIRS, 384), BF16),
        [
            kept_spec((SPACE, KX, 128)), own_spec((KX, 128)),
            full_spec((operator_rows, 128)), full_spec((KOWN, PAIRS, 256)),
        ],
        kept_spec((SPACE // 2, PAIRS, 384)), name="mix_modes",
    )(own, spectra, jnp.asarray(ONES), operator, sides)
    gathered = gather_z(sent)

    mine = lax.dynamic_index_in_dim(jnp.asarray(BLOCKS), i, 0, keepdims=False)
    late_bias, _ = lax.optimization_barrier((layer_bias[None], sent))
    planes, wk, vectors, placed, spread_high, spread_low, pairs = call(
        planes_body, 2,
        (
            shaped((ROWS, 16, GW)), shaped((48, C), BF16), shaped((3, C, 128)),
            shaped((8, 128, 128), BF16), shaped((KOWN, 128, 128), BF16),
            shaped((KOWN, 128, 128), BF16), shaped((144,), jnp.int32),
        ),
        [
            full_spec(fine), full_spec((512, 512)), full_spec((16, C)), row_spec, row_spec,
            full_spec((C, C)), row_spec, row_spec, full_spec((KOWN * 2, 128, 128)),
        ],
        (
            full_spec((ROWS, 16, GW)), full_spec((48, C)), full_spec((3, C, 128)),
            full_spec((8, 128, 128)), full_spec((KOWN, 128, 128)), full_spec((KOWN, 128, 128)),
            pl.BlockSpec(memory_space=pltpu.SMEM),
        ),
        [pltpu.VMEM((128, 512), F32)], name="velocity_planes",
    )(
        own, receiver_rows, velocity, jnp.asarray(SELECT), encoder, bias, amplitude, point_weight, late_bias,
        out_weight[None], jnp.asarray(LANES),
    )

    gathered, planes, mine = lax.optimization_barrier((gathered, planes, mine))
    others = from_core(gathered)
    predicted, slopes, stats = call(
        forward_body, 2,
        (shaped((PAIRS, GW)), shaped((PAIRS * C, GW), BF16), shaped((SPACE, 8, 128))),
        [
            kept_spec((SPACE // 2, PAIRS, 384)), kept_spec((SPACE // 2, PAIRS, 384)),
            full_spec((ROWS, 16, GW)), full_spec((48, GW)),
            full_spec((48, C)), full_spec((PAIRS, GW)), full_spec((3, C, 128)),
            full_spec((PAIRS, GW)),
        ],
        (
            full_spec((PAIRS, GW)), pl.BlockSpec(memory_space=pl.ANY),
            kept_spec((SPACE, 8, 128)),
        ),
        [
            pltpu.VMEM((3 * SPACE * PAIRS, 128), F32), pltpu.VMEM((8, GW), F32),
            pltpu.VMEM((PAIRS * C, GW), BF16), pltpu.SemaphoreType.DMA((PAIRS // 2,)),
        ], name="forward_rows",
    )(own, pairs, gathered, others, planes, table, wk, bumps, vectors, record)
    stats = lax.all_to_all(stats, "space", 0, 0, tiled=True)

    columns, near, after, far, last, misfits = call(
        backward_body, 3,
        (shaped((SPACE, ROWS, 384), BF16),) + (shaped((GW, 128), BF16),) * 4 + (shaped((8, 128)),),
        [
            kept_spec((SPACE, 8, 128)), full_spec((PAIRS, GW)),
            full_spec((PAIRS, GW)), pl.BlockSpec(memory_space=pl.ANY), full_spec((48, GW)),
            full_spec((8, 128, 128)),
        ],
        (kept_spec((SPACE, ROWS, 384)),) + (kept_spec((GW, 128)),) * 4 + (full_spec((8, 128)),),
        [
            pltpu.VMEM((16, GW), F32), pltpu.VMEM((ROWS * 48, 128), F32),
            pltpu.VMEM((4, GW, 128), F32), pltpu.VMEM((PAIRS * C, GW), BF16),
            pltpu.SemaphoreType.DMA((PAIRS // 2,)),
        ],
        name="backward_rows",
    )(own, pairs, shot, stats, record, predicted, slopes, table, placed)

    columns = lax.all_to_all(columns, "space", 0, 0, tiled=True)
    adjoint = call(
        adjoint_body, 0, shaped((KOWN * KX, 128)),
        [kept_spec((SPACE, ROWS, 384)), full_spec((96, GH))],
        kept_spec((KOWN * KX, 128)), name="adjoint_rows", limit=SMALL,
    )(columns, both_rows)
    arrived = from_x(after, far, last)
    blocks = call(
        along_x_body, 1, (shaped((128, 128)),) * 4, [kept_spec((GW, 128))] * 4,
        (kept_spec((128, 128)),) * 4, [pltpu.VMEM((GW, 128), F32)], name="along_x", limit=SMALL,
    )(shot, near, *arrived)
    sums = call(
        along_y_body, 0, shaped((MODES + 128, 128)),
        [kept_spec((128, 128))] * 4 + [kept_spec((MODES, 128))],
        kept_spec((MODES + 128, 128)), name="along_y", limit=SMALL,
    )(blocks[0], *from_y(*blocks[1:]), adjoint)
    local, sums = call(
        along_z_body, 1, (shaped((64, 128)), shaped((MODES + 8, 128))),
        [kept_spec((MODES + 128, 128))] * 2,
        (kept_spec((64, 128)), kept_spec((MODES + 8, 128))), [pltpu.VMEM((128, 128), F32)],
        name="along_z", limit=SMALL,
    )(shot, sums, lax.ppermute(sums, "shot", turn(2, 16, SHOT, 1)))
    parts = from_x(sums, sums, sums)
    local = local.reshape(4, 16, 8, 4, 4).transpose(1, 4, 0, 2, 3).reshape(64, 128)
    parts, local = lax.optimization_barrier((parts, local))
    sums = (sums + parts[0]) + (parts[1] + parts[2])

    modes = call(
        adjoint_mix_body, 0, shaped((SPACE // 2, KX + 8, 128)),
        [kept_spec((MODES + 8, 128))] * 4
        + [
            full_spec((operator_rows, 128)), full_spec((KOWN, 128, 128)),
            full_spec((KOWN, 128, 128)), full_spec((8, 128)),
        ],
        kept_spec((SPACE // 2, KX + 8, 128)), name="adjoint_mix", limit=SMALL,
    )(sums, *from_y(sums, sums, sums), operator, spread_high, spread_low, misfits)
    modes = gather_z(modes)
    other_modes = from_core(modes)
    block, misfit = call(
        output_body, 1, (shaped((64, 128)), shaped((1, 4))),
        [
            kept_spec((SPACE // 2, KX + 8, 128)), kept_spec((SPACE // 2, KX + 8, 128)),
            own_spec((ROWS, 96)), full_spec((1024, 64)),
            full_spec((64, 128)), full_spec((96, 128)), full_spec((96, 96)),
            full_spec((1, 1024)), full_spec((1024, 1024)),
        ],
        (full_spec((64, 128)), full_spec((1, 4))), [pltpu.VMEM((128, 128), F32)],
        name="output_block", limit=SMALL,
    )(
        own, modes, other_modes, jnp.asarray(ROWS_BACK), mine, local, jnp.asarray(DIAG_ROWS),
        jnp.asarray(OFF_ROWS), jnp.asarray(DIAG_WIDE), jnp.asarray(OFF_WIDE),
    )
    return (misfit.reshape(4), block.T)


def solution(mesh):
    in_specs = (
        P("space", None),
        P(),
        P(),
        P(),
        P("shot"),
        P("shot"),
        P("shot", None),
        P(),
        P(None, "space", None, None),
        P(),
        P(),
        P("shot", None, None),
    )
    out_specs = (P("shot"), P("space", "shot"))
    return jax.shard_map(shards, mesh=mesh, in_specs=in_specs, out_specs=out_specs, check_vma=False)
```

```python
import math

import jax
import jax.numpy as jnp
import ml_dtypes
import numpy as np
from jax import lax
from jax.experimental import pallas as pl
from jax.experimental.pallas import tpu as pltpu
from jax.sharding import PartitionSpec as P

C = 64
KX = 48
KY = 24
GH = 256
GW = 512
REC = 16
SPACE = 8
SHOT = 32
ROWS = GH // SPACE
KOWN = KY // SPACE
COUNT = 64
FIRST = 72
PAIRS = 64
EPSILON = 1e-06
VELOCITY_MEAN = 3.0
VELOCITY_SCALE = 1.5
HIGHEST = lax.Precision.HIGHEST
F32 = jnp.float32
BF16 = jnp.bfloat16
SMALL = 28 << 20
LARGE = 56 << 20


def bf(values):
    return np.asarray(values, np.float32).astype(ml_dtypes.bfloat16)


def as64(values):
    return values.astype(np.float64)


def make_tables():
    k = np.arange(KY)
    w = np.arange(GW)
    phase = (k[:, None] * w[None, :] % GW) * (2.0 * math.pi / GW)
    plain = bf(np.stack([np.cos(phase), -np.sin(phase)], 1) / math.sqrt(GW))
    f = np.where(np.arange(KX) < KX // 2, np.arange(KX), np.arange(KX) - KX)
    phase = (f[:, None] * np.arange(GH)[None, :] % GH) * (2.0 * math.pi / GH)
    cos_rows = bf(np.cos(phase) / math.sqrt(GH))
    sin_rows = bf(np.sin(phase) / math.sqrt(GH))
    return plain, cos_rows, sin_rows


PLAIN, COS_ROWS, SIN_ROWS = make_tables()
MODE_WEIGHT = np.where(np.arange(KY) == 0, 1.0, 2.0)


def columns_table():
    table = np.zeros((GW, 4, SPACE, 32), np.float32)
    plain = PLAIN.astype(np.float32).reshape(SPACE, 6, GW)
    for b in range(4):
        table[:, b, :, 6 * b : 6 * b + 6] = plain.transpose(2, 0, 1)
    return bf(table.reshape(4 * GW, 256))


def rows_table():
    table = np.zeros((SPACE, 4, KX, 2, ROWS, 4), np.float32)
    for p in range(SPACE):
        for a in range(4):
            table[p, a, :, 0, :, a] = COS_ROWS[:, ROWS * p : ROWS * p + ROWS]
            table[p, a, :, 1, :, a] = SIN_ROWS[:, ROWS * p : ROWS * p + ROWS]
    return bf(table.reshape(SPACE, 4 * KX, 256))


def ones_table():
    wsum = as64(PLAIN).sum(-1)
    c, s = as64(COS_ROWS).sum(-1), as64(SIN_ROWS).sum(-1)
    table = np.zeros((SPACE, KX, 128), np.float32)
    for q in range(SPACE):
        for k in range(KOWN):
            re, im = wsum[3 * q + k]
            table[q, :, 24 + 2 * k] = c * re + s * im
            table[q, :, 25 + 2 * k] = c * im - s * re
    return table


def select_table():
    table = np.zeros((128, 4, 4, 128), np.float32)
    for b in range(4):
        table[np.arange(128), b, b, np.arange(128)] = 1.0
    return bf(table.reshape(512, 512))


def weighted_table():
    plain = PLAIN.astype(np.float32) * MODE_WEIGHT[:, None, None]
    return bf(plain.reshape(SPACE, KOWN, 2, GW).transpose(1, 2, 0, 3).reshape(48, GW))


def gram_tables():
    full = np.concatenate([as64(COS_ROWS), as64(SIN_ROWS)], 0)
    gram_rows = full @ full.T
    e = as64(PLAIN).reshape(48, GW)
    gram = e @ e.T
    wide = np.zeros((SPACE, 4, 32, SPACE, 4, 32))
    gram = gram.reshape(SPACE, 6, SPACE, 6)
    for a in range(4):
        for b in range(4):
            wide[:, a, b * 6 : b * 6 + 6, :, a, b * 6 : b * 6 + 6] = gram
    wide = wide.reshape(1024, 1024)
    diag_rows = np.broadcast_to(np.diag(gram_rows)[:, None], (96, 128))
    off_rows = bf(gram_rows - np.diag(np.diag(gram_rows)))
    diag_wide = np.diag(wide)[None, :]
    off_wide = bf(wide - np.diag(np.diag(wide)))
    return (
        np.asarray(diag_rows, np.float32),
        off_rows,
        np.asarray(diag_wide, np.float32),
        off_wide,
    )


COLUMNS = columns_table()
ROW_SUMS = rows_table()
ONES = ones_table()
SELECT = select_table()
WEIGHTED = weighted_table()
DIAG_ROWS, OFF_ROWS, DIAG_WIDE, OFF_WIDE = gram_tables()
PAIRED_ROWS = np.zeros((2, 64, GH), np.float32)
PAIRED_ROWS[0, :KX], PAIRED_ROWS[1, :KX] = COS_ROWS, SIN_ROWS
PAIRED_ROWS = bf(PAIRED_ROWS.reshape(128, GH))
OWN_COLUMNS = np.zeros((SPACE, 8, GW), np.float32)
OWN_COLUMNS[:, :6] = PLAIN.reshape(SPACE, 6, GW)
OWN_COLUMNS = bf(OWN_COLUMNS)


def lanes_table():
    table = np.zeros((KOWN, 2, 128, 128), np.float32)
    for k in range(KOWN):
        for part in range(2):
            for ab in range(16):
                table[k, part, ab, 32 * (ab // 4) + 6 * (ab % 4) + 2 * k + part] = 1.0
    return bf(table.reshape(KOWN * 2, 128, 128))


def block_table():
    table = np.zeros((SHOT, SPACE, 4, 32, 16, 4), np.float32)
    plain = PLAIN.astype(np.float32).reshape(SPACE, 6, SHOT, 16)
    for b in range(4):
        table[:, :, :, 6 * b : 6 * b + 6, :, b] = plain.transpose(2, 0, 1, 3)[:, :, None]
    return bf(table.reshape(SHOT, 1024, 64))


REPEAT = np.zeros((64, 16), np.float32)
REPEAT[np.arange(64), np.arange(64) // 4] = 1.0
REPEAT = bf(REPEAT)
PICK = np.zeros((4, 128, 128), np.float32)
for g in range(4):
    PICK[g, np.arange(128), 32 * g + np.arange(128) // 4] = 1.0
PICK = bf(PICK)
LANES = lanes_table()
BLOCKS = block_table()
BOTH_ROWS = bf(np.concatenate([COS_ROWS.astype(np.float32), SIN_ROWS.astype(np.float32)], 0))
ROWS_BACK = bf(
    BOTH_ROWS.astype(np.float32).T.reshape(SPACE, ROWS, 96)
)


def split(values):
    high = values.astype(BF16)
    return high, (values - high.astype(F32)).astype(BF16)


def dot(a, b, dims=((1,), (0,))):
    return lax.dot_general(a, b, (dims, ((), ())), preferred_element_type=F32)


def dot_split(a, b):
    high, low = split(b)
    return dot(a, high) + dot(a, low)


def minus_i(x):
    lane = lax.broadcasted_iota(jnp.int32, x.shape, 1)
    swapped = pltpu.roll(x, 64, 1)
    return jnp.where(lane < 64, swapped, -swapped)


def times_i(x):
    lane = lax.broadcasted_iota(jnp.int32, x.shape, 1)
    swapped = pltpu.roll(x, 64, 1)
    return jnp.where(lane < 64, -swapped, swapped)


def full_spec(shape):
    return pl.BlockSpec(shape, lambda *_: (0,) * len(shape))


def own_spec(shape, place=0):
    return pl.BlockSpec((1,) + shape, lambda i, *own: (own[place][0],) + (0,) * len(shape))


def kept_spec(shape):
    return pl.BlockSpec(memory_space=pltpu.VMEM)


def call(body, prefetch, out_shape, in_specs, out_specs, scratch=(), name=None, limit=LARGE):
    return pl.pallas_call(
        body,
        out_shape=out_shape,
        grid_spec=pltpu.PrefetchScalarGridSpec(
            num_scalar_prefetch=prefetch,
            grid=(1,),
            in_specs=in_specs,
            out_specs=out_specs,
            scratch_shapes=list(scratch),
        ),
        compiler_params=pltpu.CompilerParams(vmem_limit_bytes=limit),
        name=name,
    )


def shaped(shape, dtype=F32):
    return jax.ShapeDtypeStruct(shape, dtype)


def velocity_body(own, v_ref, cols_ref, rows_ref, out_ref):
    vn = (v_ref[...] - VELOCITY_MEAN) / VELOCITY_SCALE
    high, low = split(vn)
    xx = dot(high, cols_ref[...]) + dot(low, cols_ref[...])
    even = lax.broadcasted_iota(jnp.int32, xx.shape, 1) % 2 == 0
    turned = jnp.where(even, pltpu.roll(xx, 255, 1), -pltpu.roll(xx, 1, 1))
    stacked = jnp.concatenate([xx, turned], axis=0)
    yy = dot_split(rows_ref[0], stacked)
    group = lax.broadcasted_iota(jnp.int32, (KX, 128), 1) // 32
    for q in range(SPACE):
        total = jnp.zeros((KX, 128), F32)
        for a in range(4):
            piece = yy[KX * a : KX * a + KX, 128 * (q // 4) : 128 * (q // 4) + 128]
            shift = (32 * a - 32 * (q % 4)) % 128
            if shift:
                piece = pltpu.roll(piece, shift, 1)
            total = jnp.where(group == a, piece, total)
        out_ref[q] = total


def column_of(row):
    return jnp.broadcast_to(row, (128, C)).T


def planes_body(
    own, rows_ref, v_ref, sel_ref, enc_ref, bias_ref, amp_ref, point_ref, layer_ref, weight_ref, lanes_ref,
    out_ref, wk_ref, vec_ref, place_ref, high_ref, low_ref, list_ref, tmp,
):
    def find(r, count):
        row = rows_ref[r >> 4, r & 15] - own[0] * ROWS
        list_ref[count] = r
        list_ref[FIRST + count] = row
        return count + jnp.where((row >= 0) & (row < ROWS), 1, 0)

    list_ref[COUNT] = lax.fori_loop(0, PAIRS, find, 0)
    for m in range(4):
        vn = (v_ref[:, 512 * m : 512 * m + 512] - VELOCITY_MEAN) / VELOCITY_SCALE
        high, low = split(vn)
        tmp[...] = dot(high, sel_ref[...]) + dot(low, sel_ref[...])
        for h in range(ROWS):
            for b in range(4):
                out_ref[h, 4 * b : 4 * b + 4, 128 * m : 128 * m + 128] = tmp[
                    4 * h : 4 * h + 4, 128 * b : 128 * b + 128
                ]
    stack = jnp.concatenate(
        [enc_ref[...], bias_ref[...], amp_ref[...], jnp.zeros((6, C), F32)], axis=0
    )
    high, low = split(stack)
    pointed = dot(high, point_ref[...]) + dot(low, point_ref[...])
    swapped = jnp.concatenate(
        [pointed[4 * a + b : 4 * a + b + 1] for b in range(4) for a in range(4)], axis=0
    )
    high, low = split(swapped)
    wk_ref[0:16] = high
    wk_ref[16:32] = high
    wk_ref[32:48] = low
    vec_ref[0] = column_of(pointed[17:18])
    vec_ref[1] = column_of(pointed[16:17] + layer_ref[...])
    vec_ref[2] = column_of(weight_ref[...])
    turned = jnp.concatenate([pointed[:16], jnp.zeros((112, C), F32)], axis=0).T
    scaled = turned * (1.0 / VELOCITY_SCALE)
    for e in range(8):
        high, low = split(pltpu.roll(scaled, 16 * e, 1) if e else scaled)
        place_ref[e, 0:C] = high
        place_ref[e, C : 2 * C] = low
    th, tl = split(scaled)
    for k in range(KOWN):
        reach = jnp.where((own[0] == 0) & (k == 0), 1.0, 0.5)
        for part in range(2):
            wide = (dot(th, lanes_ref[2 * k + part]) + dot(tl, lanes_ref[2 * k + part])) * reach
            high, low = split(wide)
            high_ref[k, C * part : C * part + C] = high
            low_ref[k, C * part : C * part + C] = low


def operator_body(
    own, source_row, source_column, enc_ref, bias_ref, amp_ref, w_ref, index_ref, rows_ref,
    cols_ref, out_ref, side_ref, bump_ref,
):
    stack = jnp.concatenate(
        [enc_ref[...], bias_ref[...], amp_ref[...], jnp.zeros((6, C), F32)], axis=0
    )
    high, low = split(stack)
    lhs = jnp.concatenate([high.astype(F32), low.astype(F32)], axis=0).astype(BF16)

    def step(j, carry):
        for k in range(KOWN):
            both = dot(lhs, w_ref[j, k])
            out_ref[pl.ds(k * KX * 24 + j, 24, stride=KX), :] = both[:24] + both[24:]
        return carry

    lax.fori_loop(0, KX, step, 0, unroll=8)
    square = (REC, REC)
    same = lax.broadcasted_iota(jnp.int32, square, 0) == lax.broadcasted_iota(jnp.int32, square, 1)
    receivers, row, column = [], [], []
    for s in range(4):
        wide = jnp.broadcast_to(index_ref[s : s + 1, :].astype(F32), square)
        receivers.append(jnp.sum(jnp.where(same, wide, 0.0), axis=1, keepdims=True))
        row.append(jnp.full((REC, 1), source_row[s], jnp.int32).astype(F32))
        column.append(jnp.full((REC, 1), source_column[s], jnp.int32).astype(F32))
    receiver = jnp.concatenate(receivers, axis=0)
    row = jnp.concatenate(row, axis=0)
    column = jnp.concatenate(column, axis=0)
    line = lax.broadcasted_iota(jnp.int32, (PAIRS, GH), 1).astype(F32)
    chosen = jnp.where(line == receiver, 1.0, 0.0).astype(BF16)
    at_rows = dot(chosen, rows_ref[...], ((1,), (1,)))
    gap = line - row
    high, low = split(jnp.exp(gap * gap * (-1.0 / 32.0)))
    row_side = dot(high, rows_ref[...], ((1,), (1,))) + dot(low, rows_ref[...], ((1,), (1,)))
    gap = lax.broadcasted_iota(jnp.int32, (PAIRS, GW), 1).astype(F32) - column
    bump = jnp.exp(gap * gap * (-1.0 / 32.0))
    high, low = split(bump)
    column_side = dot(high, cols_ref[0], ((1,), (1,))) + dot(low, cols_ref[0], ((1,), (1,)))
    gap = receiver - row
    bump_ref[...] = bump * jnp.exp(gap * gap * (-1.0 / 32.0))
    lane = lax.broadcasted_iota(jnp.int32, (PAIRS, 128), 1)
    first = at_rows * row_side
    second = at_rows * pltpu.roll(row_side, 64, 1)
    both = jnp.where(
        lane < 64, first + pltpu.roll(first, 64, 1), second - pltpu.roll(second, 64, 1)
    )
    turned = times_i(both)
    for k in range(KOWN):
        side_ref[k, :, 0:128] = at_rows.astype(BF16)
        side_ref[k, :, 128:256] = (
            both * column_side[:, 2 * k : 2 * k + 1] + turned * column_side[:, 2 * k + 1 : 2 * k + 2]
        ).astype(BF16)


def mix_body(own, v_ref, ones_ref, t_ref, l_ref, out_ref):
    spectrum = ones_ref[0]
    for q in range(SPACE):
        spectrum = spectrum + v_ref[q]
    for k in range(KOWN):
        first = jnp.zeros((KX, 128), F32)
        second = jnp.zeros((KX, 128), F32)
        for ab in range(17):
            lane = (ab // 4) * 32 + (ab % 4) * 6 + 2 * k if ab < 16 else 24 + 2 * k
            plane = t_ref[pl.ds((k * 24 + ab) * KX, KX), :]
            first = first + spectrum[:, lane : lane + 1] * plane
            second = second + spectrum[:, lane + 1 : lane + 2] * plane
        modes = first + times_i(second)
        source = t_ref[pl.ds((k * 24 + 17) * KX, KX), :]
        none = jnp.zeros((16, 128), F32)
        rhs = jnp.concatenate(
            [modes, none, times_i(modes), none, source, none, times_i(source), none], axis=0
        )
        values = dot(l_ref[k], rhs.astype(BF16)).astype(BF16)
        for z in range(SPACE // 2):
            out_ref[z, :, 128 * k : 128 * k + 128] = values


def gain_row():
    return 0.5 + lax.broadcasted_iota(jnp.int32, (1, GW), 1).astype(F32) * (1.0 / GW)


def forward_body(
    own, list_ref, d_ref, other_ref, planes_ref, table_ref, wk_ref, col_ref, vec_ref, obs_ref,
    pred_ref, slope_ref, stats_ref, dd, acc, slopes, sems,
):
    p = own[0]
    count = list_ref[COUNT]
    gain = gain_row()
    for m in range(3):
        for z in range(SPACE // 2):
            for source, core in ((d_ref, p % 2), (other_ref, 1 - p % 2)):
                start = pl.multiple_of(PAIRS * (SPACE * m + 2 * z + core), PAIRS)
                dd[pl.ds(start, PAIRS), :] = source[z, :, 128 * m : 128 * m + 128].astype(F32)
    acc[...] = jnp.zeros_like(acc)
    root = math.sqrt(2.0 / math.pi)

    def preactivation(n):
        r = list_ref[n]
        pieces = []
        for m in range(3):
            block = dd[pl.ds(SPACE * PAIRS * m + r, SPACE, stride=PAIRS), :]
            pieces.append(block[:, :64])
            pieces.append(pltpu.roll(block, 64, 1)[:, :64])
        lhs = jnp.concatenate(pieces, axis=0).astype(BF16)
        lhs = jnp.concatenate([lhs, wk_ref[...]], axis=0)
        high, low = split(planes_ref[list_ref[FIRST + n]])
        rhs = jnp.concatenate([table_ref[...], high, low, high], axis=0)
        return r, dot(lhs, rhs, ((0,), (0,)))

    def outgoing(t):
        rows = pl.ds(pl.multiple_of(2 * C * t, 2 * C), 2 * C)
        return pltpu.make_async_copy(slopes.at[rows], slope_ref.at[rows], sems.at[t])

    def step(t, carry):
        second = jnp.minimum(2 * t + 1, count - 1)
        both = [preactivation(2 * t), preactivation(second)]
        weights = [1.0, jnp.where(2 * t + 1 < count, 1.0, 0.0)]
        for e, (r, x) in enumerate(both):
            amp, const, weight = vec_ref[0], vec_ref[1], vec_ref[2]
            col = col_ref[pl.ds(r, 1), :]
            total = []
            for m in range(4):
                lanes = slice(128 * m, 128 * m + 128)
                xm = x[:, lanes] + const + amp * col[:, lanes]
                square = xm * xm
                u = jnp.tanh(root * (xm + 0.044715 * (square * xm)))
                cdf = 0.5 * (1.0 + u)
                slope = cdf + xm * (
                    (0.5 * root) * (1.0 - u * u) * (1.0 + 3.0 * 0.044715 * square)
                )
                slopes[pl.ds(pl.multiple_of(C * (2 * t + e), C), C), lanes] = (
                    slope * weight
                ).astype(BF16)
                total.append(jnp.sum(weight * (xm * cdf), axis=0, keepdims=True))
            predicted = jnp.concatenate(total, axis=1)
            pred_ref[pl.ds(r, 1), :] = predicted
            weighted = predicted * gain * weights[e]
            target = obs_ref[pl.ds(r, 1), :] * gain
            s = r >> 4
            acc[pl.ds(s, 1), :] += weighted * weighted
            acc[pl.ds(s + 4, 1), :] += weighted * target
        outgoing(t).start()
        return carry

    def finish(t, carry):
        outgoing(t).wait()
        return carry

    lax.fori_loop(0, (count + 1) >> 1, step, 0)
    stats = acc[:, :128] + acc[:, 128:256] + acc[:, 256:384] + acc[:, 384:]
    for q in range(SPACE):
        stats_ref[q] = stats
    lax.fori_loop(0, (count + 1) >> 1, finish, 0)


def backward_body(
    own, list_ref, shot, stats_ref, obs_ref, pred_ref, slope_ref, table_ref, place_ref,
    cols_ref, near_ref, next_ref, far_ref, last_ref, misfit_ref, coef, acc, planes, slopes, sems,
):
    pairs = list_ref[COUNT]

    def incoming(t):
        rows = pl.ds(pl.multiple_of(2 * C * t, 2 * C), 2 * C)
        return pltpu.make_async_copy(slope_ref.at[rows], slopes.at[rows], sems.at[t])

    def begin(t, carry):
        incoming(t).start()
        return carry

    lax.fori_loop(0, (pairs + 1) >> 1, begin, 0)
    count = float(REC * GW)
    stats = stats_ref[0]
    for q in range(1, SPACE):
        stats = stats + stats_ref[q]
    stats = jnp.sum(stats, axis=1, keepdims=True)
    gain = gain_row()
    for s in range(4):
        target = obs_ref[REC * s : REC * s + REC, :] * gain
        tt = jnp.sum(jnp.sum(target * target, axis=0, keepdims=True), axis=1, keepdims=True) / count
        ww = stats[s : s + 1] / count
        wt = stats[s + 4 : s + 5] / count
        sp2 = ww + EPSILON
        isp = 1.0 / jnp.sqrt(sp2)
        isq = 1.0 / jnp.sqrt(tt + EPSILON)
        kappa = ww / sp2 - wt * isp * isq
        coef[s : s + 1, :] = jnp.broadcast_to(isp, (1, GW))
        coef[s + 4 : s + 5, :] = jnp.broadcast_to(isq, (1, GW))
        coef[s + 8 : s + 9, :] = jnp.broadcast_to(kappa, (1, GW))
        coef[s + 12 : s + 13, :] = jnp.zeros((1, GW), F32)
    acc[...] = jnp.zeros_like(acc)
    planes[...] = jnp.zeros_like(planes)

    def inner_gradient(t, e, r, valid):
        s = r >> 4
        isp = coef[pl.ds(s, 1), :]
        isq = coef[pl.ds(s + 4, 1), :]
        kappa = coef[pl.ds(s + 8, 1), :]
        weighted = pred_ref[pl.ds(r, 1), :] * gain * isp
        target = obs_ref[pl.ds(r, 1), :] * gain * isq
        differ = (weighted - target) * valid
        coef[pl.ds(s + 12, 1), :] += differ * differ
        data = (GH * GW / count) * gain * isp * (differ - kappa * weighted * valid)
        slope = slopes[pl.ds(pl.multiple_of(C * (2 * t + e), C), C), :].astype(F32)
        return (slope * data).astype(BF16)

    def step(t, carry):
        second = jnp.minimum(2 * t + 1, pairs - 1)
        valid = jnp.where(2 * t + 1 < pairs, 1.0, 0.0)
        incoming(t).wait()
        one = inner_gradient(t, 0, list_ref[2 * t], 1.0)
        two = inner_gradient(t, 1, list_ref[second], valid)
        spectra = dot(table_ref[...], jnp.concatenate([one, two], axis=0), ((1,), (1,)))
        for e, (n, inner) in enumerate(((2 * t, one), (second, two))):
            row = list_ref[FIRST + n]
            half = slice(64 * e, 64 * e + 64)
            acc[pl.ds(pl.multiple_of(row * 48, 8), 48), half] += spectra[:, half]
            twice = jnp.concatenate([inner, inner], axis=0)
            planes[row >> 3] += dot(twice, place_ref[row & 7], ((0,), (0,)))
        return carry

    lax.fori_loop(0, (pairs + 1) >> 1, step, 0)
    lane = lax.broadcasted_iota(jnp.int32, (ROWS, 128), 1)
    for q in range(SPACE):
        for m in range(3):
            even = acc[pl.ds(16 * m + q, ROWS, stride=48), :]
            odd = acc[pl.ds(16 * m + 8 + q, ROWS, stride=48), :]
            joined = jnp.where(lane < 64, even + pltpu.roll(even, 64, 1), odd + pltpu.roll(odd, 64, 1))
            cols_ref[q, :, 128 * m : 128 * m + 128] = joined.astype(BF16)
    x = shot[0] % 4
    for by, grad_ref in enumerate((near_ref, next_ref, far_ref, last_ref)):
        column = (x + by) % 4
        for zy in range(8):
            for g in range(4):
                start = pl.multiple_of(64 * zy + 16 * column, 16)
                grad_ref[64 * zy + 16 * g : 64 * zy + 16 * g + 16, :] = planes[
                    g, pl.ds(start, 16), :
                ].astype(BF16)
    for s in range(4):
        row = coef[s + 12 : s + 13, :]
        misfit_ref[s : s + 1, :] = (
            row[:, :128] + row[:, 128:256] + row[:, 256:384] + row[:, 384:]
        )
    misfit_ref[4:8, :] = jnp.zeros((4, 128), F32)


def adjoint_body(a_ref, rows_ref, out_ref):
    values = jnp.concatenate([a_ref[q] for q in range(SPACE)], axis=0)
    y = dot(rows_ref[...], values)
    for k in range(KOWN):
        lanes = slice(128 * k, 128 * k + 128)
        out_ref[KX * k : KX * k + KX, :] = y[:KX, lanes] + minus_i(y[KX:, lanes])


MODES = KOWN * KX


def along_x_body(shot, a_ref, b_ref, c_ref, d_ref, near_ref, next_ref, far_ref, last_ref, tmp):
    tmp[...] = (a_ref[...].astype(F32) + b_ref[...].astype(F32)) + (
        c_ref[...].astype(F32) + d_ref[...].astype(F32)
    )
    y = shot[0] // 4 % 4
    for by, out_ref in enumerate((near_ref, next_ref, far_ref, last_ref)):
        for z in range(2):
            start = pl.multiple_of(64 * (4 * z + (y + by) % 4), 64)
            out_ref[64 * z : 64 * z + 64, :] = tmp[pl.ds(start, 64), :].astype(out_ref.dtype)


def along_y_body(a_ref, b_ref, c_ref, d_ref, modes_ref, out_ref, send_ref):
    modes = modes_ref[...]
    total = (a_ref[...] + b_ref[...].astype(F32)) + (
        c_ref[...].astype(F32) + d_ref[...].astype(F32)
    )
    out_ref[0:MODES, :] = modes
    out_ref[MODES:, :] = total
    send_ref[0:MODES, :] = modes.astype(BF16)
    send_ref[MODES:, :] = total.astype(BF16)


def keep_and_send(modes, squares, out_ref, send_ref):
    out_ref[0:MODES, :] = modes
    out_ref[MODES : MODES + 16, :] = jnp.broadcast_to(squares, (16, 128))
    send_ref[0:MODES, :] = modes.astype(BF16)
    high = squares.astype(BF16).astype(F32)
    rest = squares - high
    middle = rest.astype(BF16).astype(F32)
    row = lax.broadcasted_iota(jnp.int32, (16, 128), 0)
    terms = jnp.where(row == 0, high, jnp.where(row == 1, middle, rest - middle))
    send_ref[MODES : MODES + 16, :] = jnp.where(row < 3, terms, 0.0).astype(BF16)


def sum_of(own_ref, parts):
    modes = own_ref[0:MODES, :]
    squares = own_ref[MODES : MODES + 1, :]
    for part in parts:
        modes = modes + part[0:MODES, :].astype(F32)
        terms = part[MODES : MODES + 16, :].astype(F32)
        squares = squares + jnp.sum(terms, axis=0, keepdims=True)
    return modes, squares


def along_z_body(shot, a_ref, b_ref, local_ref, out_ref, send_ref, tmp):
    total = a_ref[...] + b_ref[...].astype(F32)
    planes = total[MODES:]
    tmp[...] = planes
    local_ref[...] = tmp[pl.ds(pl.multiple_of(64 * (shot[0] // 16), 64), 64), :]
    squares = jnp.sum(planes * planes, axis=0, keepdims=True)
    keep_and_send(total[0:MODES], squares, out_ref, send_ref)


def join_body(a_ref, b_ref, c_ref, d_ref, out_ref, send_ref):
    modes, squares = sum_of(a_ref, (b_ref, c_ref, d_ref))
    keep_and_send(modes, squares, out_ref, send_ref)


def arrange_body(in_ref, repeat_ref, pick_ref, out_ref):
    row = lax.broadcasted_iota(jnp.int32, (64, 128), 0)
    lane = lax.broadcasted_iota(jnp.int32, (64, 128), 1)
    same = row % 4 == lane % 4
    total = jnp.zeros((64, 128), F32)
    for g in range(4):
        rest = in_ref[16 * g : 16 * g + 16, :]
        for _ in range(3):
            part = rest.astype(BF16)
            rest = rest - part.astype(F32)
            wide = jnp.where(same, dot(repeat_ref[...], part), 0.0).astype(BF16)
            total = total + dot(wide, pick_ref[g])
    out_ref[...] = total


def adjoint_mix_body(
    near_ref, next_ref, far_ref, last_ref, t_ref, high_ref, low_ref, extra_ref, out_ref
):
    lane = lax.broadcasted_iota(jnp.int32, (KX, 128), 1)
    spectra, squares = sum_of(near_ref, (next_ref, far_ref, last_ref))
    total = jnp.zeros((KX, 128), F32)
    cross = jnp.zeros((KX, 128), F32)
    for k in range(KOWN):
        spectrum = spectra[KX * k : KX * k + KX]
        turned = minus_i(spectrum)
        for ab in range(16):
            base = (ab // 4) * 32 + (ab % 4) * 6 + 2 * k
            plane = t_ref[pl.ds((k * 24 + ab) * KX, KX), :]
            re = jnp.sum(spectrum * plane, axis=1, keepdims=True)
            im = jnp.sum(turned * plane, axis=1, keepdims=True)
            total = jnp.where(lane == base, re, total)
            total = jnp.where(lane == base + 1, im, total)
        sh, sl = split(spectrum)
        cross = cross + dot(sh, high_ref[k]) + dot(sl, high_ref[k]) + dot(sh, low_ref[k])
    total = total * (1.0 / VELOCITY_SCALE)
    product = jnp.sum(total * cross, axis=0, keepdims=True)
    for z in range(SPACE // 2):
        out_ref[z, :KX, :] = total
        out_ref[z, KX : KX + 1, :] = product
        out_ref[z, KX + 1 : KX + 5, :] = extra_ref[0:4, :]
        out_ref[z, KX + 5 : KX + 6, :] = squares
        out_ref[z, KX + 6 : KX + 8, :] = jnp.zeros((2, 128), F32)


def output_body(
    own, m_ref, other_ref, back_ref, block_ref, local_ref, diag_rows_ref, off_rows_ref, diag_ref, off_ref,
    out_ref, misfit_ref, tmp,
):
    lane = lax.broadcasted_iota(jnp.int32, (KX, 128), 1)
    upper, lower = [], []
    tail = jnp.zeros((8, 128), F32)
    even = own[0] % 2 == 0
    for q in range(SPACE):
        mine, theirs = m_ref[q // 2], other_ref[q // 2]
        whole = jnp.where(even, mine, theirs) if q % 2 == 0 else jnp.where(even, theirs, mine)
        x = whole[:KX]
        tail = tail + whole[KX:]
        turned = jnp.where(lane % 2 == 0, -pltpu.roll(x, 127, 1), pltpu.roll(x, 1, 1))
        upper.append(x)
        lower.append(turned)
    n = jnp.concatenate(
        [jnp.concatenate(upper, axis=1), jnp.concatenate(lower, axis=1)], axis=0
    )
    high, low = split(n)
    nearly = dot(off_rows_ref[...], high)
    diag = jnp.concatenate([diag_rows_ref[...]] * 8, axis=1)
    left = n * diag + nearly
    right = n * diag_ref[...] + dot(high, off_ref[...])
    square = jnp.sum(jnp.sum(left * right, axis=0, keepdims=True), axis=1, keepdims=True)
    sums = jnp.sum(tail, axis=1, keepdims=True)
    total = square + 2.0 * sums[0:1] + sums[5:6]
    scale = 1.0 / jnp.sqrt(total / float(16 * GH * GW) + EPSILON)
    rows = dot(back_ref[0], high) + dot(back_ref[0], low)
    group = lax.broadcasted_iota(jnp.int32, (ROWS, 1024), 1) % 128 // 32
    rows = jnp.concatenate([jnp.where(group == a, rows, 0.0) for a in range(4)], axis=0)
    rh, rl = split(rows)
    block = dot(rh, block_ref[...]) + dot(rl, block_ref[...])
    for a in range(4):
        tmp[pl.ds(a, ROWS, stride=4), 0:64] = block[ROWS * a : ROWS * a + ROWS]
    out_ref[...] = (tmp[...].T[0:64] + local_ref[...]) * scale
    place = lax.broadcasted_iota(jnp.int32, (1, 4), 1)
    misfit = jnp.zeros((1, 4), F32)
    for s in range(4):
        misfit = jnp.where(place == s, sums[s + 1 : s + 2] * (0.5 / float(REC * GW)), misfit)
    misfit_ref[...] = misfit


def turn(size, stride, count, by):
    pairs = []
    for i in range(count):
        digit = (i // stride) % size
        pairs.append((i, i + ((digit + by) % size - digit) * stride))
    return pairs


def from_x(*parts):
    return [
        lax.ppermute(part, "shot", turn(4, 1, SHOT, by + 1)) for by, part in enumerate(parts)
    ]


def from_y(*parts):
    return [
        lax.ppermute(part, "shot", turn(4, 4, SHOT, by + 1)) for by, part in enumerate(parts)
    ]


def gather_z(copies):
    return lax.all_to_all(
        copies, "space", 0, 0, axis_index_groups=[[0, 2, 4, 6], [1, 3, 5, 7]], tiled=True
    )


def from_core(values):
    return lax.ppermute(values, "space", [(n, n ^ 1) for n in range(SPACE)])


def shards(
    velocity,
    encoder_weight,
    encoder_bias,
    source_amplitude,
    source_row,
    source_column,
    receiver_rows,
    point_weight,
    spectral_weight,
    layer_bias,
    out_weight,
    observed,
):
    p = lax.axis_index("space").astype(jnp.int32)
    i = lax.axis_index("shot").astype(jnp.int32)
    own, shot = p[None], i[None]
    fine = (128, 4 * GW)
    operator_rows = KOWN * KX * 24
    encoder = encoder_weight.reshape(16, C)
    bias, amplitude = encoder_bias[None], source_amplitude[None]
    both_rows = jnp.asarray(BOTH_ROWS)
    table = jnp.asarray(WEIGHTED)
    record = observed.reshape(PAIRS, GW)
    row_spec = full_spec((1, C))

    partial = call(
        velocity_body, 1, shaped((SPACE, KX, 128)),
        [full_spec(fine), full_spec((4 * GW, 256)), own_spec((192, 256))],
        kept_spec((SPACE, KX, 128)), name="velocity_spectrum",
    )(own, velocity, jnp.asarray(COLUMNS), jnp.asarray(ROW_SUMS))
    spectra = lax.all_to_all(partial, "space", 0, 0, tiled=True)

    bias, _ = lax.optimization_barrier((bias, partial))
    operator, sides, bumps = call(
        operator_body, 3,
        (shaped((operator_rows, 128)), shaped((KOWN, PAIRS, 256), BF16), shaped((PAIRS, GW))),
        [
            full_spec((16, C)), row_spec, row_spec, full_spec((KX, KOWN, C, 128)),
            full_spec((4, REC)), full_spec((128, GH)), own_spec((8, GW)),
        ],
        (full_spec((operator_rows, 128)), full_spec((KOWN, PAIRS, 256)), full_spec((PAIRS, GW))),
        name="operator",
    )(
        own, source_row, source_column, encoder, bias, amplitude, spectral_weight, receiver_rows,
        jnp.asarray(PAIRED_ROWS),
        jnp.asarray(OWN_COLUMNS),
    )

    sent = call(
        mix_body, 1, shaped((SPACE // 2, PAIRS, 384), BF16),
        [
            kept_spec((SPACE, KX, 128)), own_spec((KX, 128)),
            full_spec((operator_rows, 128)), full_spec((KOWN, PAIRS, 256)),
        ],
        kept_spec((SPACE // 2, PAIRS, 384)), name="mix_modes",
    )(own, spectra, jnp.asarray(ONES), operator, sides)
    gathered = gather_z(sent)

    late_bias, _ = lax.optimization_barrier((layer_bias[None], sent))
    planes, wk, vectors, placed, spread_high, spread_low, pairs = call(
        planes_body, 2,
        (
            shaped((ROWS, 16, GW)), shaped((48, C), BF16), shaped((3, C, 128)),
            shaped((8, 128, 128), BF16), shaped((KOWN, 128, 128), BF16),
            shaped((KOWN, 128, 128), BF16), shaped((144,), jnp.int32),
        ),
        [
            full_spec(fine), full_spec((512, 512)), full_spec((16, C)), row_spec, row_spec,
            full_spec((C, C)), row_spec, row_spec, full_spec((KOWN * 2, 128, 128)),
        ],
        (
            full_spec((ROWS, 16, GW)), full_spec((48, C)), full_spec((3, C, 128)),
            full_spec((8, 128, 128)), full_spec((KOWN, 128, 128)), full_spec((KOWN, 128, 128)),
            pl.BlockSpec(memory_space=pltpu.SMEM),
        ),
        [pltpu.VMEM((128, 512), F32)], name="velocity_planes",
    )(
        own, receiver_rows, velocity, jnp.asarray(SELECT), encoder, bias, amplitude, point_weight, late_bias,
        out_weight[None], jnp.asarray(LANES),
    )

    gathered, planes = lax.optimization_barrier((gathered, planes))
    others = from_core(gathered)
    predicted, slopes, stats = call(
        forward_body, 2,
        (shaped((PAIRS, GW)), shaped((PAIRS * C, GW), BF16), shaped((SPACE, 8, 128))),
        [
            kept_spec((SPACE // 2, PAIRS, 384)), kept_spec((SPACE // 2, PAIRS, 384)),
            full_spec((ROWS, 16, GW)), full_spec((48, GW)),
            full_spec((48, C)), full_spec((PAIRS, GW)), full_spec((3, C, 128)),
            full_spec((PAIRS, GW)),
        ],
        (
            full_spec((PAIRS, GW)), pl.BlockSpec(memory_space=pl.ANY),
            kept_spec((SPACE, 8, 128)),
        ),
        [
            pltpu.VMEM((3 * SPACE * PAIRS, 128), F32), pltpu.VMEM((8, GW), F32),
            pltpu.VMEM((PAIRS * C, GW), BF16), pltpu.SemaphoreType.DMA((PAIRS // 2,)),
        ], name="forward_rows",
    )(own, pairs, gathered, others, planes, table, wk, bumps, vectors, record)
    stats = lax.all_to_all(stats, "space", 0, 0, tiled=True)

    columns, near, after, far, last, misfits = call(
        backward_body, 3,
        (shaped((SPACE, ROWS, 384), BF16),) + (shaped((GW, 128), BF16),) * 4 + (shaped((8, 128)),),
        [
            kept_spec((SPACE, 8, 128)), full_spec((PAIRS, GW)),
            full_spec((PAIRS, GW)), pl.BlockSpec(memory_space=pl.ANY), full_spec((48, GW)),
            full_spec((8, 128, 128)),
        ],
        (kept_spec((SPACE, ROWS, 384)),) + (kept_spec((GW, 128)),) * 4 + (full_spec((8, 128)),),
        [
            pltpu.VMEM((16, GW), F32), pltpu.VMEM((ROWS * 48, 128), F32),
            pltpu.VMEM((4, GW, 128), F32), pltpu.VMEM((PAIRS * C, GW), BF16),
            pltpu.SemaphoreType.DMA((PAIRS // 2,)),
        ],
        name="backward_rows",
    )(own, pairs, shot, stats, record, predicted, slopes, table, placed)

    columns = lax.all_to_all(columns, "space", 0, 0, tiled=True)
    adjoint = call(
        adjoint_body, 0, shaped((KOWN * KX, 128)),
        [kept_spec((SPACE, ROWS, 384)), full_spec((96, GH))],
        kept_spec((KOWN * KX, 128)), name="adjoint_rows", limit=SMALL,
    )(columns, both_rows)
    arrived = from_x(after, far, last)
    shares = call(
        along_x_body, 1, (shaped((128, 128)),) + (shaped((128, 128), BF16),) * 3,
        [kept_spec((GW, 128))] * 4, (kept_spec((128, 128)),) * 4, [pltpu.VMEM((GW, 128), F32)],
        name="along_x", limit=SMALL,
    )(shot, near, *arrived)
    sums, sent = call(
        along_y_body, 0, (shaped((MODES + 128, 128)), shaped((MODES + 128, 128), BF16)),
        [kept_spec((128, 128))] * 4 + [kept_spec((MODES, 128))],
        (kept_spec((MODES + 128, 128)),) * 2, name="along_y", limit=SMALL,
    )(shares[0], *from_y(*shares[1:]), adjoint)
    carried = (shaped((MODES + 16, 128)), shaped((MODES + 16, 128), BF16))
    carried_specs = (kept_spec((MODES + 16, 128)),) * 2
    local, sums, sent = call(
        along_z_body, 1, (shaped((64, 128)),) + carried,
        [kept_spec((MODES + 128, 128))] * 2, (kept_spec((64, 128)),) + carried_specs,
        [pltpu.VMEM((128, 128), F32)], name="along_z", limit=SMALL,
    )(shot, sums, lax.ppermute(sent, "shot", turn(2, 16, SHOT, 1)))
    parts = from_x(sent, sent, sent)
    local = call(
        arrange_body, 0, shaped((64, 128)),
        [kept_spec((64, 128)), kept_spec((64, 16)), kept_spec((4, 128, 128))],
        kept_spec((64, 128)), name="arrange", limit=SMALL,
    )(local, jnp.asarray(REPEAT), jnp.asarray(PICK))
    mine = lax.dynamic_index_in_dim(jnp.asarray(BLOCKS), i, 0, keepdims=False)
    parts, local, mine = lax.optimization_barrier((parts, local, mine))
    sums, sent = call(
        join_body, 0, carried, [kept_spec((MODES + 16, 128))] * 4, carried_specs, name="join",
        limit=SMALL,
    )(sums, *parts)

    modes = call(
        adjoint_mix_body, 0, shaped((SPACE // 2, KX + 8, 128)),
        [kept_spec((MODES + 16, 128))] * 4
        + [
            full_spec((operator_rows, 128)), full_spec((KOWN, 128, 128)),
            full_spec((KOWN, 128, 128)), full_spec((8, 128)),
        ],
        kept_spec((SPACE // 2, KX + 8, 128)), name="adjoint_mix", limit=SMALL,
    )(sums, *from_y(sent, sent, sent), operator, spread_high, spread_low, misfits)
    modes = gather_z(modes)
    other_modes = from_core(modes)
    block, misfit = call(
        output_body, 1, (shaped((64, 128)), shaped((1, 4))),
        [
            kept_spec((SPACE // 2, KX + 8, 128)), kept_spec((SPACE // 2, KX + 8, 128)),
            own_spec((ROWS, 96)), full_spec((1024, 64)),
            full_spec((64, 128)), full_spec((96, 128)), full_spec((96, 96)),
            full_spec((1, 1024)), full_spec((1024, 1024)),
        ],
        (full_spec((64, 128)), full_spec((1, 4))), [pltpu.VMEM((128, 128), F32)],
        name="output_block", limit=SMALL,
    )(
        own, modes, other_modes, jnp.asarray(ROWS_BACK), mine, local, jnp.asarray(DIAG_ROWS),
        jnp.asarray(OFF_ROWS), jnp.asarray(DIAG_WIDE), jnp.asarray(OFF_WIDE),
    )
    return (misfit.reshape(4), block.T)


def solution(mesh):
    in_specs = (
        P("space", None),
        P(),
        P(),
        P(),
        P("shot"),
        P("shot"),
        P("shot", None),
        P(),
        P(None, "space", None, None),
        P(),
        P(),
        P("shot", None, None),
    )
    out_specs = (P("shot"), P("space", "shot"))
    return jax.shard_map(shards, mesh=mesh, in_specs=in_specs, out_specs=out_specs, check_vma=False)
```

```python
import math

import jax
import jax.numpy as jnp
import ml_dtypes
import numpy as np
from jax import lax
from jax.experimental import pallas as pl
from jax.experimental.pallas import tpu as pltpu
from jax.sharding import PartitionSpec as P

C = 64
KX = 48
KY = 24
GH = 256
GW = 512
REC = 16
SPACE = 8
SHOT = 32
ROWS = GH // SPACE
KOWN = KY // SPACE
COUNT = 64
FIRST = 72
PAIRS = 64
EPSILON = 1e-06
VELOCITY_MEAN = 3.0
VELOCITY_SCALE = 1.5
HIGHEST = lax.Precision.HIGHEST
F32 = jnp.float32
BF16 = jnp.bfloat16
SMALL = 28 << 20
LARGE = 56 << 20


def bf(values):
    return np.asarray(values, np.float32).astype(ml_dtypes.bfloat16)


def as64(values):
    return values.astype(np.float64)


def make_tables():
    k = np.arange(KY)
    w = np.arange(GW)
    phase = (k[:, None] * w[None, :] % GW) * (2.0 * math.pi / GW)
    plain = bf(np.stack([np.cos(phase), -np.sin(phase)], 1) / math.sqrt(GW))
    f = np.where(np.arange(KX) < KX // 2, np.arange(KX), np.arange(KX) - KX)
    phase = (f[:, None] * np.arange(GH)[None, :] % GH) * (2.0 * math.pi / GH)
    cos_rows = bf(np.cos(phase) / math.sqrt(GH))
    sin_rows = bf(np.sin(phase) / math.sqrt(GH))
    return plain, cos_rows, sin_rows


PLAIN, COS_ROWS, SIN_ROWS = make_tables()
MODE_WEIGHT = np.where(np.arange(KY) == 0, 1.0, 2.0)


def columns_table():
    table = np.zeros((GW, 4, SPACE, 32), np.float32)
    plain = PLAIN.astype(np.float32).reshape(SPACE, 6, GW)
    for b in range(4):
        table[:, b, :, 6 * b : 6 * b + 6] = plain.transpose(2, 0, 1)
    return bf(table.reshape(4 * GW, 256))


def rows_table():
    table = np.zeros((SPACE, 4, KX, 2, ROWS, 4), np.float32)
    for p in range(SPACE):
        for a in range(4):
            table[p, a, :, 0, :, a] = COS_ROWS[:, ROWS * p : ROWS * p + ROWS]
            table[p, a, :, 1, :, a] = SIN_ROWS[:, ROWS * p : ROWS * p + ROWS]
    return bf(table.reshape(SPACE, 4 * KX, 256))


def ones_table():
    wsum = as64(PLAIN).sum(-1)
    c, s = as64(COS_ROWS).sum(-1), as64(SIN_ROWS).sum(-1)
    table = np.zeros((SPACE, KX, 128), np.float32)
    for q in range(SPACE):
        for k in range(KOWN):
            re, im = wsum[3 * q + k]
            table[q, :, 24 + 2 * k] = c * re + s * im
            table[q, :, 25 + 2 * k] = c * im - s * re
    return table


def select_table():
    table = np.zeros((128, 4, 4, 128), np.float32)
    for b in range(4):
        table[np.arange(128), b, b, np.arange(128)] = 1.0
    return bf(table.reshape(512, 512))


def weighted_table():
    plain = PLAIN.astype(np.float32) * MODE_WEIGHT[:, None, None]
    return bf(plain.reshape(SPACE, KOWN, 2, GW).transpose(1, 2, 0, 3).reshape(48, GW))


def gram_tables():
    full = np.concatenate([as64(COS_ROWS), as64(SIN_ROWS)], 0)
    gram_rows = full @ full.T
    e = as64(PLAIN).reshape(48, GW)
    gram = e @ e.T
    wide = np.zeros((SPACE, 4, 32, SPACE, 4, 32))
    gram = gram.reshape(SPACE, 6, SPACE, 6)
    for a in range(4):
        for b in range(4):
            wide[:, a, b * 6 : b * 6 + 6, :, a, b * 6 : b * 6 + 6] = gram
    wide = wide.reshape(1024, 1024)
    diag_rows = np.broadcast_to(np.diag(gram_rows)[:, None], (96, 128))
    off_rows = bf(gram_rows - np.diag(np.diag(gram_rows)))
    diag_wide = np.diag(wide)[None, :]
    off_wide = bf(wide - np.diag(np.diag(wide)))
    return (
        np.asarray(diag_rows, np.float32),
        off_rows,
        np.asarray(diag_wide, np.float32),
        off_wide,
    )


COLUMNS = columns_table()
ROW_SUMS = rows_table()
ONES = ones_table()
SELECT = select_table()
WEIGHTED = weighted_table()
DIAG_ROWS, OFF_ROWS, DIAG_WIDE, OFF_WIDE = gram_tables()
PAIRED_ROWS = np.zeros((2, 64, GH), np.float32)
PAIRED_ROWS[0, :KX], PAIRED_ROWS[1, :KX] = COS_ROWS, SIN_ROWS
PAIRED_ROWS = bf(PAIRED_ROWS.reshape(128, GH))
OWN_COLUMNS = np.zeros((SPACE, 8, GW), np.float32)
OWN_COLUMNS[:, :6] = PLAIN.reshape(SPACE, 6, GW)
OWN_COLUMNS = bf(OWN_COLUMNS)


def lanes_table():
    table = np.zeros((KOWN, 2, 128, 128), np.float32)
    for k in range(KOWN):
        for part in range(2):
            for ab in range(16):
                table[k, part, ab, 32 * (ab // 4) + 6 * (ab % 4) + 2 * k + part] = 1.0
    return bf(table.reshape(KOWN * 2, 128, 128))


def block_table():
    table = np.zeros((SHOT, SPACE, 4, 32, 16, 4), np.float32)
    plain = PLAIN.astype(np.float32).reshape(SPACE, 6, SHOT, 16)
    for b in range(4):
        table[:, :, :, 6 * b : 6 * b + 6, :, b] = plain.transpose(2, 0, 1, 3)[:, :, None]
    return bf(table.reshape(SHOT, 1024, 64))


REPEAT = np.zeros((64, 16), np.float32)
REPEAT[np.arange(64), np.arange(64) // 4] = 1.0
REPEAT = bf(REPEAT)
PICK = np.zeros((4, 128, 128), np.float32)
for g in range(4):
    PICK[g, np.arange(128), 32 * g + np.arange(128) // 4] = 1.0
PICK = bf(PICK)
LANES = lanes_table()
BLOCKS = block_table()
BOTH_ROWS = bf(np.concatenate([COS_ROWS.astype(np.float32), SIN_ROWS.astype(np.float32)], 0))
ROWS_BACK = bf(
    BOTH_ROWS.astype(np.float32).T.reshape(SPACE, ROWS, 96)
)


def split(values):
    high = values.astype(BF16)
    return high, (values - high.astype(F32)).astype(BF16)


def dot(a, b, dims=((1,), (0,))):
    return lax.dot_general(a, b, (dims, ((), ())), preferred_element_type=F32)


def dot_split(a, b):
    high, low = split(b)
    return dot(a, high) + dot(a, low)


def minus_i(x):
    lane = lax.broadcasted_iota(jnp.int32, x.shape, 1)
    swapped = pltpu.roll(x, 64, 1)
    return jnp.where(lane < 64, swapped, -swapped)


def times_i(x):
    lane = lax.broadcasted_iota(jnp.int32, x.shape, 1)
    swapped = pltpu.roll(x, 64, 1)
    return jnp.where(lane < 64, -swapped, swapped)


def full_spec(shape):
    return pl.BlockSpec(shape, lambda *_: (0,) * len(shape))


def own_spec(shape, place=0):
    return pl.BlockSpec((1,) + shape, lambda i, *own: (own[place][0],) + (0,) * len(shape))


def kept_spec(shape):
    return pl.BlockSpec(memory_space=pltpu.VMEM)


def call(body, prefetch, out_shape, in_specs, out_specs, scratch=(), name=None, limit=LARGE):
    return pl.pallas_call(
        body,
        out_shape=out_shape,
        grid_spec=pltpu.PrefetchScalarGridSpec(
            num_scalar_prefetch=prefetch,
            grid=(1,),
            in_specs=in_specs,
            out_specs=out_specs,
            scratch_shapes=list(scratch),
        ),
        compiler_params=pltpu.CompilerParams(vmem_limit_bytes=limit),
        name=name,
    )


def shaped(shape, dtype=F32):
    return jax.ShapeDtypeStruct(shape, dtype)


def velocity_body(own, v_ref, cols_ref, rows_ref, out_ref):
    vn = (v_ref[...] - VELOCITY_MEAN) / VELOCITY_SCALE
    high, low = split(vn)
    xx = dot(high, cols_ref[...]) + dot(low, cols_ref[...])
    even = lax.broadcasted_iota(jnp.int32, xx.shape, 1) % 2 == 0
    turned = jnp.where(even, pltpu.roll(xx, 255, 1), -pltpu.roll(xx, 1, 1))
    stacked = jnp.concatenate([xx, turned], axis=0)
    yy = dot_split(rows_ref[0], stacked)
    group = lax.broadcasted_iota(jnp.int32, (KX, 128), 1) // 32
    for q in range(SPACE):
        total = jnp.zeros((KX, 128), F32)
        for a in range(4):
            piece = yy[KX * a : KX * a + KX, 128 * (q // 4) : 128 * (q // 4) + 128]
            shift = (32 * a - 32 * (q % 4)) % 128
            if shift:
                piece = pltpu.roll(piece, shift, 1)
            total = jnp.where(group == a, piece, total)
        out_ref[q] = total


def column_of(row):
    return jnp.broadcast_to(row, (128, C)).T


def planes_body(
    own, rows_ref, v_ref, sel_ref, enc_ref, bias_ref, amp_ref, point_ref, layer_ref, weight_ref, lanes_ref,
    out_ref, wk_ref, vec_ref, place_ref, high_ref, low_ref, list_ref, tmp,
):
    def find(r, count):
        row = rows_ref[r >> 4, r & 15] - own[0] * ROWS
        list_ref[count] = r
        list_ref[FIRST + count] = row
        return count + jnp.where((row >= 0) & (row < ROWS), 1, 0)

    list_ref[COUNT] = lax.fori_loop(0, PAIRS, find, 0)
    for m in range(4):
        vn = (v_ref[:, 512 * m : 512 * m + 512] - VELOCITY_MEAN) / VELOCITY_SCALE
        high, low = split(vn)
        tmp[...] = dot(high, sel_ref[...]) + dot(low, sel_ref[...])
        for h in range(ROWS):
            for b in range(4):
                out_ref[h, 4 * b : 4 * b + 4, 128 * m : 128 * m + 128] = tmp[
                    4 * h : 4 * h + 4, 128 * b : 128 * b + 128
                ]
    stack = jnp.concatenate(
        [enc_ref[...], bias_ref[...], amp_ref[...], jnp.zeros((6, C), F32)], axis=0
    )
    high, low = split(stack)
    pointed = dot(high, point_ref[...]) + dot(low, point_ref[...])
    swapped = jnp.concatenate(
        [pointed[4 * a + b : 4 * a + b + 1] for b in range(4) for a in range(4)], axis=0
    )
    high, low = split(swapped)
    wk_ref[0:16] = high
    wk_ref[16:32] = high
    wk_ref[32:48] = low
    vec_ref[0] = column_of(pointed[17:18])
    vec_ref[1] = column_of(pointed[16:17] + layer_ref[...])
    vec_ref[2] = column_of(weight_ref[...])
    turned = jnp.concatenate([pointed[:16], jnp.zeros((112, C), F32)], axis=0).T
    scaled = turned * (1.0 / VELOCITY_SCALE)
    for e in range(8):
        high, low = split(pltpu.roll(scaled, 16 * e, 1) if e else scaled)
        place_ref[e, 0:C] = high
        place_ref[e, C : 2 * C] = low
    th, tl = split(scaled)
    for k in range(KOWN):
        reach = jnp.where((own[0] == 0) & (k == 0), 1.0, 0.5)
        for part in range(2):
            wide = (dot(th, lanes_ref[2 * k + part]) + dot(tl, lanes_ref[2 * k + part])) * reach
            high, low = split(wide)
            high_ref[k, C * part : C * part + C] = high
            low_ref[k, C * part : C * part + C] = low


def operator_body(
    own, source_row, source_column, enc_ref, bias_ref, amp_ref, w_ref, index_ref, rows_ref,
    cols_ref, out_ref, side_ref, bump_ref,
):
    stack = jnp.concatenate(
        [enc_ref[...], bias_ref[...], amp_ref[...], jnp.zeros((6, C), F32)], axis=0
    )
    high, low = split(stack)
    lhs = jnp.concatenate([high.astype(F32), low.astype(F32)], axis=0).astype(BF16)

    def step(j, carry):
        for k in range(KOWN):
            both = dot(lhs, w_ref[j, k])
            out_ref[pl.ds(k * KX * 24 + j, 24, stride=KX), :] = both[:24] + both[24:]
        return carry

    lax.fori_loop(0, KX, step, 0, unroll=8)
    square = (REC, REC)
    same = lax.broadcasted_iota(jnp.int32, square, 0) == lax.broadcasted_iota(jnp.int32, square, 1)
    receivers, row, column = [], [], []
    for s in range(4):
        wide = jnp.broadcast_to(index_ref[s : s + 1, :].astype(F32), square)
        receivers.append(jnp.sum(jnp.where(same, wide, 0.0), axis=1, keepdims=True))
        row.append(jnp.full((REC, 1), source_row[s], jnp.int32).astype(F32))
        column.append(jnp.full((REC, 1), source_column[s], jnp.int32).astype(F32))
    receiver = jnp.concatenate(receivers, axis=0)
    row = jnp.concatenate(row, axis=0)
    column = jnp.concatenate(column, axis=0)
    line = lax.broadcasted_iota(jnp.int32, (PAIRS, GH), 1).astype(F32)
    chosen = jnp.where(line == receiver, 1.0, 0.0).astype(BF16)
    at_rows = dot(chosen, rows_ref[...], ((1,), (1,)))
    gap = line - row
    high, low = split(jnp.exp(gap * gap * (-1.0 / 32.0)))
    row_side = dot(high, rows_ref[...], ((1,), (1,))) + dot(low, rows_ref[...], ((1,), (1,)))
    gap = lax.broadcasted_iota(jnp.int32, (PAIRS, GW), 1).astype(F32) - column
    bump = jnp.exp(gap * gap * (-1.0 / 32.0))
    high, low = split(bump)
    column_side = dot(high, cols_ref[0], ((1,), (1,))) + dot(low, cols_ref[0], ((1,), (1,)))
    gap = receiver - row
    bump_ref[...] = bump * jnp.exp(gap * gap * (-1.0 / 32.0))
    lane = lax.broadcasted_iota(jnp.int32, (PAIRS, 128), 1)
    first = at_rows * row_side
    second = at_rows * pltpu.roll(row_side, 64, 1)
    both = jnp.where(
        lane < 64, first + pltpu.roll(first, 64, 1), second - pltpu.roll(second, 64, 1)
    )
    turned = times_i(both)
    for k in range(KOWN):
        side_ref[k, :, 0:128] = at_rows.astype(BF16)
        side_ref[k, :, 128:256] = (
            both * column_side[:, 2 * k : 2 * k + 1] + turned * column_side[:, 2 * k + 1 : 2 * k + 2]
        ).astype(BF16)


def mix_body(own, v_ref, ones_ref, t_ref, l_ref, out_ref):
    spectrum = ones_ref[0]
    for q in range(SPACE):
        spectrum = spectrum + v_ref[q]
    for k in range(KOWN):
        first = jnp.zeros((KX, 128), F32)
        second = jnp.zeros((KX, 128), F32)
        for ab in range(17):
            lane = (ab // 4) * 32 + (ab % 4) * 6 + 2 * k if ab < 16 else 24 + 2 * k
            plane = t_ref[pl.ds((k * 24 + ab) * KX, KX), :]
            first = first + spectrum[:, lane : lane + 1] * plane
            second = second + spectrum[:, lane + 1 : lane + 2] * plane
        modes = first + times_i(second)
        source = t_ref[pl.ds((k * 24 + 17) * KX, KX), :]
        none = jnp.zeros((16, 128), F32)
        rhs = jnp.concatenate(
            [modes, none, times_i(modes), none, source, none, times_i(source), none], axis=0
        )
        values = dot(l_ref[k], rhs.astype(BF16)).astype(BF16)
        for z in range(SPACE // 2):
            out_ref[z, :, 128 * k : 128 * k + 128] = values


def gain_row():
    return 0.5 + lax.broadcasted_iota(jnp.int32, (1, GW), 1).astype(F32) * (1.0 / GW)


def forward_body(
    own, list_ref, d_ref, other_ref, planes_ref, table_ref, wk_ref, col_ref, vec_ref, obs_ref,
    pred_ref, slope_ref, stats_ref, dd, acc, slopes, sems,
):
    p = own[0]
    count = list_ref[COUNT]
    gain = gain_row()
    for m in range(3):
        for z in range(SPACE // 2):
            for source, core in ((d_ref, p % 2), (other_ref, 1 - p % 2)):
                start = pl.multiple_of(PAIRS * (SPACE * m + 2 * z + core), PAIRS)
                dd[pl.ds(start, PAIRS), :] = source[z, :, 128 * m : 128 * m + 128].astype(F32)
    acc[...] = jnp.zeros_like(acc)
    root = math.sqrt(2.0 / math.pi)

    def preactivation(n):
        r = list_ref[n]
        pieces = []
        for m in range(3):
            block = dd[pl.ds(SPACE * PAIRS * m + r, SPACE, stride=PAIRS), :]
            pieces.append(block[:, :64])
            pieces.append(pltpu.roll(block, 64, 1)[:, :64])
        lhs = jnp.concatenate(pieces, axis=0).astype(BF16)
        lhs = jnp.concatenate([lhs, wk_ref[...]], axis=0)
        high, low = split(planes_ref[list_ref[FIRST + n]])
        rhs = jnp.concatenate([table_ref[...], high, low, high], axis=0)
        return r, dot(lhs, rhs, ((0,), (0,)))

    def outgoing(t):
        rows = pl.ds(pl.multiple_of(2 * C * t, 2 * C), 2 * C)
        return pltpu.make_async_copy(slopes.at[rows], slope_ref.at[rows], sems.at[t])

    def step(t, carry):
        second = jnp.minimum(2 * t + 1, count - 1)
        both = [preactivation(2 * t), preactivation(second)]
        weights = [1.0, jnp.where(2 * t + 1 < count, 1.0, 0.0)]
        for e, (r, x) in enumerate(both):
            amp, const, weight = vec_ref[0], vec_ref[1], vec_ref[2]
            col = col_ref[pl.ds(r, 1), :]
            total = []
            for m in range(4):
                lanes = slice(128 * m, 128 * m + 128)
                xm = x[:, lanes] + const + amp * col[:, lanes]
                square = xm * xm
                u = jnp.tanh(root * (xm + 0.044715 * (square * xm)))
                cdf = 0.5 * (1.0 + u)
                slope = cdf + xm * (
                    (0.5 * root) * (1.0 - u * u) * (1.0 + 3.0 * 0.044715 * square)
                )
                slopes[pl.ds(pl.multiple_of(C * (2 * t + e), C), C), lanes] = (
                    slope * weight
                ).astype(BF16)
                total.append(jnp.sum(weight * (xm * cdf), axis=0, keepdims=True))
            predicted = jnp.concatenate(total, axis=1)
            pred_ref[pl.ds(r, 1), :] = predicted
            weighted = predicted * gain * weights[e]
            target = obs_ref[pl.ds(r, 1), :] * gain
            s = r >> 4
            acc[pl.ds(s, 1), :] += weighted * weighted
            acc[pl.ds(s + 4, 1), :] += weighted * target
        outgoing(t).start()
        return carry

    def finish(t, carry):
        outgoing(t).wait()
        return carry

    lax.fori_loop(0, (count + 1) >> 1, step, 0)
    stats = acc[:, :128] + acc[:, 128:256] + acc[:, 256:384] + acc[:, 384:]
    for q in range(SPACE):
        stats_ref[q] = stats
    lax.fori_loop(0, (count + 1) >> 1, finish, 0)


def backward_body(
    own, list_ref, shot, stats_ref, obs_ref, pred_ref, slope_ref, table_ref, place_ref,
    cols_ref, near_ref, next_ref, far_ref, last_ref, misfit_ref, coef, acc, planes, slopes, sems,
):
    pairs = list_ref[COUNT]

    def incoming(t):
        rows = pl.ds(pl.multiple_of(2 * C * t, 2 * C), 2 * C)
        return pltpu.make_async_copy(slope_ref.at[rows], slopes.at[rows], sems.at[t])

    def begin(t, carry):
        incoming(t).start()
        return carry

    lax.fori_loop(0, (pairs + 1) >> 1, begin, 0)
    count = float(REC * GW)
    stats = stats_ref[0]
    for q in range(1, SPACE):
        stats = stats + stats_ref[q]
    stats = jnp.sum(stats, axis=1, keepdims=True)
    gain = gain_row()
    for s in range(4):
        target = obs_ref[REC * s : REC * s + REC, :] * gain
        tt = jnp.sum(jnp.sum(target * target, axis=0, keepdims=True), axis=1, keepdims=True) / count
        ww = stats[s : s + 1] / count
        wt = stats[s + 4 : s + 5] / count
        sp2 = ww + EPSILON
        isp = 1.0 / jnp.sqrt(sp2)
        isq = 1.0 / jnp.sqrt(tt + EPSILON)
        kappa = ww / sp2 - wt * isp * isq
        coef[s : s + 1, :] = jnp.broadcast_to(isp, (1, GW))
        coef[s + 4 : s + 5, :] = jnp.broadcast_to(isq, (1, GW))
        coef[s + 8 : s + 9, :] = jnp.broadcast_to(kappa, (1, GW))
        coef[s + 12 : s + 13, :] = jnp.zeros((1, GW), F32)
    acc[...] = jnp.zeros_like(acc)
    planes[...] = jnp.zeros_like(planes)

    def inner_gradient(t, e, r, valid):
        s = r >> 4
        isp = coef[pl.ds(s, 1), :]
        isq = coef[pl.ds(s + 4, 1), :]
        kappa = coef[pl.ds(s + 8, 1), :]
        weighted = pred_ref[pl.ds(r, 1), :] * gain * isp
        target = obs_ref[pl.ds(r, 1), :] * gain * isq
        differ = (weighted - target) * valid
        coef[pl.ds(s + 12, 1), :] += differ * differ
        data = (GH * GW / count) * gain * isp * (differ - kappa * weighted * valid)
        slope = slopes[pl.ds(pl.multiple_of(C * (2 * t + e), C), C), :].astype(F32)
        return (slope * data).astype(BF16)

    def step(t, carry):
        second = jnp.minimum(2 * t + 1, pairs - 1)
        valid = jnp.where(2 * t + 1 < pairs, 1.0, 0.0)
        incoming(t).wait()
        one = inner_gradient(t, 0, list_ref[2 * t], 1.0)
        two = inner_gradient(t, 1, list_ref[second], valid)
        spectra = dot(table_ref[...], jnp.concatenate([one, two], axis=0), ((1,), (1,)))
        for e, (n, inner) in enumerate(((2 * t, one), (second, two))):
            row = list_ref[FIRST + n]
            half = slice(64 * e, 64 * e + 64)
            acc[pl.ds(pl.multiple_of(row * 48, 8), 48), half] += spectra[:, half]
            twice = jnp.concatenate([inner, inner], axis=0)
            planes[row >> 3] += dot(twice, place_ref[row & 7], ((0,), (0,)))
        return carry

    lax.fori_loop(0, (pairs + 1) >> 1, step, 0)
    lane = lax.broadcasted_iota(jnp.int32, (ROWS, 128), 1)
    for q in range(SPACE):
        for m in range(3):
            even = acc[pl.ds(16 * m + q, ROWS, stride=48), :]
            odd = acc[pl.ds(16 * m + 8 + q, ROWS, stride=48), :]
            joined = jnp.where(lane < 64, even + pltpu.roll(even, 64, 1), odd + pltpu.roll(odd, 64, 1))
            cols_ref[q, :, 128 * m : 128 * m + 128] = joined.astype(BF16)
    x = shot[0] % 4
    for by, grad_ref in enumerate((near_ref, next_ref, far_ref, last_ref)):
        column = (x + by) % 4
        for zy in range(8):
            for g in range(4):
                start = pl.multiple_of(64 * zy + 16 * column, 16)
                grad_ref[64 * zy + 16 * g : 64 * zy + 16 * g + 16, :] = planes[
                    g, pl.ds(start, 16), :
                ].astype(BF16)
    for s in range(4):
        row = coef[s + 12 : s + 13, :]
        misfit_ref[s : s + 1, :] = (
            row[:, :128] + row[:, 128:256] + row[:, 256:384] + row[:, 384:]
        )
    misfit_ref[4:8, :] = jnp.zeros((4, 128), F32)


def adjoint_body(a_ref, rows_ref, out_ref):
    values = jnp.concatenate([a_ref[q] for q in range(SPACE)], axis=0)
    y = dot(rows_ref[...], values)
    for k in range(KOWN):
        lanes = slice(128 * k, 128 * k + 128)
        out_ref[KX * k : KX * k + KX, :] = y[:KX, lanes] + minus_i(y[KX:, lanes])


MODES = KOWN * KX


def hold_body(near_ref, misfit_ref, near_out_ref, misfit_out_ref):
    near_out_ref[...] = near_ref[...]
    misfit_out_ref[...] = misfit_ref[...]


def along_x_body(shot, a_ref, b_ref, c_ref, d_ref, near_ref, next_ref, far_ref, last_ref, tmp):
    tmp[...] = (a_ref[...].astype(F32) + b_ref[...].astype(F32)) + (
        c_ref[...].astype(F32) + d_ref[...].astype(F32)
    )
    y = shot[0] // 4 % 4
    for by, out_ref in enumerate((near_ref, next_ref, far_ref, last_ref)):
        for z in range(2):
            start = pl.multiple_of(64 * (4 * z + (y + by) % 4), 64)
            out_ref[64 * z : 64 * z + 64, :] = tmp[pl.ds(start, 64), :].astype(out_ref.dtype)


def along_y_body(a_ref, b_ref, c_ref, d_ref, modes_ref, out_ref, send_ref):
    modes = modes_ref[...]
    total = (a_ref[...] + b_ref[...].astype(F32)) + (
        c_ref[...].astype(F32) + d_ref[...].astype(F32)
    )
    out_ref[0:MODES, :] = modes
    out_ref[MODES:, :] = total
    send_ref[0:MODES, :] = modes.astype(BF16)
    send_ref[MODES:, :] = total.astype(BF16)


def keep_and_send(modes, squares, out_ref, send_ref):
    out_ref[0:MODES, :] = modes
    out_ref[MODES : MODES + 16, :] = jnp.broadcast_to(squares, (16, 128))
    send_ref[0:MODES, :] = modes.astype(BF16)
    high = squares.astype(BF16).astype(F32)
    rest = squares - high
    middle = rest.astype(BF16).astype(F32)
    row = lax.broadcasted_iota(jnp.int32, (16, 128), 0)
    terms = jnp.where(row == 0, high, jnp.where(row == 1, middle, rest - middle))
    send_ref[MODES : MODES + 16, :] = jnp.where(row < 3, terms, 0.0).astype(BF16)


def sum_of(own_ref, parts):
    modes = own_ref[0:MODES, :]
    squares = own_ref[MODES : MODES + 1, :]
    for part in parts:
        modes = modes + part[0:MODES, :].astype(F32)
        terms = part[MODES : MODES + 16, :].astype(F32)
        squares = squares + jnp.sum(terms, axis=0, keepdims=True)
    return modes, squares


def along_z_body(shot, a_ref, b_ref, local_ref, out_ref, send_ref, tmp):
    total = a_ref[...] + b_ref[...].astype(F32)
    planes = total[MODES:]
    tmp[...] = planes
    local_ref[...] = tmp[pl.ds(pl.multiple_of(64 * (shot[0] // 16), 64), 64), :]
    squares = jnp.sum(planes * planes, axis=0, keepdims=True)
    keep_and_send(total[0:MODES], squares, out_ref, send_ref)


def join_body(a_ref, b_ref, c_ref, d_ref, out_ref, send_ref):
    modes, squares = sum_of(a_ref, (b_ref, c_ref, d_ref))
    keep_and_send(modes, squares, out_ref, send_ref)


def arrange_body(in_ref, repeat_ref, pick_ref, out_ref):
    row = lax.broadcasted_iota(jnp.int32, (64, 128), 0)
    lane = lax.broadcasted_iota(jnp.int32, (64, 128), 1)
    same = row % 4 == lane % 4
    total = jnp.zeros((64, 128), F32)
    for g in range(4):
        rest = in_ref[16 * g : 16 * g + 16, :]
        for _ in range(3):
            part = rest.astype(BF16)
            rest = rest - part.astype(F32)
            wide = jnp.where(same, dot(repeat_ref[...], part), 0.0).astype(BF16)
            total = total + dot(wide, pick_ref[g])
    out_ref[...] = total


def adjoint_mix_body(
    near_ref, next_ref, far_ref, last_ref, t_ref, high_ref, low_ref, extra_ref, out_ref
):
    lane = lax.broadcasted_iota(jnp.int32, (KX, 128), 1)
    spectra, squares = sum_of(near_ref, (next_ref, far_ref, last_ref))
    total = jnp.zeros((KX, 128), F32)
    cross = jnp.zeros((KX, 128), F32)
    for k in range(KOWN):
        spectrum = spectra[KX * k : KX * k + KX]
        turned = minus_i(spectrum)
        for ab in range(16):
            base = (ab // 4) * 32 + (ab % 4) * 6 + 2 * k
            plane = t_ref[pl.ds((k * 24 + ab) * KX, KX), :]
            re = jnp.sum(spectrum * plane, axis=1, keepdims=True)
            im = jnp.sum(turned * plane, axis=1, keepdims=True)
            total = jnp.where(lane == base, re, total)
            total = jnp.where(lane == base + 1, im, total)
        sh, sl = split(spectrum)
        cross = cross + dot(sh, high_ref[k]) + dot(sl, high_ref[k]) + dot(sh, low_ref[k])
    total = total * (1.0 / VELOCITY_SCALE)
    product = jnp.sum(total * cross, axis=0, keepdims=True)
    for z in range(SPACE // 2):
        out_ref[z, :KX, :] = total
        out_ref[z, KX : KX + 1, :] = product
        out_ref[z, KX + 1 : KX + 5, :] = extra_ref[0:4, :]
        out_ref[z, KX + 5 : KX + 6, :] = squares
        out_ref[z, KX + 6 : KX + 8, :] = jnp.zeros((2, 128), F32)


def output_body(
    own, m_ref, other_ref, back_ref, block_ref, local_ref, diag_rows_ref, off_rows_ref, diag_ref, off_ref,
    out_ref, misfit_ref, tmp,
):
    lane = lax.broadcasted_iota(jnp.int32, (KX, 128), 1)
    upper, lower = [], []
    tail = jnp.zeros((8, 128), F32)
    even = own[0] % 2 == 0
    for q in range(SPACE):
        mine, theirs = m_ref[q // 2], other_ref[q // 2]
        whole = jnp.where(even, mine, theirs) if q % 2 == 0 else jnp.where(even, theirs, mine)
        x = whole[:KX]
        tail = tail + whole[KX:]
        turned = jnp.where(lane % 2 == 0, -pltpu.roll(x, 127, 1), pltpu.roll(x, 1, 1))
        upper.append(x)
        lower.append(turned)
    n = jnp.concatenate(
        [jnp.concatenate(upper, axis=1), jnp.concatenate(lower, axis=1)], axis=0
    )
    high, low = split(n)
    nearly = dot(off_rows_ref[...], high)
    diag = jnp.concatenate([diag_rows_ref[...]] * 8, axis=1)
    left = n * diag + nearly
    right = n * diag_ref[...] + dot(high, off_ref[...])
    square = jnp.sum(jnp.sum(left * right, axis=0, keepdims=True), axis=1, keepdims=True)
    sums = jnp.sum(tail, axis=1, keepdims=True)
    total = square + 2.0 * sums[0:1] + sums[5:6]
    scale = 1.0 / jnp.sqrt(total / float(16 * GH * GW) + EPSILON)
    rows = dot(back_ref[0], high) + dot(back_ref[0], low)
    group = lax.broadcasted_iota(jnp.int32, (ROWS, 1024), 1) % 128 // 32
    rows = jnp.concatenate([jnp.where(group == a, rows, 0.0) for a in range(4)], axis=0)
    rh, rl = split(rows)
    block = dot(rh, block_ref[...]) + dot(rl, block_ref[...])
    for a in range(4):
        tmp[pl.ds(a, ROWS, stride=4), 0:64] = block[ROWS * a : ROWS * a + ROWS]
    out_ref[...] = (tmp[...].T[0:64] + local_ref[...]) * scale
    place = lax.broadcasted_iota(jnp.int32, (1, 4), 1)
    misfit = jnp.zeros((1, 4), F32)
    for s in range(4):
        misfit = jnp.where(place == s, sums[s + 1 : s + 2] * (0.5 / float(REC * GW)), misfit)
    misfit_ref[...] = misfit


def turn(size, stride, count, by):
    pairs = []
    for i in range(count):
        digit = (i // stride) % size
        pairs.append((i, i + ((digit + by) % size - digit) * stride))
    return pairs


def from_x(*parts):
    return [
        lax.ppermute(part, "shot", turn(4, 1, SHOT, by + 1)) for by, part in enumerate(parts)
    ]


def from_y(*parts):
    return [
        lax.ppermute(part, "shot", turn(4, 4, SHOT, by + 1)) for by, part in enumerate(parts)
    ]


def gather_z(copies):
    return lax.all_to_all(
        copies, "space", 0, 0, axis_index_groups=[[0, 2, 4, 6], [1, 3, 5, 7]], tiled=True
    )


def from_core(values):
    return lax.ppermute(values, "space", [(n, n ^ 1) for n in range(SPACE)])


def shards(
    velocity,
    encoder_weight,
    encoder_bias,
    source_amplitude,
    source_row,
    source_column,
    receiver_rows,
    point_weight,
    spectral_weight,
    layer_bias,
    out_weight,
    observed,
):
    p = lax.axis_index("space").astype(jnp.int32)
    i = lax.axis_index("shot").astype(jnp.int32)
    own, shot = p[None], i[None]
    fine = (128, 4 * GW)
    operator_rows = KOWN * KX * 24
    encoder = encoder_weight.reshape(16, C)
    bias, amplitude = encoder_bias[None], source_amplitude[None]
    both_rows = jnp.asarray(BOTH_ROWS)
    table = jnp.asarray(WEIGHTED)
    record = observed.reshape(PAIRS, GW)
    row_spec = full_spec((1, C))

    partial = call(
        velocity_body, 1, shaped((SPACE, KX, 128)),
        [full_spec(fine), full_spec((4 * GW, 256)), own_spec((192, 256))],
        kept_spec((SPACE, KX, 128)), name="velocity_spectrum",
    )(own, velocity, jnp.asarray(COLUMNS), jnp.asarray(ROW_SUMS))
    spectra = lax.all_to_all(partial, "space", 0, 0, tiled=True)

    bias, _ = lax.optimization_barrier((bias, partial))
    operator, sides, bumps = call(
        operator_body, 3,
        (shaped((operator_rows, 128)), shaped((KOWN, PAIRS, 256), BF16), shaped((PAIRS, GW))),
        [
            full_spec((16, C)), row_spec, row_spec, full_spec((KX, KOWN, C, 128)),
            full_spec((4, REC)), full_spec((128, GH)), own_spec((8, GW)),
        ],
        (full_spec((operator_rows, 128)), full_spec((KOWN, PAIRS, 256)), full_spec((PAIRS, GW))),
        name="operator",
    )(
        own, source_row, source_column, encoder, bias, amplitude, spectral_weight, receiver_rows,
        jnp.asarray(PAIRED_ROWS),
        jnp.asarray(OWN_COLUMNS),
    )

    sent = call(
        mix_body, 1, shaped((SPACE // 2, PAIRS, 384), BF16),
        [
            kept_spec((SPACE, KX, 128)), own_spec((KX, 128)),
            full_spec((operator_rows, 128)), full_spec((KOWN, PAIRS, 256)),
        ],
        kept_spec((SPACE // 2, PAIRS, 384)), name="mix_modes",
    )(own, spectra, jnp.asarray(ONES), operator, sides)
    gathered = gather_z(sent)

    late_bias, _ = lax.optimization_barrier((layer_bias[None], sent))
    planes, wk, vectors, placed, spread_high, spread_low, pairs = call(
        planes_body, 2,
        (
            shaped((ROWS, 16, GW)), shaped((48, C), BF16), shaped((3, C, 128)),
            shaped((8, 128, 128), BF16), shaped((KOWN, 128, 128), BF16),
            shaped((KOWN, 128, 128), BF16), shaped((144,), jnp.int32),
        ),
        [
            full_spec(fine), full_spec((512, 512)), full_spec((16, C)), row_spec, row_spec,
            full_spec((C, C)), row_spec, row_spec, full_spec((KOWN * 2, 128, 128)),
        ],
        (
            full_spec((ROWS, 16, GW)), full_spec((48, C)), full_spec((3, C, 128)),
            full_spec((8, 128, 128)), full_spec((KOWN, 128, 128)), full_spec((KOWN, 128, 128)),
            pl.BlockSpec(memory_space=pltpu.SMEM),
        ),
        [pltpu.VMEM((128, 512), F32)], name="velocity_planes",
    )(
        own, receiver_rows, velocity, jnp.asarray(SELECT), encoder, bias, amplitude, point_weight, late_bias,
        out_weight[None], jnp.asarray(LANES),
    )

    gathered, planes = lax.optimization_barrier((gathered, planes))
    others = from_core(gathered)
    predicted, slopes, stats = call(
        forward_body, 2,
        (shaped((PAIRS, GW)), shaped((PAIRS * C, GW), BF16), shaped((SPACE, 8, 128))),
        [
            kept_spec((SPACE // 2, PAIRS, 384)), kept_spec((SPACE // 2, PAIRS, 384)),
            full_spec((ROWS, 16, GW)), full_spec((48, GW)),
            full_spec((48, C)), full_spec((PAIRS, GW)), full_spec((3, C, 128)),
            full_spec((PAIRS, GW)),
        ],
        (
            full_spec((PAIRS, GW)), pl.BlockSpec(memory_space=pl.ANY),
            kept_spec((SPACE, 8, 128)),
        ),
        [
            pltpu.VMEM((3 * SPACE * PAIRS, 128), F32), pltpu.VMEM((8, GW), F32),
            pltpu.VMEM((PAIRS * C, GW), BF16), pltpu.SemaphoreType.DMA((PAIRS // 2,)),
        ], name="forward_rows",
    )(own, pairs, gathered, others, planes, table, wk, bumps, vectors, record)
    stats = lax.all_to_all(stats, "space", 0, 0, tiled=True)

    columns, near, after, far, last, misfits = call(
        backward_body, 3,
        (shaped((SPACE, ROWS, 384), BF16),) + (shaped((GW, 128), BF16),) * 4 + (shaped((8, 128)),),
        [
            kept_spec((SPACE, 8, 128)), full_spec((PAIRS, GW)),
            full_spec((PAIRS, GW)), pl.BlockSpec(memory_space=pl.ANY), full_spec((48, GW)),
            full_spec((8, 128, 128)),
        ],
        (kept_spec((SPACE, ROWS, 384)),) + (kept_spec((GW, 128)),) * 4 + (full_spec((8, 128)),),
        [
            pltpu.VMEM((16, GW), F32), pltpu.VMEM((ROWS * 48, 128), F32),
            pltpu.VMEM((4, GW, 128), F32), pltpu.VMEM((PAIRS * C, GW), BF16),
            pltpu.SemaphoreType.DMA((PAIRS // 2,)),
        ],
        name="backward_rows",
    )(own, pairs, shot, stats, record, predicted, slopes, table, placed)

    columns = lax.all_to_all(columns, "space", 0, 0, tiled=True)
    adjoint = call(
        adjoint_body, 0, shaped((KOWN * KX, 128)),
        [kept_spec((SPACE, ROWS, 384)), full_spec((96, GH))],
        kept_spec((KOWN * KX, 128)), name="adjoint_rows", limit=SMALL,
    )(columns, both_rows)
    arrived = from_x(after, far, last)
    near, misfits = call(
        hold_body, 0, (shaped((GW, 128), BF16), shaped((8, 128))),
        [kept_spec((GW, 128)), kept_spec((8, 128))], (kept_spec((GW, 128)), kept_spec((8, 128))),
        name="hold", limit=SMALL,
    )(near, misfits)
    near, misfits, *arrived = lax.optimization_barrier((near, misfits, *arrived))
    shares = call(
        along_x_body, 1, (shaped((128, 128)),) + (shaped((128, 128), BF16),) * 3,
        [kept_spec((GW, 128))] * 4, (kept_spec((128, 128)),) * 4, [pltpu.VMEM((GW, 128), F32)],
        name="along_x", limit=SMALL,
    )(shot, near, *arrived)
    sums, sent = call(
        along_y_body, 0, (shaped((MODES + 128, 128)), shaped((MODES + 128, 128), BF16)),
        [kept_spec((128, 128))] * 4 + [kept_spec((MODES, 128))],
        (kept_spec((MODES + 128, 128)),) * 2, name="along_y", limit=SMALL,
    )(shares[0], *from_y(*shares[1:]), adjoint)
    carried = (shaped((MODES + 16, 128)), shaped((MODES + 16, 128), BF16))
    carried_specs = (kept_spec((MODES + 16, 128)),) * 2
    local, sums, sent = call(
        along_z_body, 1, (shaped((64, 128)),) + carried,
        [kept_spec((MODES + 128, 128))] * 2, (kept_spec((64, 128)),) + carried_specs,
        [pltpu.VMEM((128, 128), F32)], name="along_z", limit=SMALL,
    )(shot, sums, lax.ppermute(sent, "shot", turn(2, 16, SHOT, 1)))
    parts = from_x(sent, sent, sent)
    local = call(
        arrange_body, 0, shaped((64, 128)),
        [kept_spec((64, 128)), kept_spec((64, 16)), kept_spec((4, 128, 128))],
        kept_spec((64, 128)), name="arrange", limit=SMALL,
    )(local, jnp.asarray(REPEAT), jnp.asarray(PICK))
    mine = lax.dynamic_index_in_dim(jnp.asarray(BLOCKS), i, 0, keepdims=False)
    parts, local, mine = lax.optimization_barrier((parts, local, mine))
    sums, sent = call(
        join_body, 0, carried, [kept_spec((MODES + 16, 128))] * 4, carried_specs, name="join",
        limit=SMALL,
    )(sums, *parts)

    modes = call(
        adjoint_mix_body, 0, shaped((SPACE // 2, KX + 8, 128)),
        [kept_spec((MODES + 16, 128))] * 4
        + [
            full_spec((operator_rows, 128)), full_spec((KOWN, 128, 128)),
            full_spec((KOWN, 128, 128)), full_spec((8, 128)),
        ],
        kept_spec((SPACE // 2, KX + 8, 128)), name="adjoint_mix", limit=SMALL,
    )(sums, *from_y(sent, sent, sent), operator, spread_high, spread_low, misfits)
    modes = gather_z(modes)
    other_modes = from_core(modes)
    block, misfit = call(
        output_body, 1, (shaped((64, 128)), shaped((1, 4))),
        [
            kept_spec((SPACE // 2, KX + 8, 128)), kept_spec((SPACE // 2, KX + 8, 128)),
            own_spec((ROWS, 96)), full_spec((1024, 64)),
            full_spec((64, 128)), full_spec((96, 128)), full_spec((96, 96)),
            full_spec((1, 1024)), full_spec((1024, 1024)),
        ],
        (full_spec((64, 128)), full_spec((1, 4))), [pltpu.VMEM((128, 128), F32)],
        name="output_block", limit=SMALL,
    )(
        own, modes, other_modes, jnp.asarray(ROWS_BACK), mine, local, jnp.asarray(DIAG_ROWS),
        jnp.asarray(OFF_ROWS), jnp.asarray(DIAG_WIDE), jnp.asarray(OFF_WIDE),
    )
    return (misfit.reshape(4), block.T)


def solution(mesh):
    in_specs = (
        P("space", None),
        P(),
        P(),
        P(),
        P("shot"),
        P("shot"),
        P("shot", None),
        P(),
        P(None, "space", None, None),
        P(),
        P(),
        P("shot", None, None),
    )
    out_specs = (P("shot"), P("space", "shot"))
    return jax.shard_map(shards, mesh=mesh, in_specs=in_specs, out_specs=out_specs, check_vma=False)
```

```python
import math

import jax
import jax.numpy as jnp
import ml_dtypes
import numpy as np
from jax import lax
from jax.experimental import pallas as pl
from jax.experimental.pallas import tpu as pltpu
from jax.sharding import PartitionSpec as P

C = 64
KX = 48
KY = 24
GH = 256
GW = 512
REC = 16
SPACE = 8
SHOT = 32
ROWS = GH // SPACE
KOWN = KY // SPACE
COUNT = 64
FIRST = 72
PAIRS = 64
EPSILON = 1e-06
VELOCITY_MEAN = 3.0
VELOCITY_SCALE = 1.5
HIGHEST = lax.Precision.HIGHEST
F32 = jnp.float32
BF16 = jnp.bfloat16
SMALL = 28 << 20
LARGE = 56 << 20


def bf(values):
    return np.asarray(values, np.float32).astype(ml_dtypes.bfloat16)


def as64(values):
    return values.astype(np.float64)


def make_tables():
    k = np.arange(KY)
    w = np.arange(GW)
    phase = (k[:, None] * w[None, :] % GW) * (2.0 * math.pi / GW)
    plain = bf(np.stack([np.cos(phase), -np.sin(phase)], 1) / math.sqrt(GW))
    f = np.where(np.arange(KX) < KX // 2, np.arange(KX), np.arange(KX) - KX)
    phase = (f[:, None] * np.arange(GH)[None, :] % GH) * (2.0 * math.pi / GH)
    cos_rows = bf(np.cos(phase) / math.sqrt(GH))
    sin_rows = bf(np.sin(phase) / math.sqrt(GH))
    return plain, cos_rows, sin_rows


PLAIN, COS_ROWS, SIN_ROWS = make_tables()
MODE_WEIGHT = np.where(np.arange(KY) == 0, 1.0, 2.0)


def columns_table():
    table = np.zeros((GW, 4, SPACE, 32), np.float32)
    plain = PLAIN.astype(np.float32).reshape(SPACE, 6, GW)
    for b in range(4):
        table[:, b, :, 6 * b : 6 * b + 6] = plain.transpose(2, 0, 1)
    return bf(table.reshape(4 * GW, 256))


def rows_table():
    table = np.zeros((SPACE, 4, KX, 2, ROWS, 4), np.float32)
    for p in range(SPACE):
        for a in range(4):
            table[p, a, :, 0, :, a] = COS_ROWS[:, ROWS * p : ROWS * p + ROWS]
            table[p, a, :, 1, :, a] = SIN_ROWS[:, ROWS * p : ROWS * p + ROWS]
    return bf(table.reshape(SPACE, 4 * KX, 256))


def ones_table():
    wsum = as64(PLAIN).sum(-1)
    c, s = as64(COS_ROWS).sum(-1), as64(SIN_ROWS).sum(-1)
    table = np.zeros((SPACE, KX, 128), np.float32)
    for q in range(SPACE):
        for k in range(KOWN):
            re, im = wsum[3 * q + k]
            table[q, :, 24 + 2 * k] = c * re + s * im
            table[q, :, 25 + 2 * k] = c * im - s * re
    return table


def select_table():
    table = np.zeros((128, 4, 4, 128), np.float32)
    for b in range(4):
        table[np.arange(128), b, b, np.arange(128)] = 1.0
    return bf(table.reshape(512, 512))


def weighted_table():
    plain = PLAIN.astype(np.float32) * MODE_WEIGHT[:, None, None]
    return bf(plain.reshape(SPACE, KOWN, 2, GW).transpose(1, 2, 0, 3).reshape(48, GW))


def gram_tables():
    full = np.concatenate([as64(COS_ROWS), as64(SIN_ROWS)], 0)
    gram_rows = full @ full.T
    e = as64(PLAIN).reshape(48, GW)
    gram = e @ e.T
    wide = np.zeros((SPACE, 4, 32, SPACE, 4, 32))
    gram = gram.reshape(SPACE, 6, SPACE, 6)
    for a in range(4):
        for b in range(4):
            wide[:, a, b * 6 : b * 6 + 6, :, a, b * 6 : b * 6 + 6] = gram
    wide = wide.reshape(1024, 1024)
    diag_rows = np.broadcast_to(np.diag(gram_rows)[:, None], (96, 128))
    off_rows = bf(gram_rows - np.diag(np.diag(gram_rows)))
    diag_wide = np.diag(wide)[None, :]
    off_wide = bf(wide - np.diag(np.diag(wide)))
    return (
        np.asarray(diag_rows, np.float32),
        off_rows,
        np.asarray(diag_wide, np.float32),
        off_wide,
    )


COLUMNS = columns_table()
ROW_SUMS = rows_table()
ONES = ones_table()
SELECT = select_table()
WEIGHTED = weighted_table()
DIAG_ROWS, OFF_ROWS, DIAG_WIDE, OFF_WIDE = gram_tables()
PAIRED_ROWS = np.zeros((2, 64, GH), np.float32)
PAIRED_ROWS[0, :KX], PAIRED_ROWS[1, :KX] = COS_ROWS, SIN_ROWS
PAIRED_ROWS = bf(PAIRED_ROWS.reshape(128, GH))
OWN_COLUMNS = np.zeros((SPACE, 8, GW), np.float32)
OWN_COLUMNS[:, :6] = PLAIN.reshape(SPACE, 6, GW)
OWN_COLUMNS = bf(OWN_COLUMNS)


def lanes_table():
    table = np.zeros((KOWN, 2, 128, 128), np.float32)
    for k in range(KOWN):
        for part in range(2):
            for ab in range(16):
                table[k, part, ab, 32 * (ab // 4) + 6 * (ab % 4) + 2 * k + part] = 1.0
    return bf(table.reshape(KOWN * 2, 128, 128))


def block_table():
    table = np.zeros((SHOT, SPACE, 4, 32, 16, 4), np.float32)
    plain = PLAIN.astype(np.float32).reshape(SPACE, 6, SHOT, 16)
    for b in range(4):
        table[:, :, :, 6 * b : 6 * b + 6, :, b] = plain.transpose(2, 0, 1, 3)[:, :, None]
    return bf(table.reshape(SHOT, 1024, 64))


REPEAT = np.zeros((64, 16), np.float32)
REPEAT[np.arange(64), np.arange(64) // 4] = 1.0
REPEAT = bf(REPEAT)
PICK = np.zeros((4, 128, 128), np.float32)
for g in range(4):
    PICK[g, np.arange(128), 32 * g + np.arange(128) // 4] = 1.0
PICK = bf(PICK)
LANES = lanes_table()
BLOCKS = block_table()
BOTH_ROWS = bf(np.concatenate([COS_ROWS.astype(np.float32), SIN_ROWS.astype(np.float32)], 0))
ROWS_BACK = bf(
    BOTH_ROWS.astype(np.float32).T.reshape(SPACE, ROWS, 96)
)


def split(values):
    high = values.astype(BF16)
    return high, (values - high.astype(F32)).astype(BF16)


def dot(a, b, dims=((1,), (0,))):
    return lax.dot_general(a, b, (dims, ((), ())), preferred_element_type=F32)


def dot_split(a, b):
    high, low = split(b)
    return dot(a, high) + dot(a, low)


def minus_i(x):
    lane = lax.broadcasted_iota(jnp.int32, x.shape, 1)
    swapped = pltpu.roll(x, 64, 1)
    return jnp.where(lane < 64, swapped, -swapped)


def times_i(x):
    lane = lax.broadcasted_iota(jnp.int32, x.shape, 1)
    swapped = pltpu.roll(x, 64, 1)
    return jnp.where(lane < 64, -swapped, swapped)


def full_spec(shape):
    return pl.BlockSpec(shape, lambda *_: (0,) * len(shape))


def own_spec(shape, place=0):
    return pl.BlockSpec((1,) + shape, lambda i, *own: (own[place][0],) + (0,) * len(shape))


def kept_spec(shape):
    return pl.BlockSpec(memory_space=pltpu.VMEM)


def call(body, prefetch, out_shape, in_specs, out_specs, scratch=(), name=None, limit=LARGE):
    return pl.pallas_call(
        body,
        out_shape=out_shape,
        grid_spec=pltpu.PrefetchScalarGridSpec(
            num_scalar_prefetch=prefetch,
            grid=(1,),
            in_specs=in_specs,
            out_specs=out_specs,
            scratch_shapes=list(scratch),
        ),
        compiler_params=pltpu.CompilerParams(vmem_limit_bytes=limit),
        name=name,
    )


def shaped(shape, dtype=F32):
    return jax.ShapeDtypeStruct(shape, dtype)


def velocity_body(own, v_ref, cols_ref, rows_ref, out_ref):
    vn = (v_ref[...] - VELOCITY_MEAN) / VELOCITY_SCALE
    high, low = split(vn)
    xx = dot(high, cols_ref[...]) + dot(low, cols_ref[...])
    even = lax.broadcasted_iota(jnp.int32, xx.shape, 1) % 2 == 0
    turned = jnp.where(even, pltpu.roll(xx, 255, 1), -pltpu.roll(xx, 1, 1))
    stacked = jnp.concatenate([xx, turned], axis=0)
    yy = dot_split(rows_ref[0], stacked)
    group = lax.broadcasted_iota(jnp.int32, (KX, 128), 1) // 32
    for q in range(SPACE):
        total = jnp.zeros((KX, 128), F32)
        for a in range(4):
            piece = yy[KX * a : KX * a + KX, 128 * (q // 4) : 128 * (q // 4) + 128]
            shift = (32 * a - 32 * (q % 4)) % 128
            if shift:
                piece = pltpu.roll(piece, shift, 1)
            total = jnp.where(group == a, piece, total)
        out_ref[q] = total


def column_of(row):
    return jnp.broadcast_to(row, (128, C)).T


def planes_body(
    own, rows_ref, v_ref, sel_ref, enc_ref, bias_ref, amp_ref, point_ref, layer_ref, weight_ref,
    out_ref, wk_ref, vec_ref, list_ref, tmp,
):
    def find(r, count):
        row = rows_ref[r >> 4, r & 15] - own[0] * ROWS
        list_ref[count] = r
        list_ref[FIRST + count] = row
        return count + jnp.where((row >= 0) & (row < ROWS), 1, 0)

    list_ref[COUNT] = lax.fori_loop(0, PAIRS, find, 0)
    for m in range(4):
        vn = (v_ref[:, 512 * m : 512 * m + 512] - VELOCITY_MEAN) / VELOCITY_SCALE
        high, low = split(vn)
        tmp[...] = dot(high, sel_ref[...]) + dot(low, sel_ref[...])
        for h in range(ROWS):
            for b in range(4):
                out_ref[h, 4 * b : 4 * b + 4, 128 * m : 128 * m + 128] = tmp[
                    4 * h : 4 * h + 4, 128 * b : 128 * b + 128
                ]
    stack = jnp.concatenate(
        [enc_ref[...], bias_ref[...], amp_ref[...], jnp.zeros((6, C), F32)], axis=0
    )
    high, low = split(stack)
    pointed = dot(high, point_ref[...]) + dot(low, point_ref[...])
    swapped = jnp.concatenate(
        [pointed[4 * a + b : 4 * a + b + 1] for b in range(4) for a in range(4)], axis=0
    )
    high, low = split(swapped)
    wk_ref[0:16] = high
    wk_ref[16:32] = high
    wk_ref[32:48] = low
    vec_ref[0] = column_of(pointed[17:18])
    vec_ref[1] = column_of(pointed[16:17] + layer_ref[...])
    vec_ref[2] = column_of(weight_ref[...])


def weights_body(own, enc_ref, point_ref, lanes_ref, place_ref, high_ref, low_ref):
    high, low = split(enc_ref[...])
    pointed = dot(high, point_ref[...]) + dot(low, point_ref[...])
    turned = jnp.concatenate([pointed[:16], jnp.zeros((112, C), F32)], axis=0).T
    scaled = turned * (1.0 / VELOCITY_SCALE)
    for e in range(8):
        high, low = split(pltpu.roll(scaled, 16 * e, 1) if e else scaled)
        place_ref[e, 0:C] = high
        place_ref[e, C : 2 * C] = low
    th, tl = split(scaled)
    for k in range(KOWN):
        reach = jnp.where((own[0] == 0) & (k == 0), 1.0, 0.5)
        for part in range(2):
            wide = (dot(th, lanes_ref[2 * k + part]) + dot(tl, lanes_ref[2 * k + part])) * reach
            high, low = split(wide)
            high_ref[k, C * part : C * part + C] = high
            low_ref[k, C * part : C * part + C] = low


def operator_body(
    own, source_row, source_column, enc_ref, bias_ref, amp_ref, w_ref, index_ref, rows_ref,
    cols_ref, out_ref, side_ref, bump_ref,
):
    stack = jnp.concatenate(
        [enc_ref[...], bias_ref[...], amp_ref[...], jnp.zeros((6, C), F32)], axis=0
    )
    high, low = split(stack)
    lhs = jnp.concatenate([high.astype(F32), low.astype(F32)], axis=0).astype(BF16)

    def step(j, carry):
        for k in range(KOWN):
            both = dot(lhs, w_ref[j, k])
            out_ref[pl.ds(k * KX * 24 + j, 24, stride=KX), :] = both[:24] + both[24:]
        return carry

    lax.fori_loop(0, KX, step, 0, unroll=8)
    square = (REC, REC)
    same = lax.broadcasted_iota(jnp.int32, square, 0) == lax.broadcasted_iota(jnp.int32, square, 1)
    receivers, row, column = [], [], []
    for s in range(4):
        wide = jnp.broadcast_to(index_ref[s : s + 1, :].astype(F32), square)
        receivers.append(jnp.sum(jnp.where(same, wide, 0.0), axis=1, keepdims=True))
        row.append(jnp.full((REC, 1), source_row[s], jnp.int32).astype(F32))
        column.append(jnp.full((REC, 1), source_column[s], jnp.int32).astype(F32))
    receiver = jnp.concatenate(receivers, axis=0)
    row = jnp.concatenate(row, axis=0)
    column = jnp.concatenate(column, axis=0)
    line = lax.broadcasted_iota(jnp.int32, (PAIRS, GH), 1).astype(F32)
    chosen = jnp.where(line == receiver, 1.0, 0.0).astype(BF16)
    at_rows = dot(chosen, rows_ref[...], ((1,), (1,)))
    gap = line - row
    high, low = split(jnp.exp(gap * gap * (-1.0 / 32.0)))
    row_side = dot(high, rows_ref[...], ((1,), (1,))) + dot(low, rows_ref[...], ((1,), (1,)))
    gap = lax.broadcasted_iota(jnp.int32, (PAIRS, GW), 1).astype(F32) - column
    bump = jnp.exp(gap * gap * (-1.0 / 32.0))
    high, low = split(bump)
    column_side = dot(high, cols_ref[0], ((1,), (1,))) + dot(low, cols_ref[0], ((1,), (1,)))
    gap = receiver - row
    bump_ref[...] = bump * jnp.exp(gap * gap * (-1.0 / 32.0))
    lane = lax.broadcasted_iota(jnp.int32, (PAIRS, 128), 1)
    first = at_rows * row_side
    second = at_rows * pltpu.roll(row_side, 64, 1)
    both = jnp.where(
        lane < 64, first + pltpu.roll(first, 64, 1), second - pltpu.roll(second, 64, 1)
    )
    turned = times_i(both)
    for k in range(KOWN):
        side_ref[k, :, 0:128] = at_rows.astype(BF16)
        side_ref[k, :, 128:256] = (
            both * column_side[:, 2 * k : 2 * k + 1] + turned * column_side[:, 2 * k + 1 : 2 * k + 2]
        ).astype(BF16)


def mix_body(own, v_ref, ones_ref, t_ref, l_ref, out_ref):
    spectrum = ones_ref[0]
    for q in range(SPACE):
        spectrum = spectrum + v_ref[q]
    for k in range(KOWN):
        first = jnp.zeros((KX, 128), F32)
        second = jnp.zeros((KX, 128), F32)
        for ab in range(17):
            lane = (ab // 4) * 32 + (ab % 4) * 6 + 2 * k if ab < 16 else 24 + 2 * k
            plane = t_ref[pl.ds((k * 24 + ab) * KX, KX), :]
            first = first + spectrum[:, lane : lane + 1] * plane
            second = second + spectrum[:, lane + 1 : lane + 2] * plane
        modes = first + times_i(second)
        source = t_ref[pl.ds((k * 24 + 17) * KX, KX), :]
        none = jnp.zeros((16, 128), F32)
        rhs = jnp.concatenate(
            [modes, none, times_i(modes), none, source, none, times_i(source), none], axis=0
        )
        values = dot(l_ref[k], rhs.astype(BF16)).astype(BF16)
        for z in range(SPACE // 2):
            out_ref[z, :, 128 * k : 128 * k + 128] = values


def gain_row():
    return 0.5 + lax.broadcasted_iota(jnp.int32, (1, GW), 1).astype(F32) * (1.0 / GW)


def forward_body(
    own, list_ref, d_ref, other_ref, planes_ref, table_ref, wk_ref, col_ref, vec_ref, obs_ref,
    pred_ref, slope_ref, stats_ref, dd, acc, slopes, sems,
):
    p = own[0]
    count = list_ref[COUNT]
    gain = gain_row()
    for m in range(3):
        for z in range(SPACE // 2):
            for source, core in ((d_ref, p % 2), (other_ref, 1 - p % 2)):
                start = pl.multiple_of(PAIRS * (SPACE * m + 2 * z + core), PAIRS)
                dd[pl.ds(start, PAIRS), :] = source[z, :, 128 * m : 128 * m + 128].astype(F32)
    acc[...] = jnp.zeros_like(acc)
    root = math.sqrt(2.0 / math.pi)

    def preactivation(n):
        r = list_ref[n]
        pieces = []
        for m in range(3):
            block = dd[pl.ds(SPACE * PAIRS * m + r, SPACE, stride=PAIRS), :]
            pieces.append(block[:, :64])
            pieces.append(pltpu.roll(block, 64, 1)[:, :64])
        lhs = jnp.concatenate(pieces, axis=0).astype(BF16)
        lhs = jnp.concatenate([lhs, wk_ref[...]], axis=0)
        high, low = split(planes_ref[list_ref[FIRST + n]])
        rhs = jnp.concatenate([table_ref[...], high, low, high], axis=0)
        return r, dot(lhs, rhs, ((0,), (0,)))

    def outgoing(t):
        rows = pl.ds(pl.multiple_of(2 * C * t, 2 * C), 2 * C)
        return pltpu.make_async_copy(slopes.at[rows], slope_ref.at[rows], sems.at[t])

    def step(t, carry):
        second = jnp.minimum(2 * t + 1, count - 1)
        both = [preactivation(2 * t), preactivation(second)]
        weights = [1.0, jnp.where(2 * t + 1 < count, 1.0, 0.0)]
        for e, (r, x) in enumerate(both):
            amp, const, weight = vec_ref[0], vec_ref[1], vec_ref[2]
            col = col_ref[pl.ds(r, 1), :]
            total = []
            for m in range(4):
                lanes = slice(128 * m, 128 * m + 128)
                xm = x[:, lanes] + const + amp * col[:, lanes]
                square = xm * xm
                u = jnp.tanh(root * (xm + 0.044715 * (square * xm)))
                cdf = 0.5 * (1.0 + u)
                slope = cdf + xm * (
                    (0.5 * root) * (1.0 - u * u) * (1.0 + 3.0 * 0.044715 * square)
                )
                slopes[pl.ds(pl.multiple_of(C * (2 * t + e), C), C), lanes] = (
                    slope * weight
                ).astype(BF16)
                total.append(jnp.sum(weight * (xm * cdf), axis=0, keepdims=True))
            predicted = jnp.concatenate(total, axis=1)
            pred_ref[pl.ds(r, 1), :] = predicted
            weighted = predicted * gain * weights[e]
            target = obs_ref[pl.ds(r, 1), :] * gain
            s = r >> 4
            acc[pl.ds(s, 1), :] += weighted * weighted
            acc[pl.ds(s + 4, 1), :] += weighted * target
        outgoing(t).start()
        return carry

    def finish(t, carry):
        outgoing(t).wait()
        return carry

    lax.fori_loop(0, (count + 1) >> 1, step, 0)
    stats = acc[:, :128] + acc[:, 128:256] + acc[:, 256:384] + acc[:, 384:]
    for q in range(SPACE):
        stats_ref[q] = stats
    lax.fori_loop(0, (count + 1) >> 1, finish, 0)


def backward_body(
    own, list_ref, shot, stats_ref, obs_ref, pred_ref, slope_ref, table_ref, place_ref,
    cols_ref, near_ref, next_ref, far_ref, last_ref, misfit_ref, coef, acc, planes, slopes, sems,
):
    pairs = list_ref[COUNT]

    def incoming(t):
        rows = pl.ds(pl.multiple_of(2 * C * t, 2 * C), 2 * C)
        return pltpu.make_async_copy(slope_ref.at[rows], slopes.at[rows], sems.at[t])

    def begin(t, carry):
        incoming(t).start()
        return carry

    lax.fori_loop(0, (pairs + 1) >> 1, begin, 0)
    count = float(REC * GW)
    stats = stats_ref[0]
    for q in range(1, SPACE):
        stats = stats + stats_ref[q]
    stats = jnp.sum(stats, axis=1, keepdims=True)
    gain = gain_row()
    for s in range(4):
        target = obs_ref[REC * s : REC * s + REC, :] * gain
        tt = jnp.sum(jnp.sum(target * target, axis=0, keepdims=True), axis=1, keepdims=True) / count
        ww = stats[s : s + 1] / count
        wt = stats[s + 4 : s + 5] / count
        sp2 = ww + EPSILON
        isp = 1.0 / jnp.sqrt(sp2)
        isq = 1.0 / jnp.sqrt(tt + EPSILON)
        kappa = ww / sp2 - wt * isp * isq
        coef[s : s + 1, :] = jnp.broadcast_to(isp, (1, GW))
        coef[s + 4 : s + 5, :] = jnp.broadcast_to(isq, (1, GW))
        coef[s + 8 : s + 9, :] = jnp.broadcast_to(kappa, (1, GW))
        coef[s + 12 : s + 13, :] = jnp.zeros((1, GW), F32)
    acc[...] = jnp.zeros_like(acc)
    planes[...] = jnp.zeros_like(planes)

    def inner_gradient(t, e, r, valid):
        s = r >> 4
        isp = coef[pl.ds(s, 1), :]
        isq = coef[pl.ds(s + 4, 1), :]
        kappa = coef[pl.ds(s + 8, 1), :]
        weighted = pred_ref[pl.ds(r, 1), :] * gain * isp
        target = obs_ref[pl.ds(r, 1), :] * gain * isq
        differ = (weighted - target) * valid
        coef[pl.ds(s + 12, 1), :] += differ * differ
        data = (GH * GW / count) * gain * isp * (differ - kappa * weighted * valid)
        slope = slopes[pl.ds(pl.multiple_of(C * (2 * t + e), C), C), :].astype(F32)
        return (slope * data).astype(BF16)

    def step(t, carry):
        second = jnp.minimum(2 * t + 1, pairs - 1)
        valid = jnp.where(2 * t + 1 < pairs, 1.0, 0.0)
        incoming(t).wait()
        one = inner_gradient(t, 0, list_ref[2 * t], 1.0)
        two = inner_gradient(t, 1, list_ref[second], valid)
        spectra = dot(table_ref[...], jnp.concatenate([one, two], axis=0), ((1,), (1,)))
        for e, (n, inner) in enumerate(((2 * t, one), (second, two))):
            row = list_ref[FIRST + n]
            half = slice(64 * e, 64 * e + 64)
            acc[pl.ds(pl.multiple_of(row * 48, 8), 48), half] += spectra[:, half]
            twice = jnp.concatenate([inner, inner], axis=0)
            planes[row >> 3] += dot(twice, place_ref[row & 7], ((0,), (0,)))
        return carry

    lax.fori_loop(0, (pairs + 1) >> 1, step, 0)
    lane = lax.broadcasted_iota(jnp.int32, (ROWS, 128), 1)
    for q in range(SPACE):
        for m in range(3):
            even = acc[pl.ds(16 * m + q, ROWS, stride=48), :]
            odd = acc[pl.ds(16 * m + 8 + q, ROWS, stride=48), :]
            joined = jnp.where(lane < 64, even + pltpu.roll(even, 64, 1), odd + pltpu.roll(odd, 64, 1))
            cols_ref[q, :, 128 * m : 128 * m + 128] = joined.astype(BF16)
    x = shot[0] % 4
    for by, grad_ref in enumerate((near_ref, next_ref, far_ref, last_ref)):
        column = (x + by) % 4
        for zy in range(8):
            for g in range(4):
                start = pl.multiple_of(64 * zy + 16 * column, 16)
                grad_ref[64 * zy + 16 * g : 64 * zy + 16 * g + 16, :] = planes[
                    g, pl.ds(start, 16), :
                ].astype(BF16)
    for s in range(4):
        row = coef[s + 12 : s + 13, :]
        misfit_ref[s : s + 1, :] = (
            row[:, :128] + row[:, 128:256] + row[:, 256:384] + row[:, 384:]
        )
    misfit_ref[4:8, :] = jnp.zeros((4, 128), F32)


def adjoint_body(a_ref, rows_ref, out_ref):
    values = jnp.concatenate([a_ref[q] for q in range(SPACE)], axis=0)
    y = dot(rows_ref[...], values)
    for k in range(KOWN):
        lanes = slice(128 * k, 128 * k + 128)
        out_ref[KX * k : KX * k + KX, :] = y[:KX, lanes] + minus_i(y[KX:, lanes])


MODES = KOWN * KX


def hold_body(near_ref, misfit_ref, near_out_ref, misfit_out_ref):
    near_out_ref[...] = near_ref[...]
    misfit_out_ref[...] = misfit_ref[...]


def along_x_body(shot, a_ref, b_ref, c_ref, d_ref, near_ref, next_ref, far_ref, last_ref, tmp):
    tmp[...] = (a_ref[...].astype(F32) + b_ref[...].astype(F32)) + (
        c_ref[...].astype(F32) + d_ref[...].astype(F32)
    )
    y = shot[0] // 4 % 4
    for by, out_ref in enumerate((near_ref, next_ref, far_ref, last_ref)):
        for z in range(2):
            start = pl.multiple_of(64 * (4 * z + (y + by) % 4), 64)
            out_ref[64 * z : 64 * z + 64, :] = tmp[pl.ds(start, 64), :].astype(out_ref.dtype)


def along_y_body(a_ref, b_ref, c_ref, d_ref, modes_ref, out_ref, send_ref):
    modes = modes_ref[...]
    total = (a_ref[...] + b_ref[...].astype(F32)) + (
        c_ref[...].astype(F32) + d_ref[...].astype(F32)
    )
    out_ref[0:MODES, :] = modes
    out_ref[MODES:, :] = total
    send_ref[0:MODES, :] = modes.astype(BF16)
    send_ref[MODES:, :] = total.astype(BF16)


def keep_and_send(modes, squares, out_ref, send_ref):
    out_ref[0:MODES, :] = modes
    out_ref[MODES : MODES + 16, :] = jnp.broadcast_to(squares, (16, 128))
    send_ref[0:MODES, :] = modes.astype(BF16)
    high = squares.astype(BF16).astype(F32)
    rest = squares - high
    middle = rest.astype(BF16).astype(F32)
    row = lax.broadcasted_iota(jnp.int32, (16, 128), 0)
    terms = jnp.where(row == 0, high, jnp.where(row == 1, middle, rest - middle))
    send_ref[MODES : MODES + 16, :] = jnp.where(row < 3, terms, 0.0).astype(BF16)


def sum_of(own_ref, parts):
    modes = own_ref[0:MODES, :]
    squares = own_ref[MODES : MODES + 1, :]
    for part in parts:
        modes = modes + part[0:MODES, :].astype(F32)
        terms = part[MODES : MODES + 16, :].astype(F32)
        squares = squares + jnp.sum(terms, axis=0, keepdims=True)
    return modes, squares


def along_z_body(shot, a_ref, b_ref, local_ref, out_ref, send_ref, tmp):
    total = a_ref[...] + b_ref[...].astype(F32)
    planes = total[MODES:]
    tmp[...] = planes
    local_ref[...] = tmp[pl.ds(pl.multiple_of(64 * (shot[0] // 16), 64), 64), :]
    squares = jnp.sum(planes * planes, axis=0, keepdims=True)
    keep_and_send(total[0:MODES], squares, out_ref, send_ref)


def join_body(a_ref, b_ref, c_ref, d_ref, out_ref, send_ref):
    modes, squares = sum_of(a_ref, (b_ref, c_ref, d_ref))
    keep_and_send(modes, squares, out_ref, send_ref)


def arrange_body(in_ref, repeat_ref, pick_ref, out_ref):
    row = lax.broadcasted_iota(jnp.int32, (64, 128), 0)
    lane = lax.broadcasted_iota(jnp.int32, (64, 128), 1)
    same = row % 4 == lane % 4
    total = jnp.zeros((64, 128), F32)
    for g in range(4):
        rest = in_ref[16 * g : 16 * g + 16, :]
        for _ in range(3):
            part = rest.astype(BF16)
            rest = rest - part.astype(F32)
            wide = jnp.where(same, dot(repeat_ref[...], part), 0.0).astype(BF16)
            total = total + dot(wide, pick_ref[g])
    out_ref[...] = total


def adjoint_mix_body(
    near_ref, next_ref, far_ref, last_ref, t_ref, high_ref, low_ref, extra_ref, out_ref
):
    lane = lax.broadcasted_iota(jnp.int32, (KX, 128), 1)
    spectra, squares = sum_of(near_ref, (next_ref, far_ref, last_ref))
    total = jnp.zeros((KX, 128), F32)
    cross = jnp.zeros((KX, 128), F32)
    for k in range(KOWN):
        spectrum = spectra[KX * k : KX * k + KX]
        turned = minus_i(spectrum)
        for ab in range(16):
            base = (ab // 4) * 32 + (ab % 4) * 6 + 2 * k
            plane = t_ref[pl.ds((k * 24 + ab) * KX, KX), :]
            re = jnp.sum(spectrum * plane, axis=1, keepdims=True)
            im = jnp.sum(turned * plane, axis=1, keepdims=True)
            total = jnp.where(lane == base, re, total)
            total = jnp.where(lane == base + 1, im, total)
        sh, sl = split(spectrum)
        cross = cross + dot(sh, high_ref[k]) + dot(sl, high_ref[k]) + dot(sh, low_ref[k])
    total = total * (1.0 / VELOCITY_SCALE)
    product = jnp.sum(total * cross, axis=0, keepdims=True)
    for z in range(SPACE // 2):
        out_ref[z, :KX, :] = total
        out_ref[z, KX : KX + 1, :] = product
        out_ref[z, KX + 1 : KX + 5, :] = extra_ref[0:4, :]
        out_ref[z, KX + 5 : KX + 6, :] = squares
        out_ref[z, KX + 6 : KX + 8, :] = jnp.zeros((2, 128), F32)


def output_body(
    own, m_ref, other_ref, back_ref, block_ref, local_ref, diag_rows_ref, off_rows_ref, diag_ref, off_ref,
    out_ref, misfit_ref, tmp,
):
    lane = lax.broadcasted_iota(jnp.int32, (KX, 128), 1)
    upper, lower = [], []
    tail = jnp.zeros((8, 128), F32)
    even = own[0] % 2 == 0
    for q in range(SPACE):
        mine, theirs = m_ref[q // 2], other_ref[q // 2]
        whole = jnp.where(even, mine, theirs) if q % 2 == 0 else jnp.where(even, theirs, mine)
        x = whole[:KX]
        tail = tail + whole[KX:]
        turned = jnp.where(lane % 2 == 0, -pltpu.roll(x, 127, 1), pltpu.roll(x, 1, 1))
        upper.append(x)
        lower.append(turned)
    n = jnp.concatenate(
        [jnp.concatenate(upper, axis=1), jnp.concatenate(lower, axis=1)], axis=0
    )
    high, low = split(n)
    nearly = dot(off_rows_ref[...], high)
    diag = jnp.concatenate([diag_rows_ref[...]] * 8, axis=1)
    left = n * diag + nearly
    right = n * diag_ref[...] + dot(high, off_ref[...])
    square = jnp.sum(jnp.sum(left * right, axis=0, keepdims=True), axis=1, keepdims=True)
    sums = jnp.sum(tail, axis=1, keepdims=True)
    total = square + 2.0 * sums[0:1] + sums[5:6]
    scale = 1.0 / jnp.sqrt(total / float(16 * GH * GW) + EPSILON)
    rows = dot(back_ref[0], high) + dot(back_ref[0], low)
    group = lax.broadcasted_iota(jnp.int32, (ROWS, 1024), 1) % 128 // 32
    rows = jnp.concatenate([jnp.where(group == a, rows, 0.0) for a in range(4)], axis=0)
    rh, rl = split(rows)
    block = dot(rh, block_ref[...]) + dot(rl, block_ref[...])
    for a in range(4):
        tmp[pl.ds(a, ROWS, stride=4), 0:64] = block[ROWS * a : ROWS * a + ROWS]
    out_ref[...] = (tmp[...].T[0:64] + local_ref[...]) * scale
    place = lax.broadcasted_iota(jnp.int32, (1, 4), 1)
    misfit = jnp.zeros((1, 4), F32)
    for s in range(4):
        misfit = jnp.where(place == s, sums[s + 1 : s + 2] * (0.5 / float(REC * GW)), misfit)
    misfit_ref[...] = misfit


def turn(size, stride, count, by):
    pairs = []
    for i in range(count):
        digit = (i // stride) % size
        pairs.append((i, i + ((digit + by) % size - digit) * stride))
    return pairs


def from_x(*parts):
    return [
        lax.ppermute(part, "shot", turn(4, 1, SHOT, by + 1)) for by, part in enumerate(parts)
    ]


def from_y(*parts):
    return [
        lax.ppermute(part, "shot", turn(4, 4, SHOT, by + 1)) for by, part in enumerate(parts)
    ]


def gather_z(copies):
    return lax.all_to_all(
        copies, "space", 0, 0, axis_index_groups=[[0, 2, 4, 6], [1, 3, 5, 7]], tiled=True
    )


def from_core(values):
    return lax.ppermute(values, "space", [(n, n ^ 1) for n in range(SPACE)])


def shards(
    velocity,
    encoder_weight,
    encoder_bias,
    source_amplitude,
    source_row,
    source_column,
    receiver_rows,
    point_weight,
    spectral_weight,
    layer_bias,
    out_weight,
    observed,
):
    p = lax.axis_index("space").astype(jnp.int32)
    i = lax.axis_index("shot").astype(jnp.int32)
    own, shot = p[None], i[None]
    fine = (128, 4 * GW)
    operator_rows = KOWN * KX * 24
    encoder = encoder_weight.reshape(16, C)
    bias, amplitude = encoder_bias[None], source_amplitude[None]
    both_rows = jnp.asarray(BOTH_ROWS)
    table = jnp.asarray(WEIGHTED)
    record = observed.reshape(PAIRS, GW)
    row_spec = full_spec((1, C))

    partial = call(
        velocity_body, 1, shaped((SPACE, KX, 128)),
        [full_spec(fine), full_spec((4 * GW, 256)), own_spec((192, 256))],
        kept_spec((SPACE, KX, 128)), name="velocity_spectrum",
    )(own, velocity, jnp.asarray(COLUMNS), jnp.asarray(ROW_SUMS))
    spectra = lax.all_to_all(partial, "space", 0, 0, tiled=True)

    bias, _ = lax.optimization_barrier((bias, partial))
    operator, sides, bumps = call(
        operator_body, 3,
        (shaped((operator_rows, 128)), shaped((KOWN, PAIRS, 256), BF16), shaped((PAIRS, GW))),
        [
            full_spec((16, C)), row_spec, row_spec, full_spec((KX, KOWN, C, 128)),
            full_spec((4, REC)), full_spec((128, GH)), own_spec((8, GW)),
        ],
        (full_spec((operator_rows, 128)), full_spec((KOWN, PAIRS, 256)), full_spec((PAIRS, GW))),
        name="operator",
    )(
        own, source_row, source_column, encoder, bias, amplitude, spectral_weight, receiver_rows,
        jnp.asarray(PAIRED_ROWS),
        jnp.asarray(OWN_COLUMNS),
    )

    sent = call(
        mix_body, 1, shaped((SPACE // 2, PAIRS, 384), BF16),
        [
            kept_spec((SPACE, KX, 128)), own_spec((KX, 128)),
            full_spec((operator_rows, 128)), full_spec((KOWN, PAIRS, 256)),
        ],
        kept_spec((SPACE // 2, PAIRS, 384)), name="mix_modes",
    )(own, spectra, jnp.asarray(ONES), operator, sides)
    gathered = gather_z(sent)

    late_bias, _ = lax.optimization_barrier((layer_bias[None], sent))
    planes, wk, vectors, pairs = call(
        planes_body, 2,
        (
            shaped((ROWS, 16, GW)), shaped((48, C), BF16), shaped((3, C, 128)),
            shaped((144,), jnp.int32),
        ),
        [
            full_spec(fine), full_spec((512, 512)), full_spec((16, C)), row_spec, row_spec,
            full_spec((C, C)), row_spec, row_spec,
        ],
        (
            full_spec((ROWS, 16, GW)), full_spec((48, C)), full_spec((3, C, 128)),
            pl.BlockSpec(memory_space=pltpu.SMEM),
        ),
        [pltpu.VMEM((128, 512), F32)], name="velocity_planes",
    )(
        own, receiver_rows, velocity, jnp.asarray(SELECT), encoder, bias, amplitude, point_weight, late_bias,
        out_weight[None],
    )

    gathered, planes = lax.optimization_barrier((gathered, planes))
    others = from_core(gathered)
    predicted, slopes, stats = call(
        forward_body, 2,
        (shaped((PAIRS, GW)), shaped((PAIRS * C, GW), BF16), shaped((SPACE, 8, 128))),
        [
            kept_spec((SPACE // 2, PAIRS, 384)), kept_spec((SPACE // 2, PAIRS, 384)),
            full_spec((ROWS, 16, GW)), full_spec((48, GW)),
            full_spec((48, C)), full_spec((PAIRS, GW)), full_spec((3, C, 128)),
            full_spec((PAIRS, GW)),
        ],
        (
            full_spec((PAIRS, GW)), pl.BlockSpec(memory_space=pl.ANY),
            kept_spec((SPACE, 8, 128)),
        ),
        [
            pltpu.VMEM((3 * SPACE * PAIRS, 128), F32), pltpu.VMEM((8, GW), F32),
            pltpu.VMEM((PAIRS * C, GW), BF16), pltpu.SemaphoreType.DMA((PAIRS // 2,)),
        ], name="forward_rows",
    )(own, pairs, gathered, others, planes, table, wk, bumps, vectors, record)
    stats = lax.all_to_all(stats, "space", 0, 0, tiled=True)

    late_encoder, _ = lax.optimization_barrier((encoder, predicted))
    placed, spread_high, spread_low = call(
        weights_body, 1,
        (shaped((8, 128, 128), BF16),) + (shaped((KOWN, 128, 128), BF16),) * 2,
        [full_spec((16, C)), full_spec((C, C)), full_spec((KOWN * 2, 128, 128))],
        (full_spec((8, 128, 128)), full_spec((KOWN, 128, 128)), full_spec((KOWN, 128, 128))),
        name="point_weights",
    )(own, late_encoder, point_weight, jnp.asarray(LANES))
    columns, near, after, far, last, misfits = call(
        backward_body, 3,
        (shaped((SPACE, ROWS, 384), BF16),) + (shaped((GW, 128), BF16),) * 4 + (shaped((8, 128)),),
        [
            kept_spec((SPACE, 8, 128)), full_spec((PAIRS, GW)),
            full_spec((PAIRS, GW)), pl.BlockSpec(memory_space=pl.ANY), full_spec((48, GW)),
            full_spec((8, 128, 128)),
        ],
        (kept_spec((SPACE, ROWS, 384)),) + (kept_spec((GW, 128)),) * 4 + (full_spec((8, 128)),),
        [
            pltpu.VMEM((16, GW), F32), pltpu.VMEM((ROWS * 48, 128), F32),
            pltpu.VMEM((4, GW, 128), F32), pltpu.VMEM((PAIRS * C, GW), BF16),
            pltpu.SemaphoreType.DMA((PAIRS // 2,)),
        ],
        name="backward_rows",
    )(own, pairs, shot, stats, record, predicted, slopes, table, placed)

    columns = lax.all_to_all(columns, "space", 0, 0, tiled=True)
    adjoint = call(
        adjoint_body, 0, shaped((KOWN * KX, 128)),
        [kept_spec((SPACE, ROWS, 384)), full_spec((96, GH))],
        kept_spec((KOWN * KX, 128)), name="adjoint_rows", limit=SMALL,
    )(columns, both_rows)
    arrived = from_x(after, far, last)
    near, misfits = call(
        hold_body, 0, (shaped((GW, 128), BF16), shaped((8, 128))),
        [kept_spec((GW, 128)), kept_spec((8, 128))], (kept_spec((GW, 128)), kept_spec((8, 128))),
        name="hold", limit=SMALL,
    )(near, misfits)
    near, misfits, *arrived = lax.optimization_barrier((near, misfits, *arrived))
    shares = call(
        along_x_body, 1, (shaped((128, 128)),) + (shaped((128, 128), BF16),) * 3,
        [kept_spec((GW, 128))] * 4, (kept_spec((128, 128)),) * 4, [pltpu.VMEM((GW, 128), F32)],
        name="along_x", limit=SMALL,
    )(shot, near, *arrived)
    sums, sent = call(
        along_y_body, 0, (shaped((MODES + 128, 128)), shaped((MODES + 128, 128), BF16)),
        [kept_spec((128, 128))] * 4 + [kept_spec((MODES, 128))],
        (kept_spec((MODES + 128, 128)),) * 2, name="along_y", limit=SMALL,
    )(shares[0], *from_y(*shares[1:]), adjoint)
    carried = (shaped((MODES + 16, 128)), shaped((MODES + 16, 128), BF16))
    carried_specs = (kept_spec((MODES + 16, 128)),) * 2
    local, sums, sent = call(
        along_z_body, 1, (shaped((64, 128)),) + carried,
        [kept_spec((MODES + 128, 128))] * 2, (kept_spec((64, 128)),) + carried_specs,
        [pltpu.VMEM((128, 128), F32)], name="along_z", limit=SMALL,
    )(shot, sums, lax.ppermute(sent, "shot", turn(2, 16, SHOT, 1)))
    parts = from_x(sent, sent, sent)
    local = call(
        arrange_body, 0, shaped((64, 128)),
        [kept_spec((64, 128)), kept_spec((64, 16)), kept_spec((4, 128, 128))],
        kept_spec((64, 128)), name="arrange", limit=SMALL,
    )(local, jnp.asarray(REPEAT), jnp.asarray(PICK))
    mine = lax.dynamic_index_in_dim(jnp.asarray(BLOCKS), i, 0, keepdims=False)
    parts, local, mine = lax.optimization_barrier((parts, local, mine))
    sums, sent = call(
        join_body, 0, carried, [kept_spec((MODES + 16, 128))] * 4, carried_specs, name="join",
        limit=SMALL,
    )(sums, *parts)

    modes = call(
        adjoint_mix_body, 0, shaped((SPACE // 2, KX + 8, 128)),
        [kept_spec((MODES + 16, 128))] * 4
        + [
            full_spec((operator_rows, 128)), full_spec((KOWN, 128, 128)),
            full_spec((KOWN, 128, 128)), full_spec((8, 128)),
        ],
        kept_spec((SPACE // 2, KX + 8, 128)), name="adjoint_mix", limit=SMALL,
    )(sums, *from_y(sent, sent, sent), operator, spread_high, spread_low, misfits)
    modes = gather_z(modes)
    other_modes = from_core(modes)
    block, misfit = call(
        output_body, 1, (shaped((64, 128)), shaped((1, 4))),
        [
            kept_spec((SPACE // 2, KX + 8, 128)), kept_spec((SPACE // 2, KX + 8, 128)),
            own_spec((ROWS, 96)), full_spec((1024, 64)),
            full_spec((64, 128)), full_spec((96, 128)), full_spec((96, 96)),
            full_spec((1, 1024)), full_spec((1024, 1024)),
        ],
        (full_spec((64, 128)), full_spec((1, 4))), [pltpu.VMEM((128, 128), F32)],
        name="output_block", limit=SMALL,
    )(
        own, modes, other_modes, jnp.asarray(ROWS_BACK), mine, local, jnp.asarray(DIAG_ROWS),
        jnp.asarray(OFF_ROWS), jnp.asarray(DIAG_WIDE), jnp.asarray(OFF_WIDE),
    )
    return (misfit.reshape(4), block.T)


def solution(mesh):
    in_specs = (
        P("space", None),
        P(),
        P(),
        P(),
        P("shot"),
        P("shot"),
        P("shot", None),
        P(),
        P(None, "space", None, None),
        P(),
        P(),
        P("shot", None, None),
    )
    out_specs = (P("shot"), P("space", "shot"))
    return jax.shard_map(shards, mesh=mesh, in_specs=in_specs, out_specs=out_specs, check_vma=False)
```
